128 devices in a mesh: dp: 16 (over x, y), expert: 8 (over z, core).
Axes of the slice: x: 4, y: 4, z: 4, core: 2. Of those that a mesh axis runs over, the one named last changes fastest.
Arguments:
- tokens: bfloat16 [2048, 4096], P('dp', 'expert'), may hold values from -6 to 6
- output_gradient: bfloat16 [2048, 4096], P('dp', 'expert'), may hold values from -6 to 6
- routing: int32 [2048, 2], P('dp'), may hold values from 0 to 7, all different within a row; in each aligned block of 128 rows (0 to 127, 128 to 255, ...) at most 96 rows name the same one
- router_gate_values: float32 [2048, 2], P('dp'), may hold values from 0.1 to 0.9
- gate_weight: bfloat16 [8, 7168, 4096], P('expert', 'dp'), may hold values from -0.09375 to 0.09375
- up_weight: bfloat16 [8, 7168, 4096], P('expert', 'dp'), may hold values from -0.09375 to 0.09375
- down_weight: bfloat16 [8, 7168, 4096], P('expert', 'dp'), may hold values from -0.0625 to 0.0625
- adapter_lower_gate: bfloat16 [8, 16, 4096], P('expert'), may hold values from -0.09375 to 0.09375
- adapter_upper_gate: bfloat16 [8, 7168, 16], P('expert', 'dp'), may hold values from -0.375 to 0.375
- adapter_lower_up: bfloat16 [8, 16, 4096], P('expert'), may hold values from -0.09375 to 0.09375
- adapter_upper_up: bfloat16 [8, 7168, 16], P('expert', 'dp'), may hold values from -0.375 to 0.375
- adapter_lower_down: bfloat16 [8, 16, 7168], P('expert', None, 'dp'), may hold values from -0.0625 to 0.0625
- adapter_upper_down: bfloat16 [8, 4096, 16], P('expert'), may hold values from -0.375 to 0.375
Outputs:
- grad_x: bfloat16 [2048, 4096], P('dp', 'expert')
- grad_lora_a_gate: float32 [8, 16, 4096], P('expert')
- grad_lora_b_gate: float32 [8, 7168, 16], P('expert', 'dp')
- grad_lora_a_up: float32 [8, 16, 4096], P('expert')
- grad_lora_b_up: float32 [8, 7168, 16], P('expert', 'dp')
- grad_lora_a_down: float32 [8, 16, 7168], P('expert', None, 'dp')
- grad_lora_b_down: float32 [8, 4096, 16], P('expert')
The draws below stay inside these ranges and needn't reach their ends.
Inputs may be any that keep to these rules, and one draw needn't show every extreme that they name: `routing`: each row names two different experts. In the rows of one dp shard (aligned blocks of 128 rows) no expert is named by more than 96 rows, and in some blocks one expert is named by exactly 96 rows.
All inputs are finite; a program needn't handle non-finite values.
Results may differ from the reference program's by a relative error of at most 0.015.
Values may be sent and summed in bfloat16 or wider, within the bound.
A program may use at most 256 MiB of HBM per device.

```python
import math
import jax
import jax.numpy as jnp
import numpy as np
from jax import lax

MODEL_WIDTH = 4096
HIDDEN_HALF = 7168
ADAPTER_RANK = 16
TOK_DEV = 128
EXPERT_TOTAL = 8
CAP = 96
TOKENS = 2048
N_DP = 16


def block_levels(own_key, shape, cuts, least, high):
    gain = 1.0
    for axis_at, shards_of in cuts:
        heights = jax.random.uniform(jax.random.fold_in(jax.random.fold_in(own_key, 6), axis_at), (shards_of,), jnp.float32, least / len(cuts), high / len(cuts))
        gain = gain * jnp.repeat(jnp.exp(heights), shape[axis_at] // shards_of).reshape((-1,) + (1,) * (len(shape) - 1 - axis_at))
    return gain


def shared_out(stream_key, own, number, rows, number_of, top, reach, slope):
    sequence = jax.random.permutation(stream_key, number_of)
    crowded, usual = load_shares(number_of, rows * top, reach, slope, True), load_shares(number_of, rows * top, reach, slope, False)
    places = jnp.arange(number_of)

    def named(lengths, rotation):
        used = int((lengths > 0).sum())
        fixed = max(1, used // 4)
        shifted = fixed + (places - fixed + rotation * (used - fixed)) % max(1, number_of - fixed)
        return jnp.zeros((number_of,), jnp.int32).at[sequence[jnp.where(places < fixed, places, shifted)]].set(jnp.asarray(lengths, jnp.int32))

    lengths = jnp.where(number % 4 == 0, named(crowded, number // 4), named(usual, number - number // 4 - 1))
    mixed = jax.random.permutation(jax.random.fold_in(own, 3), number_of)
    source_of, receiver = mixed[0:number_of // 2 * 2:2], mixed[1:number_of // 2 * 2:2]
    room = jnp.minimum(lengths[source_of] - 1, reach - lengths[receiver]) // 2
    room = jnp.where((source_of == sequence[0]) | (receiver == sequence[0]) | (lengths[receiver] == 0), 0, jnp.maximum(room, 0))
    shifted = jax.random.randint(jax.random.fold_in(own, 4), (number_of // 2,), 0, 1 << 20) % (room + 1)
    lengths = lengths.at[source_of].add(-shifted).at[receiver].add(shifted)
    labels = jnp.searchsorted(jnp.cumsum(lengths), jnp.arange(rows * top), side="right").astype(jnp.int32)
    listing = labels.reshape(top, rows).T
    listing = listing[jax.random.permutation(jax.random.fold_in(own, 1), rows)]
    rotation = jax.random.randint(jax.random.fold_in(own, 2), (rows, 1), 0, top)
    return jnp.take_along_axis(listing, (jnp.arange(top)[None, :] + rotation) % top, axis=1)


def load_shares(count, total, most, skew, full):
    loads = [(1 << 20) // math.isqrt(grade ** skew) + 1 for grade in range(1, count + 1)]
    largest = most if full else min(most, max(-(-total // count), total * loads[0] // sum(loads)))
    least = 1 if total - largest >= count - 1 else 0
    counts, surplus = [largest] + [least] * (count - 1), total - largest - least * (count - 1)
    while surplus > 0:
        movable = [i for i in range(1, count) if counts[i] < largest] or [i for i in range(1, count) if counts[i] < most]
        mass, remaining = sum([loads[i] for i in movable]), surplus
        for i in movable:
            addition = min(most - counts[i], max(1, remaining * loads[i] // mass), surplus)
            counts[i] = counts[i] + addition
            surplus = surplus - addition
    return np.array(counts)


def gaussian(key, shape, spread, bound, split=(), kind=jnp.bfloat16):
    array = jax.random.normal(key, shape, jnp.float32) * spread
    if len(split) > 0:
        array = block_levels(key, shape, split, -0.22, 0.18) * array
    return jnp.clip(array, min=-bound, max=bound).astype(kind)


def setup_inputs(seed: int = 0) -> dict:
    streams_of = jax.random.split(jax.random.key(seed), 14)
    tokens = gaussian(streams_of[0], (TOKENS, MODEL_WIDTH), 1.0, 6.0, ((0, 16), (1, 8)))
    output_gradient = gaussian(streams_of[1], (TOKENS, MODEL_WIDTH), 1.0, 6.0, ((0, 16), (1, 8)))
    routing_keys = jax.random.split(jax.random.fold_in(streams_of[2], 1), TOKENS // TOK_DEV)
    routing_turns = jax.random.permutation(jax.random.fold_in(streams_of[2], 3), TOKENS // TOK_DEV)
    routing = jax.vmap(lambda own, number: shared_out(jax.random.fold_in(streams_of[2], 2), own, number, TOK_DEV, EXPERT_TOTAL, 2, CAP, 2))(routing_keys, routing_turns).reshape((TOKENS, 2))
    router_gate_values = jnp.clip(0.1 + 0.79999997 * jax.random.uniform(streams_of[3], (TOKENS, 2), jnp.float32) ** block_levels(streams_of[3], (TOKENS, 2), ((0, 16),), -0.2, 0.2), 0.1, 0.9)
    gate_weight = gaussian(streams_of[4], (EXPERT_TOTAL, HIDDEN_HALF, MODEL_WIDTH), MODEL_WIDTH ** -0.5, 0.09375, ((0, 8), (1, 16)))
    up_weight = gaussian(streams_of[5], (EXPERT_TOTAL, HIDDEN_HALF, MODEL_WIDTH), MODEL_WIDTH ** -0.5, 0.09375, ((0, 8), (1, 16)))
    down_weight = gaussian(streams_of[6], (EXPERT_TOTAL, HIDDEN_HALF, MODEL_WIDTH), HIDDEN_HALF ** -0.5, 0.0625, ((0, 8), (1, 16)))
    adapter_lower_gate = gaussian(streams_of[7], (EXPERT_TOTAL, ADAPTER_RANK, MODEL_WIDTH), MODEL_WIDTH ** -0.5, 0.09375, ((0, 8),))
    adapter_upper_gate = gaussian(streams_of[8], (EXPERT_TOTAL, HIDDEN_HALF, ADAPTER_RANK), (ADAPTER_RANK * 16) ** -0.5, 0.375, ((0, 8), (1, 16)))
    adapter_lower_up = gaussian(streams_of[9], (EXPERT_TOTAL, ADAPTER_RANK, MODEL_WIDTH), MODEL_WIDTH ** -0.5, 0.09375, ((0, 8),))
    adapter_upper_up = gaussian(streams_of[10], (EXPERT_TOTAL, HIDDEN_HALF, ADAPTER_RANK), (ADAPTER_RANK * 16) ** -0.5, 0.375, ((0, 8), (1, 16)))
    adapter_lower_down = gaussian(streams_of[11], (EXPERT_TOTAL, ADAPTER_RANK, HIDDEN_HALF), HIDDEN_HALF ** -0.5, 0.0625, ((0, 8), (2, 16)))
    adapter_upper_down = gaussian(streams_of[12], (EXPERT_TOTAL, MODEL_WIDTH, ADAPTER_RANK), (ADAPTER_RANK * 16) ** -0.5, 0.375, ((0, 8),))
    return {"tokens": tokens, "output_gradient": output_gradient, "routing": routing, "router_gate_values": router_gate_values, "gate_weight": gate_weight, "up_weight": up_weight, "down_weight": down_weight, "adapter_lower_gate": adapter_lower_gate, "adapter_upper_gate": adapter_upper_gate, "adapter_lower_up": adapter_lower_up, "adapter_upper_up": adapter_upper_up, "adapter_lower_down": adapter_lower_down, "adapter_upper_down": adapter_upper_down}


ADAPTER_SCALE = 2.0


def contract_pair(left, right, left_axis, right_axis):
    return lax.dot_general(left, right, (((left_axis,), (right_axis,)), ((), ())), preferred_element_type=jnp.float32)


def slot_numbers(route_rows, experts):
    picked = (route_rows[:, :, None] == jnp.arange(experts, dtype=jnp.int32)[None, None, :]).astype(jnp.int32)
    per_token = jnp.sum(picked, axis=1)
    earlier = jnp.cumsum(per_token, axis=0) - per_token
    return jnp.sum(earlier[:, None, :] * picked, axis=2).astype(jnp.int32)


def slot_sources(route_rows, positions, experts, capacity):
    tokens_here, choose = route_rows.shape
    target = (route_rows * capacity + positions).reshape(-1)
    owners = jnp.repeat(jnp.arange(tokens_here, dtype=jnp.int32), choose)
    member_ids = jnp.tile(jnp.arange(choose, dtype=jnp.int32), tokens_here)
    source = jnp.full((experts * capacity,), tokens_here, jnp.int32).at[target].set(owners)
    member = jnp.zeros((experts * capacity,), jnp.int32).at[target].set(member_ids)
    return source, member


def rows_backward_pass(input_rows, output_gradient_rows, params):
    gate_weight, up_weight, down_weight, a_gate, gate_adapter_upper, a_up, up_adapter_upper, down_adapter_lower, b_down = params
    gate_projected_lower = contract_pair(a_gate, input_rows, 1, 1).astype(jnp.bfloat16)
    up_projected_lower = contract_pair(a_up, input_rows, 1, 1).astype(jnp.bfloat16)
    gate_preactivation = contract_pair(gate_weight, input_rows, 1, 1) + ADAPTER_SCALE * contract_pair(gate_adapter_upper, gate_projected_lower, 1, 0)
    up_preactivation = contract_pair(up_weight, input_rows, 1, 1) + ADAPTER_SCALE * contract_pair(up_adapter_upper, up_projected_lower, 1, 0)
    sigmoid_gate = jax.nn.sigmoid(gate_preactivation)
    silu_gate = gate_preactivation * sigmoid_gate
    hidden_units = (silu_gate * up_preactivation).astype(jnp.bfloat16)
    down_projected_lower = contract_pair(b_down, output_gradient_rows, 0, 1).astype(jnp.bfloat16)
    hidden_gradient = contract_pair(down_weight, output_gradient_rows, 1, 1) + ADAPTER_SCALE * contract_pair(down_adapter_lower, down_projected_lower, 0, 0)
    gate_gradient = (hidden_gradient * up_preactivation * sigmoid_gate * (1.0 + gate_preactivation * (1.0 - sigmoid_gate))).astype(jnp.bfloat16)
    up_gradient = (hidden_gradient * silu_gate).astype(jnp.bfloat16)
    gate_partial = contract_pair(gate_adapter_upper, gate_gradient, 0, 0).astype(jnp.bfloat16)
    up_partial = contract_pair(up_adapter_upper, up_gradient, 0, 0).astype(jnp.bfloat16)
    down_partial = contract_pair(down_adapter_lower, hidden_units, 1, 0).astype(jnp.bfloat16)
    paired_partials = jnp.concatenate([gate_partial, up_partial], 0)
    paired_factors = jnp.concatenate([a_gate, a_up], 0)
    gradient_rows_out = contract_pair(gate_gradient, gate_weight, 0, 0) + contract_pair(up_gradient, up_weight, 0, 0) + ADAPTER_SCALE * contract_pair(paired_partials, paired_factors, 0, 0)
    shared_slice = (ADAPTER_SCALE * contract_pair(gate_partial, input_rows, 1, 0),
              ADAPTER_SCALE * contract_pair(up_partial, input_rows, 1, 0),
              ADAPTER_SCALE * contract_pair(output_gradient_rows, down_partial, 0, 1))
    owned_slice = (ADAPTER_SCALE * contract_pair(gate_gradient, gate_projected_lower, 1, 1),
             ADAPTER_SCALE * contract_pair(up_gradient, up_projected_lower, 1, 1),
             ADAPTER_SCALE * contract_pair(down_projected_lower, hidden_units, 1, 1))
    return gradient_rows_out, shared_slice, owned_slice


def reference(tokens, output_gradient, routing, router_gate_values, gate_weight, up_weight, down_weight, adapter_lower_gate, adapter_upper_gate, adapter_lower_up, adapter_upper_up, adapter_lower_down, adapter_upper_down):
    shards = N_DP
    route_blocks = routing.reshape(shards, TOK_DEV, 2)

    def shard_places(route_rows):
        return slot_numbers(route_rows, EXPERT_TOTAL)

    places = jax.vmap(shard_places)(route_blocks)

    def shard_slots(route_rows, positions):
        return slot_sources(route_rows, positions, EXPERT_TOTAL, CAP)

    sources, members = jax.vmap(shard_slots)(route_blocks, places)
    shard_base = jnp.arange(shards, dtype=jnp.int32)[:, None] * TOK_DEV
    global_src = jnp.where(sources < TOK_DEV, sources + shard_base, TOKENS).astype(jnp.int32)
    gate_index = jnp.where(sources < TOK_DEV, global_src * 2 + members, 2 * TOKENS).astype(jnp.int32)
    slot_order = global_src.reshape(shards, EXPERT_TOTAL, CAP).transpose(1, 0, 2).reshape(EXPERT_TOTAL, shards * CAP)
    gate_order = gate_index.reshape(shards, EXPERT_TOTAL, CAP).transpose(1, 0, 2).reshape(EXPERT_TOTAL, shards * CAP)
    gate_flat = jnp.concatenate([router_gate_values.reshape(-1), jnp.zeros((1,), router_gate_values.dtype)])
    padded_x = jnp.concatenate([tokens, jnp.zeros((1, MODEL_WIDTH), tokens.dtype)], 0)
    padded_dy = jnp.concatenate([output_gradient, jnp.zeros((1, MODEL_WIDTH), output_gradient.dtype)], 0)
    input_rows_local = padded_x[slot_order]
    gradient_rows_local = (gate_flat[gate_order][..., None] * padded_dy[slot_order].astype(jnp.float32)).astype(jnp.bfloat16)
    block_width = HIDDEN_HALF // N_DP

    def single_expert(pack):
        input_rows, output_gradient_rows, gate_w, up_w, down_w, gate_lower_factor, gate_lb, up_lower_factor, up_lb, down_la, down_upper_factor = pack
        blocks = (gate_w.reshape(N_DP, block_width, MODEL_WIDTH), up_w.reshape(N_DP, block_width, MODEL_WIDTH),
                  down_w.reshape(N_DP, block_width, MODEL_WIDTH), gate_lb.reshape(N_DP, block_width, ADAPTER_RANK),
                  up_lb.reshape(N_DP, block_width, ADAPTER_RANK),
                  down_la.reshape(ADAPTER_RANK, N_DP, block_width).transpose(1, 0, 2))

        def block_step(totals, block_slice):
            gate_weight_block, up_weight_block, down_weight_block, gate_upper_factor, up_upper_factor, down_lower_factor = block_slice
            gradient_rows_out, shared_slice, owned_slice = rows_backward_pass(input_rows, output_gradient_rows, (gate_weight_block, up_weight_block, down_weight_block, gate_lower_factor, gate_upper_factor, up_lower_factor, up_upper_factor, down_lower_factor, down_upper_factor))
            rounded = lax.optimization_barrier(gradient_rows_out.astype(jnp.bfloat16)).astype(jnp.float32)
            return (totals[0] + rounded, jax.tree.map(jnp.add, totals[1], shared_slice)), owned_slice

        initial = (jnp.zeros((N_DP * CAP, MODEL_WIDTH), jnp.float32),
                   (jnp.zeros((ADAPTER_RANK, MODEL_WIDTH), jnp.float32), jnp.zeros((ADAPTER_RANK, MODEL_WIDTH), jnp.float32), jnp.zeros((MODEL_WIDTH, ADAPTER_RANK), jnp.float32)))
        (rows_sum, shared_slice), owned_slice = lax.scan(block_step, initial, blocks)
        grad_b_gate = owned_slice[0].reshape(HIDDEN_HALF, ADAPTER_RANK)
        grad_b_up = owned_slice[1].reshape(HIDDEN_HALF, ADAPTER_RANK)
        grad_a_down = owned_slice[2].transpose(1, 0, 2).reshape(ADAPTER_RANK, HIDDEN_HALF)
        return rows_sum, shared_slice[0], grad_b_gate, shared_slice[1], grad_b_up, grad_a_down, shared_slice[2]

    result_list = lax.map(single_expert, (input_rows_local, gradient_rows_local, gate_weight, up_weight, down_weight, adapter_lower_gate, adapter_upper_gate, adapter_lower_up, adapter_upper_up, adapter_lower_down, adapter_upper_down))
    rows_all = result_list[0].reshape(EXPERT_TOTAL * shards * CAP, MODEL_WIDTH)
    lookup = (route_blocks * (shards * CAP) + jnp.arange(shards, dtype=jnp.int32)[:, None, None] * CAP + places).reshape(TOKENS, 2).astype(jnp.int32)
    grad_x = jnp.sum(rows_all[lookup], axis=1).astype(jnp.bfloat16)
    return grad_x, result_list[1], result_list[2], result_list[3], result_list[4], result_list[5], result_list[6]
```

```python
import jax
import jax.numpy as jnp
from jax import lax
from jax.sharding import PartitionSpec as P

ADAPTER_SCALE = 2.0
NUM_CHUNKS = 2


def contract_pair(left, right, left_axis, right_axis):
    return lax.dot_general(
        left, right, (((left_axis,), (right_axis,)), ((), ())), preferred_element_type=jnp.float32
    )


def slot_numbers(route_rows, experts):
    picked = (route_rows[:, :, None] == jnp.arange(experts, dtype=jnp.int32)[None, None, :]).astype(
        jnp.int32
    )
    per_token = jnp.sum(picked, axis=1)
    earlier = jnp.cumsum(per_token, axis=0) - per_token
    return jnp.sum(earlier[:, None, :] * picked, axis=2)


def slot_sources(route_rows, positions, experts, capacity):
    tokens_here, choose = route_rows.shape
    target = (route_rows * capacity + positions).reshape(-1)
    owners = jnp.repeat(jnp.arange(tokens_here, dtype=jnp.int32), choose)
    member_ids = jnp.tile(jnp.arange(choose, dtype=jnp.int32), tokens_here)
    source = jnp.full((experts * capacity,), tokens_here, jnp.int32).at[target].set(owners)
    member = jnp.zeros((experts * capacity,), jnp.int32).at[target].set(member_ids)
    return (source, member)


def rows_backward_pass(input_rows, output_gradient_rows, params):
    (
        gate_weight,
        up_weight,
        down_weight,
        a_gate,
        gate_adapter_upper,
        a_up,
        up_adapter_upper,
        down_adapter_lower,
        b_down,
    ) = params
    gate_projected_lower = contract_pair(a_gate, input_rows, 1, 1).astype(jnp.bfloat16)
    up_projected_lower = contract_pair(a_up, input_rows, 1, 1).astype(jnp.bfloat16)
    gate_preactivation = contract_pair(
        gate_weight, input_rows, 1, 1
    ) + ADAPTER_SCALE * contract_pair(gate_adapter_upper, gate_projected_lower, 1, 0)
    up_preactivation = contract_pair(up_weight, input_rows, 1, 1) + ADAPTER_SCALE * contract_pair(
        up_adapter_upper, up_projected_lower, 1, 0
    )
    sigmoid_gate = jax.nn.sigmoid(gate_preactivation)
    silu_gate = gate_preactivation * sigmoid_gate
    hidden_units = (silu_gate * up_preactivation).astype(jnp.bfloat16)
    down_projected_lower = contract_pair(b_down, output_gradient_rows, 0, 1).astype(jnp.bfloat16)
    hidden_gradient = contract_pair(
        down_weight, output_gradient_rows, 1, 1
    ) + ADAPTER_SCALE * contract_pair(down_adapter_lower, down_projected_lower, 0, 0)
    gate_gradient = (
        hidden_gradient
        * up_preactivation
        * sigmoid_gate
        * (1.0 + gate_preactivation * (1.0 - sigmoid_gate))
    ).astype(jnp.bfloat16)
    up_gradient = (hidden_gradient * silu_gate).astype(jnp.bfloat16)
    gate_partial = contract_pair(gate_adapter_upper, gate_gradient, 0, 0).astype(jnp.bfloat16)
    up_partial = contract_pair(up_adapter_upper, up_gradient, 0, 0).astype(jnp.bfloat16)
    down_partial = contract_pair(down_adapter_lower, hidden_units, 1, 0).astype(jnp.bfloat16)
    paired_partials = jnp.concatenate([gate_partial, up_partial], 0)
    paired_factors = jnp.concatenate([a_gate, a_up], 0)
    gradient_rows_out = (
        contract_pair(gate_gradient, gate_weight, 0, 0)
        + contract_pair(up_gradient, up_weight, 0, 0)
        + ADAPTER_SCALE * contract_pair(paired_partials, paired_factors, 0, 0)
    )
    shared_slice = (
        ADAPTER_SCALE * contract_pair(gate_partial, input_rows, 1, 0),
        ADAPTER_SCALE * contract_pair(up_partial, input_rows, 1, 0),
        ADAPTER_SCALE * contract_pair(output_gradient_rows, down_partial, 0, 1),
    )
    owned_slice = (
        ADAPTER_SCALE * contract_pair(gate_gradient, gate_projected_lower, 1, 1),
        ADAPTER_SCALE * contract_pair(up_gradient, up_projected_lower, 1, 1),
        ADAPTER_SCALE * contract_pair(down_projected_lower, hidden_units, 1, 1),
    )
    return (gradient_rows_out, shared_slice, owned_slice)


def local(
    tokens,
    output_gradient,
    routing,
    router_gate_values,
    gate_weight,
    up_weight,
    down_weight,
    adapter_lower_gate,
    adapter_upper_gate,
    adapter_lower_up,
    adapter_upper_up,
    adapter_lower_down,
    adapter_upper_down,
):
    experts = lax.axis_size("expert")
    shards = lax.axis_size("dp")
    tok_local, feat_local = tokens.shape
    choose = routing.shape[1]
    complete_width = feat_local * experts
    capacity = min(tok_local, 6 * tok_local // experts)
    adapter_rank = adapter_lower_gate.shape[1]
    chunks = NUM_CHUNKS
    piece = capacity // chunks
    params = (
        gate_weight[0],
        up_weight[0],
        down_weight[0],
        adapter_lower_gate[0],
        adapter_upper_gate[0],
        adapter_lower_up[0],
        adapter_upper_up[0],
        adapter_lower_down[0],
        adapter_upper_down[0],
    )
    positions = slot_numbers(routing, experts)
    zero_row = jnp.zeros((1, feat_local), jnp.bfloat16)
    source, member = slot_sources(routing, positions, experts, capacity)
    clamped = jnp.minimum(source, tok_local - 1)
    slot_gate = jnp.where(
        source < tok_local, router_gate_values.reshape(-1)[clamped * choose + member], 0.0
    )
    send_x = jnp.concatenate([tokens, zero_row], 0)[source].reshape(experts, capacity, feat_local)
    send_dy = (
        (
            slot_gate[:, None]
            * jnp.concatenate([output_gradient, zero_row], 0)[source].astype(jnp.float32)
        )
        .astype(jnp.bfloat16)
        .reshape(experts, capacity, feat_local)
    )
    send_both = jnp.concatenate([send_x, send_dy], axis=2)
    recv_both = lax.all_to_all(send_both, "expert", split_axis=0, concat_axis=2, tiled=True)[0]
    recv_both = recv_both.reshape(capacity, experts, 2, feat_local).transpose(0, 2, 1, 3)
    recv_both = recv_both.reshape(capacity, 2 * complete_width)

    rows_pieces = []
    shared_total = None
    owned_total = None
    for c in range(chunks):
        part = recv_both[c * piece:(c + 1) * piece]
        gathered = lax.all_gather(part, "dp", axis=0, tiled=True)
        x_rows = gathered[:, :complete_width]
        dy_rows = gathered[:, complete_width:]
        rows_out, shared_slice, owned_slice = rows_backward_pass(x_rows, dy_rows, params)
        if c == 0:
            shared_total, owned_total = shared_slice, owned_slice
        else:
            shared_total = jax.tree.map(jnp.add, shared_total, shared_slice)
            owned_total = jax.tree.map(jnp.add, owned_total, owned_slice)
        rows_bf = rows_out.astype(jnp.bfloat16).reshape(shards, piece, complete_width)
        summed = lax.psum_scatter(rows_bf, "dp", scatter_dimension=0, tiled=True)[0]
        rows_pieces.append(summed)
    lora = jnp.concatenate(
        [shared_total[0], shared_total[1], shared_total[2].T], 0
    ).astype(jnp.bfloat16)
    lora_shape = lora.shape
    lora_part = lax.psum_scatter(
        lora.reshape(shards * 8, -1), "dp", scatter_dimension=0, tiled=True
    )
    summed = jnp.concatenate(rows_pieces, 0)
    lora_part = lax.optimization_barrier(lora_part)
    lora_sum = lax.all_gather(lora_part, "dp", axis=0, tiled=True).astype(jnp.float32)
    lora_sum = lora_sum.reshape(lora_shape)
    grad_a_gate = lora_sum[:adapter_rank]
    grad_a_up = lora_sum[adapter_rank:2 * adapter_rank]
    grad_b_down = lora_sum[2 * adapter_rank:].T
    returned_rows = lax.all_to_all(
        summed.reshape(capacity, experts, feat_local),
        "expert",
        split_axis=1,
        concat_axis=1,
        tiled=True,
    ).astype(jnp.float32)
    lookup = positions * experts + routing
    grad_x = jnp.sum(returned_rows.reshape(capacity * experts, feat_local)[lookup], axis=1).astype(
        jnp.bfloat16
    )
    return (
        grad_x,
        grad_a_gate[None],
        owned_total[0][None],
        grad_a_up[None],
        owned_total[1][None],
        owned_total[2][None],
        grad_b_down[None],
    )


def solution(mesh):
    return jax.shard_map(
        local,
        mesh=mesh,
        in_specs=(
            P("dp", "expert"),
            P("dp", "expert"),
            P("dp", None),
            P("dp", None),
            P("expert", "dp", None),
            P("expert", "dp", None),
            P("expert", "dp", None),
            P("expert", None, None),
            P("expert", "dp", None),
            P("expert", None, None),
            P("expert", "dp", None),
            P("expert", None, "dp"),
            P("expert", None, None),
        ),
        out_specs=(
            P("dp", "expert"),
            P("expert", None, None),
            P("expert", "dp", None),
            P("expert", None, None),
            P("expert", "dp", None),
            P("expert", None, "dp"),
            P("expert", None, None),
        ),
        check_vma=False,
    )
```

```python
import jax
import jax.numpy as jnp
from jax import lax
from jax.sharding import PartitionSpec as P

ADAPTER_SCALE = 2.0
NUM_CHUNKS = 2
PART_COLS = 128


def contract_pair(left, right, left_axis, right_axis):
    return lax.dot_general(
        left, right, (((left_axis,), (right_axis,)), ((), ())), preferred_element_type=jnp.float32
    )


def slot_numbers(route_rows, experts):
    picked = (route_rows[:, :, None] == jnp.arange(experts, dtype=jnp.int32)[None, None, :]).astype(
        jnp.int32
    )
    per_token = jnp.sum(picked, axis=1)
    earlier = jnp.cumsum(per_token, axis=0) - per_token
    return jnp.sum(earlier[:, None, :] * picked, axis=2)


def slot_sources(route_rows, positions, experts, capacity):
    tokens_here, choose = route_rows.shape
    target = (route_rows * capacity + positions).reshape(-1)
    owners = jnp.repeat(jnp.arange(tokens_here, dtype=jnp.int32), choose)
    member_ids = jnp.tile(jnp.arange(choose, dtype=jnp.int32), tokens_here)
    source = jnp.full((experts * capacity,), tokens_here, jnp.int32).at[target].set(owners)
    member = jnp.zeros((experts * capacity,), jnp.int32).at[target].set(member_ids)
    return (source, member)


def rows_backward_pass(input_rows, output_gradient_rows, params):
    (
        gate_weight,
        up_weight,
        down_weight,
        a_gate,
        gate_adapter_upper,
        a_up,
        up_adapter_upper,
        down_adapter_lower,
        b_down,
    ) = params
    gate_projected_lower = contract_pair(a_gate, input_rows, 1, 1).astype(jnp.bfloat16)
    up_projected_lower = contract_pair(a_up, input_rows, 1, 1).astype(jnp.bfloat16)
    gate_preactivation = contract_pair(
        gate_weight, input_rows, 1, 1
    ) + ADAPTER_SCALE * contract_pair(gate_adapter_upper, gate_projected_lower, 1, 0)
    up_preactivation = contract_pair(up_weight, input_rows, 1, 1) + ADAPTER_SCALE * contract_pair(
        up_adapter_upper, up_projected_lower, 1, 0
    )
    sigmoid_gate = jax.nn.sigmoid(gate_preactivation)
    silu_gate = gate_preactivation * sigmoid_gate
    hidden_units = (silu_gate * up_preactivation).astype(jnp.bfloat16)
    down_projected_lower = contract_pair(b_down, output_gradient_rows, 0, 1).astype(jnp.bfloat16)
    hidden_gradient = contract_pair(
        down_weight, output_gradient_rows, 1, 1
    ) + ADAPTER_SCALE * contract_pair(down_adapter_lower, down_projected_lower, 0, 0)
    gate_gradient = (
        hidden_gradient
        * up_preactivation
        * sigmoid_gate
        * (1.0 + gate_preactivation * (1.0 - sigmoid_gate))
    ).astype(jnp.bfloat16)
    up_gradient = (hidden_gradient * silu_gate).astype(jnp.bfloat16)
    gate_partial = contract_pair(gate_adapter_upper, gate_gradient, 0, 0).astype(jnp.bfloat16)
    up_partial = contract_pair(up_adapter_upper, up_gradient, 0, 0).astype(jnp.bfloat16)
    down_partial = contract_pair(down_adapter_lower, hidden_units, 1, 0).astype(jnp.bfloat16)
    paired_partials = jnp.concatenate([gate_partial, up_partial], 0)
    paired_factors = jnp.concatenate([a_gate, a_up], 0)
    gradient_rows_out = (
        contract_pair(gate_gradient, gate_weight, 0, 0)
        + contract_pair(up_gradient, up_weight, 0, 0)
        + ADAPTER_SCALE * contract_pair(paired_partials, paired_factors, 0, 0)
    )
    shared_slice = (
        ADAPTER_SCALE * contract_pair(gate_partial, input_rows, 1, 0),
        ADAPTER_SCALE * contract_pair(up_partial, input_rows, 1, 0),
        ADAPTER_SCALE * contract_pair(output_gradient_rows, down_partial, 0, 1),
    )
    owned_slice = (
        ADAPTER_SCALE * contract_pair(gate_gradient, gate_projected_lower, 1, 1),
        ADAPTER_SCALE * contract_pair(up_gradient, up_projected_lower, 1, 1),
        ADAPTER_SCALE * contract_pair(down_projected_lower, hidden_units, 1, 1),
    )
    return (gradient_rows_out, shared_slice, owned_slice)


def rows_backward_parts(input_rows, output_gradient_rows, params):
    (
        gate_weight,
        up_weight,
        down_weight,
        a_gate,
        gate_adapter_upper,
        a_up,
        up_adapter_upper,
        down_adapter_lower,
        b_down,
    ) = params
    gate_projected_lower = contract_pair(a_gate, input_rows, 1, 1).astype(jnp.bfloat16)
    up_projected_lower = contract_pair(a_up, input_rows, 1, 1).astype(jnp.bfloat16)
    gate_preactivation = contract_pair(
        gate_weight, input_rows, 1, 1
    ) + ADAPTER_SCALE * contract_pair(gate_adapter_upper, gate_projected_lower, 1, 0)
    up_preactivation = contract_pair(up_weight, input_rows, 1, 1) + ADAPTER_SCALE * contract_pair(
        up_adapter_upper, up_projected_lower, 1, 0
    )
    sigmoid_gate = jax.nn.sigmoid(gate_preactivation)
    silu_gate = gate_preactivation * sigmoid_gate
    hidden_units = (silu_gate * up_preactivation).astype(jnp.bfloat16)
    down_projected_lower = contract_pair(b_down, output_gradient_rows, 0, 1).astype(jnp.bfloat16)
    hidden_gradient = contract_pair(
        down_weight, output_gradient_rows, 1, 1
    ) + ADAPTER_SCALE * contract_pair(down_adapter_lower, down_projected_lower, 0, 0)
    gate_gradient = (
        hidden_gradient
        * up_preactivation
        * sigmoid_gate
        * (1.0 + gate_preactivation * (1.0 - sigmoid_gate))
    ).astype(jnp.bfloat16)
    up_gradient = (hidden_gradient * silu_gate).astype(jnp.bfloat16)
    gate_partial = contract_pair(gate_gradient, gate_adapter_upper, 0, 0).astype(jnp.bfloat16)
    up_partial = contract_pair(up_gradient, up_adapter_upper, 0, 0).astype(jnp.bfloat16)
    down_partial = contract_pair(hidden_units, down_adapter_lower, 0, 1).astype(jnp.bfloat16)
    paired_partials = jnp.concatenate([gate_partial, up_partial], 1)
    paired_factors = jnp.concatenate([a_gate, a_up], 0)
    gradient_rows_out = (
        contract_pair(gate_gradient, gate_weight, 0, 0)
        + contract_pair(up_gradient, up_weight, 0, 0)
        + ADAPTER_SCALE * contract_pair(paired_partials, paired_factors, 1, 0)
    )
    parts = jnp.concatenate([gate_partial, up_partial, down_partial], 1)
    owned_slice = (
        ADAPTER_SCALE * contract_pair(gate_gradient, gate_projected_lower, 1, 1),
        ADAPTER_SCALE * contract_pair(up_gradient, up_projected_lower, 1, 1),
        ADAPTER_SCALE * contract_pair(down_projected_lower, hidden_units, 1, 1),
    )
    return (gradient_rows_out, parts, owned_slice)


def local(
    tokens,
    output_gradient,
    routing,
    router_gate_values,
    gate_weight,
    up_weight,
    down_weight,
    adapter_lower_gate,
    adapter_upper_gate,
    adapter_lower_up,
    adapter_upper_up,
    adapter_lower_down,
    adapter_upper_down,
):
    experts = lax.axis_size("expert")
    shards = lax.axis_size("dp")
    tok_local, feat_local = tokens.shape
    choose = routing.shape[1]
    complete_width = feat_local * experts
    capacity = min(tok_local, 6 * tok_local // experts)
    adapter_rank = adapter_lower_gate.shape[1]
    chunks = NUM_CHUNKS
    piece = capacity // chunks
    params = (
        gate_weight[0],
        up_weight[0],
        down_weight[0],
        adapter_lower_gate[0],
        adapter_upper_gate[0],
        adapter_lower_up[0],
        adapter_upper_up[0],
        adapter_lower_down[0],
        adapter_upper_down[0],
    )
    positions = slot_numbers(routing, experts)
    zero_row = jnp.zeros((1, feat_local), jnp.bfloat16)
    source, member = slot_sources(routing, positions, experts, capacity)
    clamped = jnp.minimum(source, tok_local - 1)
    slot_gate = jnp.where(
        source < tok_local, router_gate_values.reshape(-1)[clamped * choose + member], 0.0
    )
    send_x = jnp.concatenate([tokens, zero_row], 0)[source].reshape(experts, capacity, feat_local)
    send_dy = (
        (
            slot_gate[:, None]
            * jnp.concatenate([output_gradient, zero_row], 0)[source].astype(jnp.float32)
        )
        .astype(jnp.bfloat16)
        .reshape(experts, capacity, feat_local)
    )
    send_both = jnp.concatenate([send_x, send_dy], axis=2)
    recv_both = lax.all_to_all(send_both, "expert", split_axis=0, concat_axis=2, tiled=True)[0]
    recv_both = recv_both.reshape(capacity, experts, 2, feat_local).transpose(0, 2, 1, 3)
    recv_both = recv_both.reshape(capacity, 2 * complete_width)

    rows_chunks = []
    part_chunks = []
    x_chunks = []
    dy_chunks = []
    owned_total = None
    for c in range(chunks):
        part = recv_both[c * piece:(c + 1) * piece]
        gathered = lax.all_gather(part, "dp", axis=0, tiled=True)
        x_rows = gathered[:, :complete_width]
        dy_rows = gathered[:, complete_width:]
        rows_out, parts, owned_slice = rows_backward_parts(x_rows, dy_rows, params)
        if c == 0:
            owned_total = owned_slice
        else:
            owned_total = jax.tree.map(jnp.add, owned_total, owned_slice)
        rows_chunks.append(rows_out.astype(jnp.bfloat16).reshape(shards, piece, complete_width))
        part_chunks.append(parts.reshape(shards, piece, 3 * adapter_rank))
        x_chunks.append(x_rows.reshape(shards, piece, complete_width))
        dy_chunks.append(dy_rows.reshape(shards, piece, complete_width))
    rows_all = jnp.concatenate(rows_chunks, 1)
    parts_all = jnp.concatenate(part_chunks, 1)
    parts_all = jnp.pad(parts_all, ((0, 0), (0, 0), (0, PART_COLS - 3 * adapter_rank)))
    packed = jnp.concatenate([rows_all, parts_all], 2)
    summed_packed = lax.psum_scatter(packed, "dp", scatter_dimension=0, tiled=True)[0]
    summed = summed_packed[:, :complete_width]
    parts_mine = summed_packed[:, complete_width:complete_width + 3 * adapter_rank]
    parts_sum = lax.all_gather(parts_mine, "dp", axis=0, tiled=True)
    parts_sum = parts_sum.reshape(shards, capacity, 3 * adapter_rank)
    x_all = jnp.concatenate(x_chunks, 1).reshape(shards * capacity, complete_width)
    dy_all = jnp.concatenate(dy_chunks, 1).reshape(shards * capacity, complete_width)
    parts_sum = parts_sum.reshape(shards * capacity, 3 * adapter_rank)
    grad_a_gate = ADAPTER_SCALE * contract_pair(parts_sum[:, :adapter_rank], x_all, 0, 0)
    grad_a_up = ADAPTER_SCALE * contract_pair(
        parts_sum[:, adapter_rank:2 * adapter_rank], x_all, 0, 0
    )
    grad_b_down = ADAPTER_SCALE * contract_pair(dy_all, parts_sum[:, 2 * adapter_rank:], 0, 0)
    returned_rows = lax.all_to_all(
        summed.reshape(capacity, experts, feat_local),
        "expert",
        split_axis=1,
        concat_axis=1,
        tiled=True,
    ).astype(jnp.float32)
    lookup = positions * experts + routing
    grad_x = jnp.sum(returned_rows.reshape(capacity * experts, feat_local)[lookup], axis=1).astype(
        jnp.bfloat16
    )
    return (
        grad_x,
        grad_a_gate[None],
        owned_total[0][None],
        grad_a_up[None],
        owned_total[1][None],
        owned_total[2][None],
        grad_b_down[None],
    )


def solution(mesh):
    return jax.shard_map(
        local,
        mesh=mesh,
        in_specs=(
            P("dp", "expert"),
            P("dp", "expert"),
            P("dp", None),
            P("dp", None),
            P("expert", "dp", None),
            P("expert", "dp", None),
            P("expert", "dp", None),
            P("expert", None, None),
            P("expert", "dp", None),
            P("expert", None, None),
            P("expert", "dp", None),
            P("expert", None, "dp"),
            P("expert", None, None),
        ),
        out_specs=(
            P("dp", "expert"),
            P("expert", None, None),
            P("expert", "dp", None),
            P("expert", None, None),
            P("expert", "dp", None),
            P("expert", None, "dp"),
            P("expert", None, None),
        ),
        check_vma=False,
    )
```

```python
import functools

import jax
import jax.numpy as jnp
from jax import lax
from jax.experimental import pallas as pl
from jax.experimental.pallas import tpu as pltpu
from jax.sharding import PartitionSpec as P

MESH = pl.DeviceIdType.MESH

ADAPTER_SCALE = 2.0
NUM_CHUNKS = 2
PART_COLS = 128


def contract_pair(left, right, left_axis, right_axis):
    return lax.dot_general(
        left, right, (((left_axis,), (right_axis,)), ((), ())), preferred_element_type=jnp.float32
    )


def slot_numbers(route_rows, experts):
    picked = (route_rows[:, :, None] == jnp.arange(experts, dtype=jnp.int32)[None, None, :]).astype(
        jnp.int32
    )
    per_token = jnp.sum(picked, axis=1)
    earlier = jnp.cumsum(per_token, axis=0) - per_token
    return jnp.sum(earlier[:, None, :] * picked, axis=2)


def slot_sources(route_rows, positions, experts, capacity):
    tokens_here, choose = route_rows.shape
    target = (route_rows * capacity + positions).reshape(-1)
    owners = jnp.repeat(jnp.arange(tokens_here, dtype=jnp.int32), choose)
    member_ids = jnp.tile(jnp.arange(choose, dtype=jnp.int32), tokens_here)
    source = jnp.full((experts * capacity,), tokens_here, jnp.int32).at[target].set(owners)
    member = jnp.zeros((experts * capacity,), jnp.int32).at[target].set(member_ids)
    return (source, member)


def rows_backward_pass(input_rows, output_gradient_rows, params):
    (
        gate_weight,
        up_weight,
        down_weight,
        a_gate,
        gate_adapter_upper,
        a_up,
        up_adapter_upper,
        down_adapter_lower,
        b_down,
    ) = params
    gate_projected_lower = contract_pair(a_gate, input_rows, 1, 1).astype(jnp.bfloat16)
    up_projected_lower = contract_pair(a_up, input_rows, 1, 1).astype(jnp.bfloat16)
    gate_preactivation = contract_pair(
        gate_weight, input_rows, 1, 1
    ) + ADAPTER_SCALE * contract_pair(gate_adapter_upper, gate_projected_lower, 1, 0)
    up_preactivation = contract_pair(up_weight, input_rows, 1, 1) + ADAPTER_SCALE * contract_pair(
        up_adapter_upper, up_projected_lower, 1, 0
    )
    sigmoid_gate = jax.nn.sigmoid(gate_preactivation)
    silu_gate = gate_preactivation * sigmoid_gate
    hidden_units = (silu_gate * up_preactivation).astype(jnp.bfloat16)
    down_projected_lower = contract_pair(b_down, output_gradient_rows, 0, 1).astype(jnp.bfloat16)
    hidden_gradient = contract_pair(
        down_weight, output_gradient_rows, 1, 1
    ) + ADAPTER_SCALE * contract_pair(down_adapter_lower, down_projected_lower, 0, 0)
    gate_gradient = (
        hidden_gradient
        * up_preactivation
        * sigmoid_gate
        * (1.0 + gate_preactivation * (1.0 - sigmoid_gate))
    ).astype(jnp.bfloat16)
    up_gradient = (hidden_gradient * silu_gate).astype(jnp.bfloat16)
    gate_partial = contract_pair(gate_adapter_upper, gate_gradient, 0, 0).astype(jnp.bfloat16)
    up_partial = contract_pair(up_adapter_upper, up_gradient, 0, 0).astype(jnp.bfloat16)
    down_partial = contract_pair(down_adapter_lower, hidden_units, 1, 0).astype(jnp.bfloat16)
    paired_partials = jnp.concatenate([gate_partial, up_partial], 0)
    paired_factors = jnp.concatenate([a_gate, a_up], 0)
    gradient_rows_out = (
        contract_pair(gate_gradient, gate_weight, 0, 0)
        + contract_pair(up_gradient, up_weight, 0, 0)
        + ADAPTER_SCALE * contract_pair(paired_partials, paired_factors, 0, 0)
    )
    shared_slice = (
        ADAPTER_SCALE * contract_pair(gate_partial, input_rows, 1, 0),
        ADAPTER_SCALE * contract_pair(up_partial, input_rows, 1, 0),
        ADAPTER_SCALE * contract_pair(output_gradient_rows, down_partial, 0, 1),
    )
    owned_slice = (
        ADAPTER_SCALE * contract_pair(gate_gradient, gate_projected_lower, 1, 1),
        ADAPTER_SCALE * contract_pair(up_gradient, up_projected_lower, 1, 1),
        ADAPTER_SCALE * contract_pair(down_projected_lower, hidden_units, 1, 1),
    )
    return (gradient_rows_out, shared_slice, owned_slice)


def rows_backward_parts(input_rows, output_gradient_rows, params):
    (
        gate_weight,
        up_weight,
        down_weight,
        a_gate,
        gate_adapter_upper,
        a_up,
        up_adapter_upper,
        down_adapter_lower,
        b_down,
    ) = params
    gate_projected_lower = contract_pair(a_gate, input_rows, 1, 1).astype(jnp.bfloat16)
    up_projected_lower = contract_pair(a_up, input_rows, 1, 1).astype(jnp.bfloat16)
    gate_preactivation = contract_pair(
        gate_weight, input_rows, 1, 1
    ) + ADAPTER_SCALE * contract_pair(gate_adapter_upper, gate_projected_lower, 1, 0)
    up_preactivation = contract_pair(up_weight, input_rows, 1, 1) + ADAPTER_SCALE * contract_pair(
        up_adapter_upper, up_projected_lower, 1, 0
    )
    sigmoid_gate = jax.nn.sigmoid(gate_preactivation)
    silu_gate = gate_preactivation * sigmoid_gate
    hidden_units = (silu_gate * up_preactivation).astype(jnp.bfloat16)
    down_projected_lower = contract_pair(b_down, output_gradient_rows, 0, 1).astype(jnp.bfloat16)
    hidden_gradient = contract_pair(
        down_weight, output_gradient_rows, 1, 1
    ) + ADAPTER_SCALE * contract_pair(down_adapter_lower, down_projected_lower, 0, 0)
    gate_gradient = (
        hidden_gradient
        * up_preactivation
        * sigmoid_gate
        * (1.0 + gate_preactivation * (1.0 - sigmoid_gate))
    ).astype(jnp.bfloat16)
    up_gradient = (hidden_gradient * silu_gate).astype(jnp.bfloat16)
    gate_partial = contract_pair(gate_gradient, gate_adapter_upper, 0, 0).astype(jnp.bfloat16)
    up_partial = contract_pair(up_gradient, up_adapter_upper, 0, 0).astype(jnp.bfloat16)
    down_partial = contract_pair(hidden_units, down_adapter_lower, 0, 1).astype(jnp.bfloat16)
    paired_partials = jnp.concatenate([gate_partial, up_partial], 1)
    paired_factors = jnp.concatenate([a_gate, a_up], 0)
    gradient_rows_out = (
        contract_pair(gate_gradient, gate_weight, 0, 0)
        + contract_pair(up_gradient, up_weight, 0, 0)
        + ADAPTER_SCALE * contract_pair(paired_partials, paired_factors, 1, 0)
    )
    parts = jnp.concatenate([gate_partial, up_partial, down_partial], 1)
    owned_slice = (
        ADAPTER_SCALE * contract_pair(gate_gradient, gate_projected_lower, 1, 1),
        ADAPTER_SCALE * contract_pair(up_gradient, up_projected_lower, 1, 1),
        ADAPTER_SCALE * contract_pair(down_projected_lower, hidden_units, 1, 1),
    )
    return (gradient_rows_out, parts, owned_slice)


def gather_dp_kernel(n, src_ref, out_ref, send_sem, recv_sem):
    me = lax.axis_index("dp")
    ex = lax.axis_index("expert")
    barrier = pltpu.get_barrier_semaphore()
    for k in range(1, n):
        peer = lax.rem(me + k, n)
        pl.semaphore_signal(barrier, inc=1, device_id=(peer, ex), device_id_type=MESH)
    pl.semaphore_wait(barrier, n - 1)
    copies = []
    for k in range(1, n):
        peer = lax.rem(me + k, n)
        cp = pltpu.make_async_remote_copy(
            src_ref,
            out_ref.at[me],
            send_sem.at[k],
            recv_sem.at[k],
            device_id=(peer, ex),
            device_id_type=MESH,
        )
        cp.start()
        copies.append(cp)
    out_ref[me] = src_ref[...]
    for cp in copies:
        cp.wait()


def gather_dp(block, n):
    return pl.pallas_call(
        functools.partial(gather_dp_kernel, n),
        out_shape=jax.ShapeDtypeStruct((n,) + block.shape, block.dtype),
        in_specs=[pl.BlockSpec(memory_space=pltpu.VMEM)],
        out_specs=pl.BlockSpec(memory_space=pltpu.VMEM),
        scratch_shapes=[pltpu.SemaphoreType.DMA((n,)), pltpu.SemaphoreType.DMA((n,))],
        compiler_params=pltpu.CompilerParams(collective_id=0, has_side_effects=True),
    )(block)


def local(
    tokens,
    output_gradient,
    routing,
    router_gate_values,
    gate_weight,
    up_weight,
    down_weight,
    adapter_lower_gate,
    adapter_upper_gate,
    adapter_lower_up,
    adapter_upper_up,
    adapter_lower_down,
    adapter_upper_down,
):
    experts = lax.axis_size("expert")
    shards = lax.axis_size("dp")
    tok_local, feat_local = tokens.shape
    choose = routing.shape[1]
    complete_width = feat_local * experts
    capacity = min(tok_local, 6 * tok_local // experts)
    adapter_rank = adapter_lower_gate.shape[1]
    chunks = NUM_CHUNKS
    piece = capacity // chunks
    params = (
        gate_weight[0],
        up_weight[0],
        down_weight[0],
        adapter_lower_gate[0],
        adapter_upper_gate[0],
        adapter_lower_up[0],
        adapter_upper_up[0],
        adapter_lower_down[0],
        adapter_upper_down[0],
    )
    positions = slot_numbers(routing, experts)
    zero_row = jnp.zeros((1, feat_local), jnp.bfloat16)
    source, member = slot_sources(routing, positions, experts, capacity)
    clamped = jnp.minimum(source, tok_local - 1)
    slot_gate = jnp.where(
        source < tok_local, router_gate_values.reshape(-1)[clamped * choose + member], 0.0
    )
    send_x = jnp.concatenate([tokens, zero_row], 0)[source].reshape(experts, capacity, feat_local)
    send_dy = (
        (
            slot_gate[:, None]
            * jnp.concatenate([output_gradient, zero_row], 0)[source].astype(jnp.float32)
        )
        .astype(jnp.bfloat16)
        .reshape(experts, capacity, feat_local)
    )
    send_both = jnp.concatenate([send_x, send_dy], axis=2)
    recv_both = lax.all_to_all(send_both, "expert", split_axis=0, concat_axis=2, tiled=True)[0]
    recv_both = recv_both.reshape(capacity, experts, 2, feat_local).transpose(2, 0, 1, 3)
    recv_both = recv_both.reshape(2, capacity, complete_width)

    rows_chunks = []
    part_chunks = []
    x_chunks = []
    dy_chunks = []
    owned_total = None
    for c in range(chunks):
        part = recv_both[:, c * piece:(c + 1) * piece]
        gathered = lax.all_gather(part, "dp", axis=1, tiled=True)
        x_rows = gathered[0]
        dy_rows = gathered[1]
        rows_out, parts, owned_slice = rows_backward_parts(x_rows, dy_rows, params)
        if c == 0:
            owned_total = owned_slice
        else:
            owned_total = jax.tree.map(jnp.add, owned_total, owned_slice)
        rows_chunks.append(rows_out.astype(jnp.bfloat16).reshape(shards, piece, complete_width))
        part_chunks.append(parts.reshape(shards, piece, 3 * adapter_rank))
        x_chunks.append(x_rows)
        dy_chunks.append(dy_rows)
    rows_all = jnp.concatenate(rows_chunks, 1)
    parts_all = jnp.concatenate(part_chunks, 1)
    parts_all = jnp.pad(parts_all, ((0, 0), (0, 0), (0, PART_COLS - 3 * adapter_rank)))
    packed = jnp.concatenate([rows_all, parts_all], 2)
    summed_packed = lax.psum_scatter(packed, "dp", scatter_dimension=0, tiled=True)[0]
    summed = summed_packed[:, :complete_width]
    parts_mine = summed_packed[:, complete_width:]
    parts_sum = gather_dp(parts_mine, shards).reshape(shards, chunks, piece, PART_COLS)
    grad_a_gate = None
    for c in range(chunks):
        parts_c = parts_sum[:, c].reshape(shards * piece, PART_COLS)
        a_gate_c = contract_pair(parts_c[:, :adapter_rank], x_chunks[c], 0, 0)
        a_up_c = contract_pair(parts_c[:, adapter_rank:2 * adapter_rank], x_chunks[c], 0, 0)
        b_down_c = contract_pair(dy_chunks[c], parts_c[:, 2 * adapter_rank:3 * adapter_rank], 0, 0)
        if grad_a_gate is None:
            grad_a_gate, grad_a_up, grad_b_down = a_gate_c, a_up_c, b_down_c
        else:
            grad_a_gate = grad_a_gate + a_gate_c
            grad_a_up = grad_a_up + a_up_c
            grad_b_down = grad_b_down + b_down_c
    grad_a_gate = ADAPTER_SCALE * grad_a_gate
    grad_a_up = ADAPTER_SCALE * grad_a_up
    grad_b_down = ADAPTER_SCALE * grad_b_down
    returned_rows = lax.all_to_all(
        summed.reshape(capacity, experts, feat_local),
        "expert",
        split_axis=1,
        concat_axis=1,
        tiled=True,
    ).astype(jnp.float32)
    lookup = positions * experts + routing
    grad_x = jnp.sum(returned_rows.reshape(capacity * experts, feat_local)[lookup], axis=1).astype(
        jnp.bfloat16
    )
    return (
        grad_x,
        grad_a_gate[None],
        owned_total[0][None],
        grad_a_up[None],
        owned_total[1][None],
        owned_total[2][None],
        grad_b_down[None],
    )


def solution(mesh):
    return jax.shard_map(
        local,
        mesh=mesh,
        in_specs=(
            P("dp", "expert"),
            P("dp", "expert"),
            P("dp", None),
            P("dp", None),
            P("expert", "dp", None),
            P("expert", "dp", None),
            P("expert", "dp", None),
            P("expert", None, None),
            P("expert", "dp", None),
            P("expert", None, None),
            P("expert", "dp", None),
            P("expert", None, "dp"),
            P("expert", None, None),
        ),
        out_specs=(
            P("dp", "expert"),
            P("expert", None, None),
            P("expert", "dp", None),
            P("expert", None, None),
            P("expert", "dp", None),
            P("expert", None, "dp"),
            P("expert", None, None),
        ),
        check_vma=False,
    )
```

```python
import functools

import jax
import jax.numpy as jnp
from jax import lax
from jax.experimental import pallas as pl
from jax.experimental.pallas import tpu as pltpu
from jax.sharding import PartitionSpec as P

MESH = pl.DeviceIdType.MESH

ADAPTER_SCALE = 2.0
NUM_CHUNKS = 3
PART_COLS = 128


def contract_pair(left, right, left_axis, right_axis):
    return lax.dot_general(
        left, right, (((left_axis,), (right_axis,)), ((), ())), preferred_element_type=jnp.float32
    )


def slot_numbers(route_rows, experts):
    picked = (route_rows[:, :, None] == jnp.arange(experts, dtype=jnp.int32)[None, None, :]).astype(
        jnp.int32
    )
    per_token = jnp.sum(picked, axis=1)
    earlier = jnp.cumsum(per_token, axis=0) - per_token
    return jnp.sum(earlier[:, None, :] * picked, axis=2)


def slot_sources(route_rows, positions, experts, capacity):
    tokens_here, choose = route_rows.shape
    target = (route_rows * capacity + positions).reshape(-1)
    owners = jnp.repeat(jnp.arange(tokens_here, dtype=jnp.int32), choose)
    member_ids = jnp.tile(jnp.arange(choose, dtype=jnp.int32), tokens_here)
    source = jnp.full((experts * capacity,), tokens_here, jnp.int32).at[target].set(owners)
    member = jnp.zeros((experts * capacity,), jnp.int32).at[target].set(member_ids)
    return (source, member)


def rows_backward_pass(input_rows, output_gradient_rows, params):
    (
        gate_weight,
        up_weight,
        down_weight,
        a_gate,
        gate_adapter_upper,
        a_up,
        up_adapter_upper,
        down_adapter_lower,
        b_down,
    ) = params
    gate_projected_lower = contract_pair(a_gate, input_rows, 1, 1).astype(jnp.bfloat16)
    up_projected_lower = contract_pair(a_up, input_rows, 1, 1).astype(jnp.bfloat16)
    gate_preactivation = contract_pair(
        gate_weight, input_rows, 1, 1
    ) + ADAPTER_SCALE * contract_pair(gate_adapter_upper, gate_projected_lower, 1, 0)
    up_preactivation = contract_pair(up_weight, input_rows, 1, 1) + ADAPTER_SCALE * contract_pair(
        up_adapter_upper, up_projected_lower, 1, 0
    )
    sigmoid_gate = jax.nn.sigmoid(gate_preactivation)
    silu_gate = gate_preactivation * sigmoid_gate
    hidden_units = (silu_gate * up_preactivation).astype(jnp.bfloat16)
    down_projected_lower = contract_pair(b_down, output_gradient_rows, 0, 1).astype(jnp.bfloat16)
    hidden_gradient = contract_pair(
        down_weight, output_gradient_rows, 1, 1
    ) + ADAPTER_SCALE * contract_pair(down_adapter_lower, down_projected_lower, 0, 0)
    gate_gradient = (
        hidden_gradient
        * up_preactivation
        * sigmoid_gate
        * (1.0 + gate_preactivation * (1.0 - sigmoid_gate))
    ).astype(jnp.bfloat16)
    up_gradient = (hidden_gradient * silu_gate).astype(jnp.bfloat16)
    gate_partial = contract_pair(gate_adapter_upper, gate_gradient, 0, 0).astype(jnp.bfloat16)
    up_partial = contract_pair(up_adapter_upper, up_gradient, 0, 0).astype(jnp.bfloat16)
    down_partial = contract_pair(down_adapter_lower, hidden_units, 1, 0).astype(jnp.bfloat16)
    paired_partials = jnp.concatenate([gate_partial, up_partial], 0)
    paired_factors = jnp.concatenate([a_gate, a_up], 0)
    gradient_rows_out = (
        contract_pair(gate_gradient, gate_weight, 0, 0)
        + contract_pair(up_gradient, up_weight, 0, 0)
        + ADAPTER_SCALE * contract_pair(paired_partials, paired_factors, 0, 0)
    )
    shared_slice = (
        ADAPTER_SCALE * contract_pair(gate_partial, input_rows, 1, 0),
        ADAPTER_SCALE * contract_pair(up_partial, input_rows, 1, 0),
        ADAPTER_SCALE * contract_pair(output_gradient_rows, down_partial, 0, 1),
    )
    owned_slice = (
        ADAPTER_SCALE * contract_pair(gate_gradient, gate_projected_lower, 1, 1),
        ADAPTER_SCALE * contract_pair(up_gradient, up_projected_lower, 1, 1),
        ADAPTER_SCALE * contract_pair(down_projected_lower, hidden_units, 1, 1),
    )
    return (gradient_rows_out, shared_slice, owned_slice)


def rows_backward_parts(input_rows, output_gradient_rows, params):
    (
        gate_weight,
        up_weight,
        down_weight,
        a_gate,
        gate_adapter_upper,
        a_up,
        up_adapter_upper,
        down_adapter_lower,
        b_down,
    ) = params
    gate_projected_lower = contract_pair(a_gate, input_rows, 1, 1).astype(jnp.bfloat16)
    up_projected_lower = contract_pair(a_up, input_rows, 1, 1).astype(jnp.bfloat16)
    gate_preactivation = contract_pair(
        gate_weight, input_rows, 1, 1
    ) + ADAPTER_SCALE * contract_pair(gate_adapter_upper, gate_projected_lower, 1, 0)
    up_preactivation = contract_pair(up_weight, input_rows, 1, 1) + ADAPTER_SCALE * contract_pair(
        up_adapter_upper, up_projected_lower, 1, 0
    )
    sigmoid_gate = jax.nn.sigmoid(gate_preactivation)
    silu_gate = gate_preactivation * sigmoid_gate
    hidden_units = (silu_gate * up_preactivation).astype(jnp.bfloat16)
    down_projected_lower = contract_pair(b_down, output_gradient_rows, 0, 1).astype(jnp.bfloat16)
    hidden_gradient = contract_pair(
        down_weight, output_gradient_rows, 1, 1
    ) + ADAPTER_SCALE * contract_pair(down_adapter_lower, down_projected_lower, 0, 0)
    gate_gradient = (
        hidden_gradient
        * up_preactivation
        * sigmoid_gate
        * (1.0 + gate_preactivation * (1.0 - sigmoid_gate))
    ).astype(jnp.bfloat16)
    up_gradient = (hidden_gradient * silu_gate).astype(jnp.bfloat16)
    gate_partial = contract_pair(gate_gradient, gate_adapter_upper, 0, 0).astype(jnp.bfloat16)
    up_partial = contract_pair(up_gradient, up_adapter_upper, 0, 0).astype(jnp.bfloat16)
    down_partial = contract_pair(hidden_units, down_adapter_lower, 0, 1).astype(jnp.bfloat16)
    paired_partials = jnp.concatenate([gate_partial, up_partial], 1)
    paired_factors = jnp.concatenate([a_gate, a_up], 0)
    gradient_rows_out = (
        contract_pair(gate_gradient, gate_weight, 0, 0)
        + contract_pair(up_gradient, up_weight, 0, 0)
        + ADAPTER_SCALE * contract_pair(paired_partials, paired_factors, 1, 0)
    )
    parts = jnp.concatenate([gate_partial, up_partial, down_partial], 1)
    owned_slice = (
        ADAPTER_SCALE * contract_pair(gate_gradient, gate_projected_lower, 1, 1),
        ADAPTER_SCALE * contract_pair(up_gradient, up_projected_lower, 1, 1),
        ADAPTER_SCALE * contract_pair(down_projected_lower, hidden_units, 1, 1),
    )
    return (gradient_rows_out, parts, owned_slice)


def gather_dp_kernel(n, src_ref, out_ref, send_sem, recv_sem):
    me = lax.axis_index("dp")
    ex = lax.axis_index("expert")
    barrier = pltpu.get_barrier_semaphore()
    for k in range(1, n):
        peer = lax.rem(me + k, n)
        pl.semaphore_signal(barrier, inc=1, device_id=(peer, ex), device_id_type=MESH)
    pl.semaphore_wait(barrier, n - 1)
    copies = []
    for k in range(1, n):
        peer = lax.rem(me + k, n)
        cp = pltpu.make_async_remote_copy(
            src_ref,
            out_ref.at[me],
            send_sem.at[k],
            recv_sem.at[k],
            device_id=(peer, ex),
            device_id_type=MESH,
        )
        cp.start()
        copies.append(cp)
    out_ref[me] = src_ref[...]
    for cp in copies:
        cp.wait()


def gather_dp(block, n):
    return pl.pallas_call(
        functools.partial(gather_dp_kernel, n),
        out_shape=jax.ShapeDtypeStruct((n,) + block.shape, block.dtype),
        in_specs=[pl.BlockSpec(memory_space=pltpu.VMEM)],
        out_specs=pl.BlockSpec(memory_space=pltpu.VMEM),
        scratch_shapes=[pltpu.SemaphoreType.DMA((n,)), pltpu.SemaphoreType.DMA((n,))],
        compiler_params=pltpu.CompilerParams(collective_id=0, has_side_effects=True),
    )(block)


def local(
    tokens,
    output_gradient,
    routing,
    router_gate_values,
    gate_weight,
    up_weight,
    down_weight,
    adapter_lower_gate,
    adapter_upper_gate,
    adapter_lower_up,
    adapter_upper_up,
    adapter_lower_down,
    adapter_upper_down,
):
    experts = lax.axis_size("expert")
    shards = lax.axis_size("dp")
    tok_local, feat_local = tokens.shape
    choose = routing.shape[1]
    complete_width = feat_local * experts
    capacity = min(tok_local, 6 * tok_local // experts)
    adapter_rank = adapter_lower_gate.shape[1]
    chunks = NUM_CHUNKS
    piece = capacity // chunks
    params = (
        gate_weight[0],
        up_weight[0],
        down_weight[0],
        adapter_lower_gate[0],
        adapter_upper_gate[0],
        adapter_lower_up[0],
        adapter_upper_up[0],
        adapter_lower_down[0],
        adapter_upper_down[0],
    )
    positions = slot_numbers(routing, experts)
    zero_row = jnp.zeros((1, feat_local), jnp.bfloat16)
    source, member = slot_sources(routing, positions, experts, capacity)
    clamped = jnp.minimum(source, tok_local - 1)
    slot_gate = jnp.where(
        source < tok_local, router_gate_values.reshape(-1)[clamped * choose + member], 0.0
    )
    send_x = jnp.concatenate([tokens, zero_row], 0)[source].reshape(experts, capacity, feat_local)
    send_dy = (
        (
            slot_gate[:, None]
            * jnp.concatenate([output_gradient, zero_row], 0)[source].astype(jnp.float32)
        )
        .astype(jnp.bfloat16)
        .reshape(experts, capacity, feat_local)
    )
    send_both = jnp.concatenate([send_x, send_dy], axis=2)
    recv_both = lax.all_to_all(send_both, "expert", split_axis=0, concat_axis=2, tiled=True)[0]
    recv_both = recv_both.reshape(capacity, experts, 2, feat_local).transpose(2, 0, 1, 3)
    recv_both = recv_both.reshape(2, capacity, complete_width)

    rows_chunks = []
    part_chunks = []
    x_chunks = []
    dy_chunks = []
    owned_total = None
    for c in range(chunks):
        part = recv_both[:, c * piece:(c + 1) * piece]
        gathered = lax.all_gather(part, "dp", axis=1, tiled=True)
        x_rows = gathered[0]
        dy_rows = gathered[1]
        rows_out, parts, owned_slice = rows_backward_parts(x_rows, dy_rows, params)
        if c == 0:
            owned_total = owned_slice
        else:
            owned_total = jax.tree.map(jnp.add, owned_total, owned_slice)
        rows_chunks.append(rows_out.astype(jnp.bfloat16).reshape(shards, piece, complete_width))
        part_chunks.append(parts.reshape(shards, piece, 3 * adapter_rank))
        x_chunks.append(x_rows)
        dy_chunks.append(dy_rows)
    rows_all = jnp.concatenate(rows_chunks, 1)
    parts_all = jnp.concatenate(part_chunks, 1)
    parts_all = jnp.pad(parts_all, ((0, 0), (0, 0), (0, PART_COLS - 3 * adapter_rank)))
    packed = jnp.concatenate([rows_all, parts_all], 2)
    summed_packed = lax.psum_scatter(packed, "dp", scatter_dimension=0, tiled=True)[0]
    summed = summed_packed[:, :complete_width]
    parts_mine = summed_packed[:, complete_width:]
    parts_sum = gather_dp(parts_mine, shards).reshape(shards, chunks, piece, PART_COLS)
    grad_a_gate = None
    for c in range(chunks):
        parts_c = parts_sum[:, c].reshape(shards * piece, PART_COLS)
        a_gate_c = contract_pair(parts_c[:, :adapter_rank], x_chunks[c], 0, 0)
        a_up_c = contract_pair(parts_c[:, adapter_rank:2 * adapter_rank], x_chunks[c], 0, 0)
        b_down_c = contract_pair(dy_chunks[c], parts_c[:, 2 * adapter_rank:3 * adapter_rank], 0, 0)
        if grad_a_gate is None:
            grad_a_gate, grad_a_up, grad_b_down = a_gate_c, a_up_c, b_down_c
        else:
            grad_a_gate = grad_a_gate + a_gate_c
            grad_a_up = grad_a_up + a_up_c
            grad_b_down = grad_b_down + b_down_c
    grad_a_gate = ADAPTER_SCALE * grad_a_gate
    grad_a_up = ADAPTER_SCALE * grad_a_up
    grad_b_down = ADAPTER_SCALE * grad_b_down
    returned_rows = lax.all_to_all(
        summed.reshape(capacity, experts, feat_local),
        "expert",
        split_axis=1,
        concat_axis=1,
        tiled=True,
    ).astype(jnp.float32)
    lookup = positions * experts + routing
    grad_x = jnp.sum(returned_rows.reshape(capacity * experts, feat_local)[lookup], axis=1).astype(
        jnp.bfloat16
    )
    return (
        grad_x,
        grad_a_gate[None],
        owned_total[0][None],
        grad_a_up[None],
        owned_total[1][None],
        owned_total[2][None],
        grad_b_down[None],
    )


def solution(mesh):
    return jax.shard_map(
        local,
        mesh=mesh,
        in_specs=(
            P("dp", "expert"),
            P("dp", "expert"),
            P("dp", None),
            P("dp", None),
            P("expert", "dp", None),
            P("expert", "dp", None),
            P("expert", "dp", None),
            P("expert", None, None),
            P("expert", "dp", None),
            P("expert", None, None),
            P("expert", "dp", None),
            P("expert", None, "dp"),
            P("expert", None, None),
        ),
        out_specs=(
            P("dp", "expert"),
            P("expert", None, None),
            P("expert", "dp", None),
            P("expert", None, None),
            P("expert", "dp", None),
            P("expert", None, "dp"),
            P("expert", None, None),
        ),
        check_vma=False,
    )
```

```python
import functools

import jax
import jax.numpy as jnp
from jax import lax
from jax.experimental import pallas as pl
from jax.experimental.pallas import tpu as pltpu
from jax.sharding import PartitionSpec as P

MESH = pl.DeviceIdType.MESH

ADAPTER_SCALE = 2.0
NUM_CHUNKS = 2
PART_COLS = 128


def contract_pair(left, right, left_axis, right_axis):
    return lax.dot_general(
        left, right, (((left_axis,), (right_axis,)), ((), ())), preferred_element_type=jnp.float32
    )


def slot_numbers(route_rows, experts):
    picked = (route_rows[:, :, None] == jnp.arange(experts, dtype=jnp.int32)[None, None, :]).astype(
        jnp.int32
    )
    per_token = jnp.sum(picked, axis=1)
    earlier = jnp.cumsum(per_token, axis=0) - per_token
    return jnp.sum(earlier[:, None, :] * picked, axis=2)


def slot_sources(route_rows, positions, experts, capacity):
    tokens_here, choose = route_rows.shape
    target = (route_rows * capacity + positions).reshape(-1)
    owners = jnp.repeat(jnp.arange(tokens_here, dtype=jnp.int32), choose)
    member_ids = jnp.tile(jnp.arange(choose, dtype=jnp.int32), tokens_here)
    source = jnp.full((experts * capacity,), tokens_here, jnp.int32).at[target].set(owners)
    member = jnp.zeros((experts * capacity,), jnp.int32).at[target].set(member_ids)
    return (source, member)


def rows_backward_pass(input_rows, output_gradient_rows, params):
    (
        gate_weight,
        up_weight,
        down_weight,
        a_gate,
        gate_adapter_upper,
        a_up,
        up_adapter_upper,
        down_adapter_lower,
        b_down,
    ) = params
    gate_projected_lower = contract_pair(a_gate, input_rows, 1, 1).astype(jnp.bfloat16)
    up_projected_lower = contract_pair(a_up, input_rows, 1, 1).astype(jnp.bfloat16)
    gate_preactivation = contract_pair(
        gate_weight, input_rows, 1, 1
    ) + ADAPTER_SCALE * contract_pair(gate_adapter_upper, gate_projected_lower, 1, 0)
    up_preactivation = contract_pair(up_weight, input_rows, 1, 1) + ADAPTER_SCALE * contract_pair(
        up_adapter_upper, up_projected_lower, 1, 0
    )
    sigmoid_gate = jax.nn.sigmoid(gate_preactivation)
    silu_gate = gate_preactivation * sigmoid_gate
    hidden_units = (silu_gate * up_preactivation).astype(jnp.bfloat16)
    down_projected_lower = contract_pair(b_down, output_gradient_rows, 0, 1).astype(jnp.bfloat16)
    hidden_gradient = contract_pair(
        down_weight, output_gradient_rows, 1, 1
    ) + ADAPTER_SCALE * contract_pair(down_adapter_lower, down_projected_lower, 0, 0)
    gate_gradient = (
        hidden_gradient
        * up_preactivation
        * sigmoid_gate
        * (1.0 + gate_preactivation * (1.0 - sigmoid_gate))
    ).astype(jnp.bfloat16)
    up_gradient = (hidden_gradient * silu_gate).astype(jnp.bfloat16)
    gate_partial = contract_pair(gate_adapter_upper, gate_gradient, 0, 0).astype(jnp.bfloat16)
    up_partial = contract_pair(up_adapter_upper, up_gradient, 0, 0).astype(jnp.bfloat16)
    down_partial = contract_pair(down_adapter_lower, hidden_units, 1, 0).astype(jnp.bfloat16)
    paired_partials = jnp.concatenate([gate_partial, up_partial], 0)
    paired_factors = jnp.concatenate([a_gate, a_up], 0)
    gradient_rows_out = (
        contract_pair(gate_gradient, gate_weight, 0, 0)
        + contract_pair(up_gradient, up_weight, 0, 0)
        + ADAPTER_SCALE * contract_pair(paired_partials, paired_factors, 0, 0)
    )
    shared_slice = (
        ADAPTER_SCALE * contract_pair(gate_partial, input_rows, 1, 0),
        ADAPTER_SCALE * contract_pair(up_partial, input_rows, 1, 0),
        ADAPTER_SCALE * contract_pair(output_gradient_rows, down_partial, 0, 1),
    )
    owned_slice = (
        ADAPTER_SCALE * contract_pair(gate_gradient, gate_projected_lower, 1, 1),
        ADAPTER_SCALE * contract_pair(up_gradient, up_projected_lower, 1, 1),
        ADAPTER_SCALE * contract_pair(down_projected_lower, hidden_units, 1, 1),
    )
    return (gradient_rows_out, shared_slice, owned_slice)


def rows_backward_parts(input_rows, output_gradient_rows, params):
    (
        gate_weight,
        up_weight,
        down_weight,
        a_gate,
        gate_adapter_upper,
        a_up,
        up_adapter_upper,
        down_adapter_lower,
        b_down,
    ) = params
    gate_projected_lower = contract_pair(a_gate, input_rows, 1, 1).astype(jnp.bfloat16)
    up_projected_lower = contract_pair(a_up, input_rows, 1, 1).astype(jnp.bfloat16)
    gate_preactivation = contract_pair(
        gate_weight, input_rows, 1, 1
    ) + ADAPTER_SCALE * contract_pair(gate_adapter_upper, gate_projected_lower, 1, 0)
    up_preactivation = contract_pair(up_weight, input_rows, 1, 1) + ADAPTER_SCALE * contract_pair(
        up_adapter_upper, up_projected_lower, 1, 0
    )
    sigmoid_gate = jax.nn.sigmoid(gate_preactivation)
    silu_gate = gate_preactivation * sigmoid_gate
    hidden_units = (silu_gate * up_preactivation).astype(jnp.bfloat16)
    down_projected_lower = contract_pair(b_down, output_gradient_rows, 0, 1).astype(jnp.bfloat16)
    hidden_gradient = contract_pair(
        down_weight, output_gradient_rows, 1, 1
    ) + ADAPTER_SCALE * contract_pair(down_adapter_lower, down_projected_lower, 0, 0)
    gate_gradient = (
        hidden_gradient
        * up_preactivation
        * sigmoid_gate
        * (1.0 + gate_preactivation * (1.0 - sigmoid_gate))
    ).astype(jnp.bfloat16)
    up_gradient = (hidden_gradient * silu_gate).astype(jnp.bfloat16)
    gate_partial = contract_pair(gate_gradient, gate_adapter_upper, 0, 0).astype(jnp.bfloat16)
    up_partial = contract_pair(up_gradient, up_adapter_upper, 0, 0).astype(jnp.bfloat16)
    down_partial = contract_pair(hidden_units, down_adapter_lower, 0, 1).astype(jnp.bfloat16)
    paired_partials = jnp.concatenate([gate_partial, up_partial], 1)
    paired_factors = jnp.concatenate([a_gate, a_up], 0)
    gradient_rows_out = (
        contract_pair(gate_gradient, gate_weight, 0, 0)
        + contract_pair(up_gradient, up_weight, 0, 0)
        + ADAPTER_SCALE * contract_pair(paired_partials, paired_factors, 1, 0)
    )
    parts = jnp.concatenate([gate_partial, up_partial, down_partial], 1)
    owned_slice = (
        ADAPTER_SCALE * contract_pair(gate_gradient, gate_projected_lower, 1, 1),
        ADAPTER_SCALE * contract_pair(up_gradient, up_projected_lower, 1, 1),
        ADAPTER_SCALE * contract_pair(down_projected_lower, hidden_units, 1, 1),
    )
    return (gradient_rows_out, parts, owned_slice)


def gather_dp_kernel(n, src_ref, out_ref, send_sem, recv_sem):
    me = lax.axis_index("dp")
    ex = lax.axis_index("expert")
    barrier = pltpu.get_barrier_semaphore()
    for k in range(1, n):
        peer = lax.rem(me + k, n)
        pl.semaphore_signal(barrier, inc=1, device_id=(peer, ex), device_id_type=MESH)
    pl.semaphore_wait(barrier, n - 1)
    copies = []
    for k in range(1, n):
        peer = lax.rem(me + k, n)
        cp = pltpu.make_async_remote_copy(
            src_ref,
            out_ref.at[me],
            send_sem.at[k],
            recv_sem.at[k],
            device_id=(peer, ex),
            device_id_type=MESH,
        )
        cp.start()
        copies.append(cp)
    out_ref[me] = src_ref[...]
    for cp in copies:
        cp.wait()


def gather_dp(block, n):
    return pl.pallas_call(
        functools.partial(gather_dp_kernel, n),
        out_shape=jax.ShapeDtypeStruct((n,) + block.shape, block.dtype),
        in_specs=[pl.BlockSpec(memory_space=pltpu.VMEM)],
        out_specs=pl.BlockSpec(memory_space=pltpu.VMEM),
        scratch_shapes=[pltpu.SemaphoreType.DMA((n,)), pltpu.SemaphoreType.DMA((n,))],
        compiler_params=pltpu.CompilerParams(collective_id=0, has_side_effects=True),
    )(block)


def a2a_expert_kernel(n, src_ref, out_ref, send_sem, recv_sem):
    me = lax.axis_index("expert")
    row = lax.axis_index("dp")
    barrier = pltpu.get_barrier_semaphore()
    for k in range(1, n):
        peer = lax.rem(me + k, n)
        pl.semaphore_signal(barrier, inc=1, device_id=(row, peer), device_id_type=MESH)
    pl.semaphore_wait(barrier, n - 1)
    copies = []
    for k in range(1, n):
        peer = lax.rem(me + k, n)
        cp = pltpu.make_async_remote_copy(
            src_ref.at[peer],
            out_ref.at[me],
            send_sem.at[k],
            recv_sem.at[k],
            device_id=(row, peer),
            device_id_type=MESH,
        )
        cp.start()
        copies.append(cp)
    out_ref[me] = src_ref[me]
    for cp in copies:
        cp.wait()


def a2a_expert(blocks):
    n = blocks.shape[0]
    return pl.pallas_call(
        functools.partial(a2a_expert_kernel, n),
        out_shape=jax.ShapeDtypeStruct(blocks.shape, blocks.dtype),
        in_specs=[pl.BlockSpec(memory_space=pltpu.VMEM)],
        out_specs=pl.BlockSpec(memory_space=pltpu.VMEM),
        scratch_shapes=[pltpu.SemaphoreType.DMA((n,)), pltpu.SemaphoreType.DMA((n,))],
        compiler_params=pltpu.CompilerParams(collective_id=1, has_side_effects=True),
    )(blocks)


def local(
    tokens,
    output_gradient,
    routing,
    router_gate_values,
    gate_weight,
    up_weight,
    down_weight,
    adapter_lower_gate,
    adapter_upper_gate,
    adapter_lower_up,
    adapter_upper_up,
    adapter_lower_down,
    adapter_upper_down,
):
    experts = lax.axis_size("expert")
    shards = lax.axis_size("dp")
    tok_local, feat_local = tokens.shape
    choose = routing.shape[1]
    complete_width = feat_local * experts
    capacity = min(tok_local, 6 * tok_local // experts)
    adapter_rank = adapter_lower_gate.shape[1]
    chunks = NUM_CHUNKS
    piece = capacity // chunks
    params = (
        gate_weight[0],
        up_weight[0],
        down_weight[0],
        adapter_lower_gate[0],
        adapter_upper_gate[0],
        adapter_lower_up[0],
        adapter_upper_up[0],
        adapter_lower_down[0],
        adapter_upper_down[0],
    )
    positions = slot_numbers(routing, experts)
    zero_row = jnp.zeros((1, feat_local), jnp.bfloat16)
    source, member = slot_sources(routing, positions, experts, capacity)
    clamped = jnp.minimum(source, tok_local - 1)
    slot_gate = jnp.where(
        source < tok_local, router_gate_values.reshape(-1)[clamped * choose + member], 0.0
    )
    send_x = jnp.concatenate([tokens, zero_row], 0)[source].reshape(experts, capacity, feat_local)
    send_dy = (
        (
            slot_gate[:, None]
            * jnp.concatenate([output_gradient, zero_row], 0)[source].astype(jnp.float32)
        )
        .astype(jnp.bfloat16)
        .reshape(experts, capacity, feat_local)
    )
    send_both = jnp.concatenate([send_x, send_dy], axis=2)
    recv_both = a2a_expert(send_both)
    recv_both = recv_both.reshape(experts, capacity, 2, feat_local).transpose(2, 1, 0, 3)
    recv_both = recv_both.reshape(2, capacity, complete_width)

    rows_chunks = []
    part_chunks = []
    x_chunks = []
    dy_chunks = []
    owned_total = None
    for c in range(chunks):
        part = recv_both[:, c * piece:(c + 1) * piece]
        gathered = lax.all_gather(part, "dp", axis=1, tiled=True)
        x_rows = gathered[0]
        dy_rows = gathered[1]
        rows_out, parts, owned_slice = rows_backward_parts(x_rows, dy_rows, params)
        if c == 0:
            owned_total = owned_slice
        else:
            owned_total = jax.tree.map(jnp.add, owned_total, owned_slice)
        rows_chunks.append(rows_out.astype(jnp.bfloat16).reshape(shards, piece, complete_width))
        part_chunks.append(parts.reshape(shards, piece, 3 * adapter_rank))
        x_chunks.append(x_rows)
        dy_chunks.append(dy_rows)
    rows_all = jnp.concatenate(rows_chunks, 1)
    parts_all = jnp.concatenate(part_chunks, 1)
    parts_all = jnp.pad(parts_all, ((0, 0), (0, 0), (0, PART_COLS - 3 * adapter_rank)))
    packed = jnp.concatenate([rows_all, parts_all], 2)
    summed_packed = lax.psum_scatter(packed, "dp", scatter_dimension=0, tiled=True)[0]
    summed = summed_packed[:, :complete_width]
    parts_mine = summed_packed[:, complete_width:]
    parts_sum = gather_dp(parts_mine, shards).reshape(shards, chunks, piece, PART_COLS)
    grad_a_gate = None
    for c in range(chunks):
        parts_c = parts_sum[:, c].reshape(shards * piece, PART_COLS)
        a_gate_c = contract_pair(parts_c[:, :adapter_rank], x_chunks[c], 0, 0)
        a_up_c = contract_pair(parts_c[:, adapter_rank:2 * adapter_rank], x_chunks[c], 0, 0)
        b_down_c = contract_pair(dy_chunks[c], parts_c[:, 2 * adapter_rank:3 * adapter_rank], 0, 0)
        if grad_a_gate is None:
            grad_a_gate, grad_a_up, grad_b_down = a_gate_c, a_up_c, b_down_c
        else:
            grad_a_gate = grad_a_gate + a_gate_c
            grad_a_up = grad_a_up + a_up_c
            grad_b_down = grad_b_down + b_down_c
    grad_a_gate = ADAPTER_SCALE * grad_a_gate
    grad_a_up = ADAPTER_SCALE * grad_a_up
    grad_b_down = ADAPTER_SCALE * grad_b_down
    returned_rows = lax.all_to_all(
        summed.reshape(capacity, experts, feat_local),
        "expert",
        split_axis=1,
        concat_axis=1,
        tiled=True,
    ).astype(jnp.float32)
    lookup = positions * experts + routing
    grad_x = jnp.sum(returned_rows.reshape(capacity * experts, feat_local)[lookup], axis=1).astype(
        jnp.bfloat16
    )
    return (
        grad_x,
        grad_a_gate[None],
        owned_total[0][None],
        grad_a_up[None],
        owned_total[1][None],
        owned_total[2][None],
        grad_b_down[None],
    )


def solution(mesh):
    return jax.shard_map(
        local,
        mesh=mesh,
        in_specs=(
            P("dp", "expert"),
            P("dp", "expert"),
            P("dp", None),
            P("dp", None),
            P("expert", "dp", None),
            P("expert", "dp", None),
            P("expert", "dp", None),
            P("expert", None, None),
            P("expert", "dp", None),
            P("expert", None, None),
            P("expert", "dp", None),
            P("expert", None, "dp"),
            P("expert", None, None),
        ),
        out_specs=(
            P("dp", "expert"),
            P("expert", None, None),
            P("expert", "dp", None),
            P("expert", None, None),
            P("expert", "dp", None),
            P("expert", None, "dp"),
            P("expert", None, None),
        ),
        check_vma=False,
    )
```

```python
import functools

import jax
import jax.numpy as jnp
from jax import lax
from jax.experimental import pallas as pl
from jax.experimental.pallas import tpu as pltpu
from jax.sharding import PartitionSpec as P

MESH = pl.DeviceIdType.MESH

ADAPTER_SCALE = 2.0
NUM_CHUNKS = 2
PART_COLS = 128


def contract_pair(left, right, left_axis, right_axis):
    return lax.dot_general(
        left, right, (((left_axis,), (right_axis,)), ((), ())), preferred_element_type=jnp.float32
    )


def slot_numbers(route_rows, experts):
    picked = (route_rows[:, :, None] == jnp.arange(experts, dtype=jnp.int32)[None, None, :]).astype(
        jnp.int32
    )
    per_token = jnp.sum(picked, axis=1)
    earlier = jnp.cumsum(per_token, axis=0) - per_token
    return jnp.sum(earlier[:, None, :] * picked, axis=2)


def slot_sources(route_rows, positions, experts, capacity):
    tokens_here, choose = route_rows.shape
    target = (route_rows * capacity + positions).reshape(-1)
    owners = jnp.repeat(jnp.arange(tokens_here, dtype=jnp.int32), choose)
    member_ids = jnp.tile(jnp.arange(choose, dtype=jnp.int32), tokens_here)
    source = jnp.full((experts * capacity,), tokens_here, jnp.int32).at[target].set(owners)
    member = jnp.zeros((experts * capacity,), jnp.int32).at[target].set(member_ids)
    return (source, member)


def rows_backward_pass(input_rows, output_gradient_rows, params):
    (
        gate_weight,
        up_weight,
        down_weight,
        a_gate,
        gate_adapter_upper,
        a_up,
        up_adapter_upper,
        down_adapter_lower,
        b_down,
    ) = params
    gate_projected_lower = contract_pair(a_gate, input_rows, 1, 1).astype(jnp.bfloat16)
    up_projected_lower = contract_pair(a_up, input_rows, 1, 1).astype(jnp.bfloat16)
    gate_preactivation = contract_pair(
        gate_weight, input_rows, 1, 1
    ) + ADAPTER_SCALE * contract_pair(gate_adapter_upper, gate_projected_lower, 1, 0)
    up_preactivation = contract_pair(up_weight, input_rows, 1, 1) + ADAPTER_SCALE * contract_pair(
        up_adapter_upper, up_projected_lower, 1, 0
    )
    sigmoid_gate = jax.nn.sigmoid(gate_preactivation)
    silu_gate = gate_preactivation * sigmoid_gate
    hidden_units = (silu_gate * up_preactivation).astype(jnp.bfloat16)
    down_projected_lower = contract_pair(b_down, output_gradient_rows, 0, 1).astype(jnp.bfloat16)
    hidden_gradient = contract_pair(
        down_weight, output_gradient_rows, 1, 1
    ) + ADAPTER_SCALE * contract_pair(down_adapter_lower, down_projected_lower, 0, 0)
    gate_gradient = (
        hidden_gradient
        * up_preactivation
        * sigmoid_gate
        * (1.0 + gate_preactivation * (1.0 - sigmoid_gate))
    ).astype(jnp.bfloat16)
    up_gradient = (hidden_gradient * silu_gate).astype(jnp.bfloat16)
    gate_partial = contract_pair(gate_adapter_upper, gate_gradient, 0, 0).astype(jnp.bfloat16)
    up_partial = contract_pair(up_adapter_upper, up_gradient, 0, 0).astype(jnp.bfloat16)
    down_partial = contract_pair(down_adapter_lower, hidden_units, 1, 0).astype(jnp.bfloat16)
    paired_partials = jnp.concatenate([gate_partial, up_partial], 0)
    paired_factors = jnp.concatenate([a_gate, a_up], 0)
    gradient_rows_out = (
        contract_pair(gate_gradient, gate_weight, 0, 0)
        + contract_pair(up_gradient, up_weight, 0, 0)
        + ADAPTER_SCALE * contract_pair(paired_partials, paired_factors, 0, 0)
    )
    shared_slice = (
        ADAPTER_SCALE * contract_pair(gate_partial, input_rows, 1, 0),
        ADAPTER_SCALE * contract_pair(up_partial, input_rows, 1, 0),
        ADAPTER_SCALE * contract_pair(output_gradient_rows, down_partial, 0, 1),
    )
    owned_slice = (
        ADAPTER_SCALE * contract_pair(gate_gradient, gate_projected_lower, 1, 1),
        ADAPTER_SCALE * contract_pair(up_gradient, up_projected_lower, 1, 1),
        ADAPTER_SCALE * contract_pair(down_projected_lower, hidden_units, 1, 1),
    )
    return (gradient_rows_out, shared_slice, owned_slice)


def rows_backward_parts(input_rows, output_gradient_rows, params):
    (
        gate_weight,
        up_weight,
        down_weight,
        a_gate,
        gate_adapter_upper,
        a_up,
        up_adapter_upper,
        down_adapter_lower,
        b_down,
    ) = params
    gate_projected_lower = contract_pair(a_gate, input_rows, 1, 1).astype(jnp.bfloat16)
    up_projected_lower = contract_pair(a_up, input_rows, 1, 1).astype(jnp.bfloat16)
    gate_preactivation = contract_pair(
        gate_weight, input_rows, 1, 1
    ) + ADAPTER_SCALE * contract_pair(gate_adapter_upper, gate_projected_lower, 1, 0)
    up_preactivation = contract_pair(up_weight, input_rows, 1, 1) + ADAPTER_SCALE * contract_pair(
        up_adapter_upper, up_projected_lower, 1, 0
    )
    sigmoid_gate = jax.nn.sigmoid(gate_preactivation)
    silu_gate = gate_preactivation * sigmoid_gate
    hidden_units = (silu_gate * up_preactivation).astype(jnp.bfloat16)
    down_partial = contract_pair(hidden_units, down_adapter_lower, 0, 1).astype(jnp.bfloat16)
    (
        output_gradient_rows,
        gate_preactivation,
        up_preactivation,
        sigmoid_gate,
        silu_gate,
        hidden_units,
        down_partial,
        gate_projected_lower,
        up_projected_lower,
    ) = lax.optimization_barrier(
        (
            output_gradient_rows,
            gate_preactivation,
            up_preactivation,
            sigmoid_gate,
            silu_gate,
            hidden_units,
            down_partial,
            gate_projected_lower,
            up_projected_lower,
        )
    )
    down_projected_lower = contract_pair(b_down, output_gradient_rows, 0, 1).astype(jnp.bfloat16)
    hidden_gradient = contract_pair(
        down_weight, output_gradient_rows, 1, 1
    ) + ADAPTER_SCALE * contract_pair(down_adapter_lower, down_projected_lower, 0, 0)
    gate_gradient = (
        hidden_gradient
        * up_preactivation
        * sigmoid_gate
        * (1.0 + gate_preactivation * (1.0 - sigmoid_gate))
    ).astype(jnp.bfloat16)
    up_gradient = (hidden_gradient * silu_gate).astype(jnp.bfloat16)
    gate_partial = contract_pair(gate_gradient, gate_adapter_upper, 0, 0).astype(jnp.bfloat16)
    up_partial = contract_pair(up_gradient, up_adapter_upper, 0, 0).astype(jnp.bfloat16)
    paired_partials = jnp.concatenate([gate_partial, up_partial], 1)
    paired_factors = jnp.concatenate([a_gate, a_up], 0)
    gradient_rows_out = (
        contract_pair(gate_gradient, gate_weight, 0, 0)
        + contract_pair(up_gradient, up_weight, 0, 0)
        + ADAPTER_SCALE * contract_pair(paired_partials, paired_factors, 1, 0)
    )
    parts = jnp.concatenate([gate_partial, up_partial, down_partial], 1)
    owned_slice = (
        ADAPTER_SCALE * contract_pair(gate_gradient, gate_projected_lower, 1, 1),
        ADAPTER_SCALE * contract_pair(up_gradient, up_projected_lower, 1, 1),
        ADAPTER_SCALE * contract_pair(down_projected_lower, hidden_units, 1, 1),
    )
    return (gradient_rows_out, parts, owned_slice)


def gather_dp_kernel(n, src_ref, out_ref, send_sem, recv_sem):
    me = lax.axis_index("dp")
    ex = lax.axis_index("expert")
    barrier = pltpu.get_barrier_semaphore()
    for k in range(1, n):
        peer = lax.rem(me + k, n)
        pl.semaphore_signal(barrier, inc=1, device_id=(peer, ex), device_id_type=MESH)
    pl.semaphore_wait(barrier, n - 1)
    copies = []
    for k in range(1, n):
        peer = lax.rem(me + k, n)
        cp = pltpu.make_async_remote_copy(
            src_ref,
            out_ref.at[me],
            send_sem.at[k],
            recv_sem.at[k],
            device_id=(peer, ex),
            device_id_type=MESH,
        )
        cp.start()
        copies.append(cp)
    out_ref[me] = src_ref[...]
    for cp in copies:
        cp.wait()


def gather_dp(block, n):
    return pl.pallas_call(
        functools.partial(gather_dp_kernel, n),
        out_shape=jax.ShapeDtypeStruct((n,) + block.shape, block.dtype),
        in_specs=[pl.BlockSpec(memory_space=pltpu.VMEM)],
        out_specs=pl.BlockSpec(memory_space=pltpu.VMEM),
        scratch_shapes=[pltpu.SemaphoreType.DMA((n,)), pltpu.SemaphoreType.DMA((n,))],
        compiler_params=pltpu.CompilerParams(collective_id=0, has_side_effects=True),
    )(block)


def a2a_expert_kernel(n, src_ref, out_ref, send_sem, recv_sem):
    me = lax.axis_index("expert")
    row = lax.axis_index("dp")
    barrier = pltpu.get_barrier_semaphore()
    for k in range(1, n):
        peer = lax.rem(me + k, n)
        pl.semaphore_signal(barrier, inc=1, device_id=(row, peer), device_id_type=MESH)
    pl.semaphore_wait(barrier, n - 1)
    copies = []
    for k in range(1, n):
        peer = lax.rem(me + k, n)
        cp = pltpu.make_async_remote_copy(
            src_ref.at[peer],
            out_ref.at[me],
            send_sem.at[k],
            recv_sem.at[k],
            device_id=(row, peer),
            device_id_type=MESH,
        )
        cp.start()
        copies.append(cp)
    out_ref[me] = src_ref[me]
    for cp in copies:
        cp.wait()


def a2a_expert(blocks):
    n = blocks.shape[0]
    return pl.pallas_call(
        functools.partial(a2a_expert_kernel, n),
        out_shape=jax.ShapeDtypeStruct(blocks.shape, blocks.dtype),
        in_specs=[pl.BlockSpec(memory_space=pltpu.VMEM)],
        out_specs=pl.BlockSpec(memory_space=pltpu.VMEM),
        scratch_shapes=[pltpu.SemaphoreType.DMA((n,)), pltpu.SemaphoreType.DMA((n,))],
        compiler_params=pltpu.CompilerParams(collective_id=1, has_side_effects=True),
    )(blocks)


def local(
    tokens,
    output_gradient,
    routing,
    router_gate_values,
    gate_weight,
    up_weight,
    down_weight,
    adapter_lower_gate,
    adapter_upper_gate,
    adapter_lower_up,
    adapter_upper_up,
    adapter_lower_down,
    adapter_upper_down,
):
    experts = lax.axis_size("expert")
    shards = lax.axis_size("dp")
    tok_local, feat_local = tokens.shape
    choose = routing.shape[1]
    complete_width = feat_local * experts
    capacity = min(tok_local, 6 * tok_local // experts)
    adapter_rank = adapter_lower_gate.shape[1]
    chunks = NUM_CHUNKS
    piece = capacity // chunks
    params = (
        gate_weight[0],
        up_weight[0],
        down_weight[0],
        adapter_lower_gate[0],
        adapter_upper_gate[0],
        adapter_lower_up[0],
        adapter_upper_up[0],
        adapter_lower_down[0],
        adapter_upper_down[0],
    )
    positions = slot_numbers(routing, experts)
    zero_row = jnp.zeros((1, feat_local), jnp.bfloat16)
    source, member = slot_sources(routing, positions, experts, capacity)
    clamped = jnp.minimum(source, tok_local - 1)
    slot_gate = jnp.where(
        source < tok_local, router_gate_values.reshape(-1)[clamped * choose + member], 0.0
    )
    send_x = jnp.concatenate([tokens, zero_row], 0)[source].reshape(experts, capacity, feat_local)
    send_dy = (
        (
            slot_gate[:, None]
            * jnp.concatenate([output_gradient, zero_row], 0)[source].astype(jnp.float32)
        )
        .astype(jnp.bfloat16)
        .reshape(experts, capacity, feat_local)
    )
    send_both = jnp.concatenate([send_x, send_dy], axis=2)
    recv_both = a2a_expert(send_both)
    recv_both = recv_both.reshape(experts, capacity, 2, feat_local).transpose(2, 1, 0, 3)
    recv_both = recv_both.reshape(2, capacity, complete_width)

    x_rows = lax.all_gather(recv_both[0], "dp", axis=0, tiled=True)
    dy_rows = lax.all_gather(recv_both[1], "dp", axis=0, tiled=True)
    rows_out, parts, owned_total = rows_backward_parts(x_rows, dy_rows, params)
    rows_all = rows_out.astype(jnp.bfloat16)
    parts_all = jnp.pad(parts, ((0, 0), (0, PART_COLS - 3 * adapter_rank)))
    packed = jnp.concatenate([rows_all, parts_all], 1).reshape(
        shards, capacity, complete_width + PART_COLS
    )
    summed_packed = lax.psum_scatter(packed, "dp", scatter_dimension=0, tiled=True)[0]
    summed = summed_packed[:, :complete_width]
    parts_mine = summed_packed[:, complete_width:]
    parts_sum = gather_dp(parts_mine, shards).reshape(shards * capacity, PART_COLS)
    grad_a_gate = ADAPTER_SCALE * contract_pair(parts_sum[:, :adapter_rank], x_rows, 0, 0)
    grad_a_up = ADAPTER_SCALE * contract_pair(
        parts_sum[:, adapter_rank:2 * adapter_rank], x_rows, 0, 0
    )
    grad_b_down = ADAPTER_SCALE * contract_pair(
        dy_rows, parts_sum[:, 2 * adapter_rank:3 * adapter_rank], 0, 0
    )
    returned_rows = lax.all_to_all(
        summed.reshape(capacity, experts, feat_local),
        "expert",
        split_axis=1,
        concat_axis=1,
        tiled=True,
    ).astype(jnp.float32)
    lookup = positions * experts + routing
    grad_x = jnp.sum(returned_rows.reshape(capacity * experts, feat_local)[lookup], axis=1).astype(
        jnp.bfloat16
    )
    return (
        grad_x,
        grad_a_gate[None],
        owned_total[0][None],
        grad_a_up[None],
        owned_total[1][None],
        owned_total[2][None],
        grad_b_down[None],
    )


def solution(mesh):
    return jax.shard_map(
        local,
        mesh=mesh,
        in_specs=(
            P("dp", "expert"),
            P("dp", "expert"),
            P("dp", None),
            P("dp", None),
            P("expert", "dp", None),
            P("expert", "dp", None),
            P("expert", "dp", None),
            P("expert", None, None),
            P("expert", "dp", None),
            P("expert", None, None),
            P("expert", "dp", None),
            P("expert", None, "dp"),
            P("expert", None, None),
        ),
        out_specs=(
            P("dp", "expert"),
            P("expert", None, None),
            P("expert", "dp", None),
            P("expert", None, None),
            P("expert", "dp", None),
            P("expert", None, "dp"),
            P("expert", None, None),
        ),
        check_vma=False,
    )
```

```python
import functools

import jax
import jax.numpy as jnp
from jax import lax
from jax.experimental import pallas as pl
from jax.experimental.pallas import tpu as pltpu
from jax.sharding import PartitionSpec as P

MESH = pl.DeviceIdType.MESH

ADAPTER_SCALE = 2.0
NUM_CHUNKS = 2
PART_COLS = 128


def contract_pair(left, right, left_axis, right_axis):
    return lax.dot_general(
        left, right, (((left_axis,), (right_axis,)), ((), ())), preferred_element_type=jnp.float32
    )


def slot_numbers(route_rows, experts):
    picked = (route_rows[:, :, None] == jnp.arange(experts, dtype=jnp.int32)[None, None, :]).astype(
        jnp.int32
    )
    per_token = jnp.sum(picked, axis=1)
    earlier = jnp.cumsum(per_token, axis=0) - per_token
    return jnp.sum(earlier[:, None, :] * picked, axis=2)


def slot_sources(route_rows, positions, experts, capacity):
    tokens_here, choose = route_rows.shape
    target = (route_rows * capacity + positions).reshape(-1)
    owners = jnp.repeat(jnp.arange(tokens_here, dtype=jnp.int32), choose)
    member_ids = jnp.tile(jnp.arange(choose, dtype=jnp.int32), tokens_here)
    source = jnp.full((experts * capacity,), tokens_here, jnp.int32).at[target].set(owners)
    member = jnp.zeros((experts * capacity,), jnp.int32).at[target].set(member_ids)
    return (source, member)


def rows_backward_pass(input_rows, output_gradient_rows, params):
    (
        gate_weight,
        up_weight,
        down_weight,
        a_gate,
        gate_adapter_upper,
        a_up,
        up_adapter_upper,
        down_adapter_lower,
        b_down,
    ) = params
    gate_projected_lower = contract_pair(a_gate, input_rows, 1, 1).astype(jnp.bfloat16)
    up_projected_lower = contract_pair(a_up, input_rows, 1, 1).astype(jnp.bfloat16)
    gate_preactivation = contract_pair(
        gate_weight, input_rows, 1, 1
    ) + ADAPTER_SCALE * contract_pair(gate_adapter_upper, gate_projected_lower, 1, 0)
    up_preactivation = contract_pair(up_weight, input_rows, 1, 1) + ADAPTER_SCALE * contract_pair(
        up_adapter_upper, up_projected_lower, 1, 0
    )
    sigmoid_gate = jax.nn.sigmoid(gate_preactivation)
    silu_gate = gate_preactivation * sigmoid_gate
    hidden_units = (silu_gate * up_preactivation).astype(jnp.bfloat16)
    down_projected_lower = contract_pair(b_down, output_gradient_rows, 0, 1).astype(jnp.bfloat16)
    hidden_gradient = contract_pair(
        down_weight, output_gradient_rows, 1, 1
    ) + ADAPTER_SCALE * contract_pair(down_adapter_lower, down_projected_lower, 0, 0)
    gate_gradient = (
        hidden_gradient
        * up_preactivation
        * sigmoid_gate
        * (1.0 + gate_preactivation * (1.0 - sigmoid_gate))
    ).astype(jnp.bfloat16)
    up_gradient = (hidden_gradient * silu_gate).astype(jnp.bfloat16)
    gate_partial = contract_pair(gate_adapter_upper, gate_gradient, 0, 0).astype(jnp.bfloat16)
    up_partial = contract_pair(up_adapter_upper, up_gradient, 0, 0).astype(jnp.bfloat16)
    down_partial = contract_pair(down_adapter_lower, hidden_units, 1, 0).astype(jnp.bfloat16)
    paired_partials = jnp.concatenate([gate_partial, up_partial], 0)
    paired_factors = jnp.concatenate([a_gate, a_up], 0)
    gradient_rows_out = (
        contract_pair(gate_gradient, gate_weight, 0, 0)
        + contract_pair(up_gradient, up_weight, 0, 0)
        + ADAPTER_SCALE * contract_pair(paired_partials, paired_factors, 0, 0)
    )
    shared_slice = (
        ADAPTER_SCALE * contract_pair(gate_partial, input_rows, 1, 0),
        ADAPTER_SCALE * contract_pair(up_partial, input_rows, 1, 0),
        ADAPTER_SCALE * contract_pair(output_gradient_rows, down_partial, 0, 1),
    )
    owned_slice = (
        ADAPTER_SCALE * contract_pair(gate_gradient, gate_projected_lower, 1, 1),
        ADAPTER_SCALE * contract_pair(up_gradient, up_projected_lower, 1, 1),
        ADAPTER_SCALE * contract_pair(down_projected_lower, hidden_units, 1, 1),
    )
    return (gradient_rows_out, shared_slice, owned_slice)


def rows_backward_parts(input_rows, output_gradient_rows, params):
    (
        gate_weight,
        up_weight,
        down_weight,
        a_gate,
        gate_adapter_upper,
        a_up,
        up_adapter_upper,
        down_adapter_lower,
        b_down,
    ) = params
    gate_projected_lower = contract_pair(a_gate, input_rows, 1, 1).astype(jnp.bfloat16)
    up_projected_lower = contract_pair(a_up, input_rows, 1, 1).astype(jnp.bfloat16)
    gate_preactivation = contract_pair(
        gate_weight, input_rows, 1, 1
    ) + ADAPTER_SCALE * contract_pair(gate_adapter_upper, gate_projected_lower, 1, 0)
    up_preactivation = contract_pair(up_weight, input_rows, 1, 1) + ADAPTER_SCALE * contract_pair(
        up_adapter_upper, up_projected_lower, 1, 0
    )
    sigmoid_gate = jax.nn.sigmoid(gate_preactivation)
    silu_gate = gate_preactivation * sigmoid_gate
    hidden_units = (silu_gate * up_preactivation).astype(jnp.bfloat16)
    down_partial = contract_pair(hidden_units, down_adapter_lower, 0, 1).astype(jnp.bfloat16)
    (
        output_gradient_rows,
        gate_preactivation,
        up_preactivation,
        sigmoid_gate,
        silu_gate,
        hidden_units,
        down_partial,
        gate_projected_lower,
        up_projected_lower,
    ) = lax.optimization_barrier(
        (
            output_gradient_rows,
            gate_preactivation,
            up_preactivation,
            sigmoid_gate,
            silu_gate,
            hidden_units,
            down_partial,
            gate_projected_lower,
            up_projected_lower,
        )
    )
    down_projected_lower = contract_pair(b_down, output_gradient_rows, 0, 1).astype(jnp.bfloat16)
    hidden_gradient = contract_pair(
        down_weight, output_gradient_rows, 1, 1
    ) + ADAPTER_SCALE * contract_pair(down_adapter_lower, down_projected_lower, 0, 0)
    gate_gradient = (
        hidden_gradient
        * up_preactivation
        * sigmoid_gate
        * (1.0 + gate_preactivation * (1.0 - sigmoid_gate))
    ).astype(jnp.bfloat16)
    up_gradient = (hidden_gradient * silu_gate).astype(jnp.bfloat16)
    gate_partial = contract_pair(gate_gradient, gate_adapter_upper, 0, 0).astype(jnp.bfloat16)
    up_partial = contract_pair(up_gradient, up_adapter_upper, 0, 0).astype(jnp.bfloat16)
    parts = jnp.concatenate([gate_partial, up_partial, down_partial], 1)
    rank3 = parts.shape[1]
    hidden_here, width = gate_weight.shape
    lhs = jnp.concatenate([gate_gradient, up_gradient, parts.T], 0)
    lora_rows = jnp.concatenate(
        [
            (ADAPTER_SCALE * a_gate.astype(jnp.float32)).astype(jnp.bfloat16),
            (ADAPTER_SCALE * a_up.astype(jnp.float32)).astype(jnp.bfloat16),
            jnp.zeros((rank3 - a_gate.shape[0] - a_up.shape[0], width), jnp.bfloat16),
        ],
        0,
    )
    left_block = jnp.concatenate([gate_weight, up_weight, lora_rows], 0)
    picker = (
        jnp.arange(2 * hidden_here + rank3, dtype=jnp.int32)[:, None] - 2 * hidden_here
        == jnp.arange(PART_COLS, dtype=jnp.int32)[None, :]
    ).astype(jnp.bfloat16)
    extended = jnp.concatenate([left_block, picker], 1)
    gradient_rows_out = lax.dot_general(
        lhs, extended, (((0,), (0,)), ((), ())), preferred_element_type=jnp.float32
    ).astype(jnp.bfloat16)
    owned_slice = (
        ADAPTER_SCALE * contract_pair(gate_gradient, gate_projected_lower, 1, 1),
        ADAPTER_SCALE * contract_pair(up_gradient, up_projected_lower, 1, 1),
        ADAPTER_SCALE * contract_pair(down_projected_lower, hidden_units, 1, 1),
    )
    return (gradient_rows_out, parts, owned_slice)


def gather_dp_kernel(n, src_ref, out_ref, send_sem, recv_sem):
    me = lax.axis_index("dp")
    ex = lax.axis_index("expert")
    barrier = pltpu.get_barrier_semaphore()
    for k in range(1, n):
        peer = lax.rem(me + k, n)
        pl.semaphore_signal(barrier, inc=1, device_id=(peer, ex), device_id_type=MESH)
    pl.semaphore_wait(barrier, n - 1)
    copies = []
    for k in range(1, n):
        peer = lax.rem(me + k, n)
        cp = pltpu.make_async_remote_copy(
            src_ref,
            out_ref.at[me],
            send_sem.at[k],
            recv_sem.at[k],
            device_id=(peer, ex),
            device_id_type=MESH,
        )
        cp.start()
        copies.append(cp)
    out_ref[me] = src_ref[...]
    for cp in copies:
        cp.wait()


def gather_dp(block, n):
    return pl.pallas_call(
        functools.partial(gather_dp_kernel, n),
        out_shape=jax.ShapeDtypeStruct((n,) + block.shape, block.dtype),
        in_specs=[pl.BlockSpec(memory_space=pltpu.VMEM)],
        out_specs=pl.BlockSpec(memory_space=pltpu.VMEM),
        scratch_shapes=[pltpu.SemaphoreType.DMA((n,)), pltpu.SemaphoreType.DMA((n,))],
        compiler_params=pltpu.CompilerParams(collective_id=0, has_side_effects=True),
    )(block)


def a2a_expert_kernel(n, src_ref, out_ref, send_sem, recv_sem):
    me = lax.axis_index("expert")
    row = lax.axis_index("dp")
    barrier = pltpu.get_barrier_semaphore()
    for k in range(1, n):
        peer = lax.rem(me + k, n)
        pl.semaphore_signal(barrier, inc=1, device_id=(row, peer), device_id_type=MESH)
    pl.semaphore_wait(barrier, n - 1)
    copies = []
    for k in range(1, n):
        peer = lax.rem(me + k, n)
        cp = pltpu.make_async_remote_copy(
            src_ref.at[peer],
            out_ref.at[me],
            send_sem.at[k],
            recv_sem.at[k],
            device_id=(row, peer),
            device_id_type=MESH,
        )
        cp.start()
        copies.append(cp)
    out_ref[me] = src_ref[me]
    for cp in copies:
        cp.wait()


def a2a_expert(blocks):
    n = blocks.shape[0]
    return pl.pallas_call(
        functools.partial(a2a_expert_kernel, n),
        out_shape=jax.ShapeDtypeStruct(blocks.shape, blocks.dtype),
        in_specs=[pl.BlockSpec(memory_space=pltpu.VMEM)],
        out_specs=pl.BlockSpec(memory_space=pltpu.VMEM),
        scratch_shapes=[pltpu.SemaphoreType.DMA((n,)), pltpu.SemaphoreType.DMA((n,))],
        compiler_params=pltpu.CompilerParams(collective_id=1, has_side_effects=True),
    )(blocks)


def local(
    tokens,
    output_gradient,
    routing,
    router_gate_values,
    gate_weight,
    up_weight,
    down_weight,
    adapter_lower_gate,
    adapter_upper_gate,
    adapter_lower_up,
    adapter_upper_up,
    adapter_lower_down,
    adapter_upper_down,
):
    experts = lax.axis_size("expert")
    shards = lax.axis_size("dp")
    tok_local, feat_local = tokens.shape
    choose = routing.shape[1]
    complete_width = feat_local * experts
    capacity = min(tok_local, 6 * tok_local // experts)
    adapter_rank = adapter_lower_gate.shape[1]
    chunks = NUM_CHUNKS
    piece = capacity // chunks
    params = (
        gate_weight[0],
        up_weight[0],
        down_weight[0],
        adapter_lower_gate[0],
        adapter_upper_gate[0],
        adapter_lower_up[0],
        adapter_upper_up[0],
        adapter_lower_down[0],
        adapter_upper_down[0],
    )
    positions = slot_numbers(routing, experts)
    zero_row = jnp.zeros((1, feat_local), jnp.bfloat16)
    source, member = slot_sources(routing, positions, experts, capacity)
    clamped = jnp.minimum(source, tok_local - 1)
    slot_gate = jnp.where(
        source < tok_local, router_gate_values.reshape(-1)[clamped * choose + member], 0.0
    )
    send_x = jnp.concatenate([tokens, zero_row], 0)[source].reshape(experts, capacity, feat_local)
    send_dy = (
        (
            slot_gate[:, None]
            * jnp.concatenate([output_gradient, zero_row], 0)[source].astype(jnp.float32)
        )
        .astype(jnp.bfloat16)
        .reshape(experts, capacity, feat_local)
    )
    send_both = jnp.concatenate([send_x, send_dy], axis=2)
    recv_both = a2a_expert(send_both)
    recv_both = recv_both.reshape(experts, capacity, 2, feat_local).transpose(2, 1, 0, 3)
    recv_both = recv_both.reshape(2, capacity, complete_width)

    x_rows = lax.all_gather(recv_both[0], "dp", axis=0, tiled=True)
    dy_rows = lax.all_gather(recv_both[1], "dp", axis=0, tiled=True)
    rows_out, parts, owned_total = rows_backward_parts(x_rows, dy_rows, params)
    packed = rows_out.reshape(shards, capacity, complete_width + PART_COLS)
    summed_packed = lax.psum_scatter(packed, "dp", scatter_dimension=0, tiled=True)[0]
    summed = summed_packed[:, :complete_width]
    parts_mine = summed_packed[:, complete_width:]
    parts_sum = gather_dp(parts_mine, shards).reshape(shards * capacity, PART_COLS)
    grad_a_gate = ADAPTER_SCALE * contract_pair(parts_sum[:, :adapter_rank], x_rows, 0, 0)
    grad_a_up = ADAPTER_SCALE * contract_pair(
        parts_sum[:, adapter_rank:2 * adapter_rank], x_rows, 0, 0
    )
    grad_b_down = ADAPTER_SCALE * contract_pair(
        dy_rows, parts_sum[:, 2 * adapter_rank:3 * adapter_rank], 0, 0
    )
    returned_rows = lax.all_to_all(
        summed.reshape(capacity, experts, feat_local),
        "expert",
        split_axis=1,
        concat_axis=1,
        tiled=True,
    ).astype(jnp.float32)
    lookup = positions * experts + routing
    grad_x = jnp.sum(returned_rows.reshape(capacity * experts, feat_local)[lookup], axis=1).astype(
        jnp.bfloat16
    )
    return (
        grad_x,
        grad_a_gate[None],
        owned_total[0][None],
        grad_a_up[None],
        owned_total[1][None],
        owned_total[2][None],
        grad_b_down[None],
    )


def solution(mesh):
    return jax.shard_map(
        local,
        mesh=mesh,
        in_specs=(
            P("dp", "expert"),
            P("dp", "expert"),
            P("dp", None),
            P("dp", None),
            P("expert", "dp", None),
            P("expert", "dp", None),
            P("expert", "dp", None),
            P("expert", None, None),
            P("expert", "dp", None),
            P("expert", None, None),
            P("expert", "dp", None),
            P("expert", None, "dp"),
            P("expert", None, None),
        ),
        out_specs=(
            P("dp", "expert"),
            P("expert", None, None),
            P("expert", "dp", None),
            P("expert", None, None),
            P("expert", "dp", None),
            P("expert", None, "dp"),
            P("expert", None, None),
        ),
        check_vma=False,
    )
```

```python
import functools

import jax
import jax.numpy as jnp
from jax import lax
from jax.experimental import pallas as pl
from jax.experimental.pallas import tpu as pltpu
from jax.sharding import PartitionSpec as P

MESH = pl.DeviceIdType.MESH

ADAPTER_SCALE = 2.0
NUM_CHUNKS = 2
PART_COLS = 128


def contract_pair(left, right, left_axis, right_axis):
    return lax.dot_general(
        left, right, (((left_axis,), (right_axis,)), ((), ())), preferred_element_type=jnp.float32
    )


def slot_numbers(route_rows, experts):
    picked = (route_rows[:, :, None] == jnp.arange(experts, dtype=jnp.int32)[None, None, :]).astype(
        jnp.int32
    )
    per_token = jnp.sum(picked, axis=1)
    earlier = jnp.cumsum(per_token, axis=0) - per_token
    return jnp.sum(earlier[:, None, :] * picked, axis=2)


def slot_sources(route_rows, positions, experts, capacity):
    tokens_here, choose = route_rows.shape
    target = (route_rows * capacity + positions).reshape(-1)
    owners = jnp.repeat(jnp.arange(tokens_here, dtype=jnp.int32), choose)
    member_ids = jnp.tile(jnp.arange(choose, dtype=jnp.int32), tokens_here)
    source = jnp.full((experts * capacity,), tokens_here, jnp.int32).at[target].set(owners)
    member = jnp.zeros((experts * capacity,), jnp.int32).at[target].set(member_ids)
    return (source, member)


def rows_backward_pass(input_rows, output_gradient_rows, params):
    (
        gate_weight,
        up_weight,
        down_weight,
        a_gate,
        gate_adapter_upper,
        a_up,
        up_adapter_upper,
        down_adapter_lower,
        b_down,
    ) = params
    gate_projected_lower = contract_pair(a_gate, input_rows, 1, 1).astype(jnp.bfloat16)
    up_projected_lower = contract_pair(a_up, input_rows, 1, 1).astype(jnp.bfloat16)
    gate_preactivation = contract_pair(
        gate_weight, input_rows, 1, 1
    ) + ADAPTER_SCALE * contract_pair(gate_adapter_upper, gate_projected_lower, 1, 0)
    up_preactivation = contract_pair(up_weight, input_rows, 1, 1) + ADAPTER_SCALE * contract_pair(
        up_adapter_upper, up_projected_lower, 1, 0
    )
    sigmoid_gate = jax.nn.sigmoid(gate_preactivation)
    silu_gate = gate_preactivation * sigmoid_gate
    hidden_units = (silu_gate * up_preactivation).astype(jnp.bfloat16)
    down_projected_lower = contract_pair(b_down, output_gradient_rows, 0, 1).astype(jnp.bfloat16)
    hidden_gradient = contract_pair(
        down_weight, output_gradient_rows, 1, 1
    ) + ADAPTER_SCALE * contract_pair(down_adapter_lower, down_projected_lower, 0, 0)
    gate_gradient = (
        hidden_gradient
        * up_preactivation
        * sigmoid_gate
        * (1.0 + gate_preactivation * (1.0 - sigmoid_gate))
    ).astype(jnp.bfloat16)
    up_gradient = (hidden_gradient * silu_gate).astype(jnp.bfloat16)
    gate_partial = contract_pair(gate_adapter_upper, gate_gradient, 0, 0).astype(jnp.bfloat16)
    up_partial = contract_pair(up_adapter_upper, up_gradient, 0, 0).astype(jnp.bfloat16)
    down_partial = contract_pair(down_adapter_lower, hidden_units, 1, 0).astype(jnp.bfloat16)
    paired_partials = jnp.concatenate([gate_partial, up_partial], 0)
    paired_factors = jnp.concatenate([a_gate, a_up], 0)
    gradient_rows_out = (
        contract_pair(gate_gradient, gate_weight, 0, 0)
        + contract_pair(up_gradient, up_weight, 0, 0)
        + ADAPTER_SCALE * contract_pair(paired_partials, paired_factors, 0, 0)
    )
    shared_slice = (
        ADAPTER_SCALE * contract_pair(gate_partial, input_rows, 1, 0),
        ADAPTER_SCALE * contract_pair(up_partial, input_rows, 1, 0),
        ADAPTER_SCALE * contract_pair(output_gradient_rows, down_partial, 0, 1),
    )
    owned_slice = (
        ADAPTER_SCALE * contract_pair(gate_gradient, gate_projected_lower, 1, 1),
        ADAPTER_SCALE * contract_pair(up_gradient, up_projected_lower, 1, 1),
        ADAPTER_SCALE * contract_pair(down_projected_lower, hidden_units, 1, 1),
    )
    return (gradient_rows_out, shared_slice, owned_slice)


def rows_backward_parts(input_rows, output_gradient_rows, params):
    (
        gate_weight,
        up_weight,
        down_weight,
        a_gate,
        gate_adapter_upper,
        a_up,
        up_adapter_upper,
        down_adapter_lower,
        b_down,
    ) = params
    gate_projected_lower = contract_pair(a_gate, input_rows, 1, 1).astype(jnp.bfloat16)
    up_projected_lower = contract_pair(a_up, input_rows, 1, 1).astype(jnp.bfloat16)
    gate_preactivation = contract_pair(
        gate_weight, input_rows, 1, 1
    ) + ADAPTER_SCALE * contract_pair(gate_adapter_upper, gate_projected_lower, 1, 0)
    up_preactivation = contract_pair(up_weight, input_rows, 1, 1) + ADAPTER_SCALE * contract_pair(
        up_adapter_upper, up_projected_lower, 1, 0
    )
    sigmoid_gate = jax.nn.sigmoid(gate_preactivation)
    silu_gate = gate_preactivation * sigmoid_gate
    hidden_units = (silu_gate * up_preactivation).astype(jnp.bfloat16)
    down_partial = contract_pair(hidden_units, down_adapter_lower, 0, 1).astype(jnp.bfloat16)
    (
        output_gradient_rows,
        gate_preactivation,
        up_preactivation,
        sigmoid_gate,
        silu_gate,
        hidden_units,
        down_partial,
        gate_projected_lower,
        up_projected_lower,
    ) = lax.optimization_barrier(
        (
            output_gradient_rows,
            gate_preactivation,
            up_preactivation,
            sigmoid_gate,
            silu_gate,
            hidden_units,
            down_partial,
            gate_projected_lower,
            up_projected_lower,
        )
    )
    down_projected_lower = contract_pair(b_down, output_gradient_rows, 0, 1).astype(jnp.bfloat16)
    hidden_gradient = contract_pair(
        down_weight, output_gradient_rows, 1, 1
    ) + ADAPTER_SCALE * contract_pair(down_adapter_lower, down_projected_lower, 0, 0)
    gate_gradient = (
        hidden_gradient
        * up_preactivation
        * sigmoid_gate
        * (1.0 + gate_preactivation * (1.0 - sigmoid_gate))
    ).astype(jnp.bfloat16)
    up_gradient = (hidden_gradient * silu_gate).astype(jnp.bfloat16)
    gate_partial = contract_pair(gate_gradient, gate_adapter_upper, 0, 0).astype(jnp.bfloat16)
    up_partial = contract_pair(up_gradient, up_adapter_upper, 0, 0).astype(jnp.bfloat16)
    parts = jnp.concatenate([gate_partial, up_partial, down_partial], 1)
    rank3 = parts.shape[1]
    hidden_here, width = gate_weight.shape
    lhs = jnp.concatenate([gate_gradient, up_gradient, parts.T], 0)
    lora_rows = jnp.concatenate(
        [
            (ADAPTER_SCALE * a_gate.astype(jnp.float32)).astype(jnp.bfloat16),
            (ADAPTER_SCALE * a_up.astype(jnp.float32)).astype(jnp.bfloat16),
            jnp.zeros((rank3 - a_gate.shape[0] - a_up.shape[0], width), jnp.bfloat16),
        ],
        0,
    )
    left_block = jnp.concatenate([gate_weight, up_weight, lora_rows], 0)
    picker = (
        jnp.arange(2 * hidden_here + rank3, dtype=jnp.int32)[:, None] - 2 * hidden_here
        == jnp.arange(PART_COLS, dtype=jnp.int32)[None, :]
    ).astype(jnp.bfloat16)
    extended = jnp.concatenate([left_block, picker], 1)
    gradient_rows_out = lax.dot_general(
        lhs, extended, (((0,), (0,)), ((), ())), preferred_element_type=jnp.float32
    ).astype(jnp.bfloat16)
    owned_slice = (
        ADAPTER_SCALE * contract_pair(gate_gradient, gate_projected_lower, 1, 1),
        ADAPTER_SCALE * contract_pair(up_gradient, up_projected_lower, 1, 1),
        ADAPTER_SCALE * contract_pair(down_projected_lower, hidden_units, 1, 1),
    )
    return (gradient_rows_out, parts, owned_slice)


def gather_dp_kernel(n, src_ref, out_ref, send_sem, recv_sem):
    me = lax.axis_index("dp")
    ex = lax.axis_index("expert")
    barrier = pltpu.get_barrier_semaphore()
    for k in range(1, n):
        peer = lax.rem(me + k, n)
        pl.semaphore_signal(barrier, inc=1, device_id=(peer, ex), device_id_type=MESH)
    pl.semaphore_wait(barrier, n - 1)
    copies = []
    for k in range(1, n):
        peer = lax.rem(me + k, n)
        cp = pltpu.make_async_remote_copy(
            src_ref,
            out_ref.at[me],
            send_sem.at[k],
            recv_sem.at[k],
            device_id=(peer, ex),
            device_id_type=MESH,
        )
        cp.start()
        copies.append(cp)
    out_ref[me] = src_ref[...]
    for cp in copies:
        cp.wait()


def gather_dp(block, n):
    return pl.pallas_call(
        functools.partial(gather_dp_kernel, n),
        out_shape=jax.ShapeDtypeStruct((n,) + block.shape, block.dtype),
        in_specs=[pl.BlockSpec(memory_space=pltpu.VMEM)],
        out_specs=pl.BlockSpec(memory_space=pltpu.VMEM),
        scratch_shapes=[pltpu.SemaphoreType.DMA((n,)), pltpu.SemaphoreType.DMA((n,))],
        compiler_params=pltpu.CompilerParams(collective_id=0, has_side_effects=True),
    )(block)


def a2a_expert_kernel(n, width, x_ref, dy_ref, x_out, dy_out, send_sem, recv_sem):
    me = lax.axis_index("expert")
    row = lax.axis_index("dp")
    barrier = pltpu.get_barrier_semaphore()
    for k in range(1, n):
        peer = lax.rem(me + k, n)
        pl.semaphore_signal(barrier, inc=1, device_id=(row, peer), device_id_type=MESH)
    pl.semaphore_wait(barrier, n - 1)
    mine = pl.ds(pl.multiple_of(me * width, width), width)
    copies = []
    for k in range(1, n):
        peer = lax.rem(me + k, n)
        for which, (src_ref, out_ref) in enumerate(((x_ref, x_out), (dy_ref, dy_out))):
            cp = pltpu.make_async_remote_copy(
                src_ref.at[peer],
                out_ref.at[:, mine],
                send_sem.at[which, k],
                recv_sem.at[which, k],
                device_id=(row, peer),
                device_id_type=MESH,
            )
            cp.start()
            copies.append(cp)
    x_out[:, mine] = x_ref[me]
    dy_out[:, mine] = dy_ref[me]
    for cp in copies:
        cp.wait()


def a2a_expert(send_x, send_dy):
    n, rows, width = send_x.shape
    out = jax.ShapeDtypeStruct((rows, n * width), send_x.dtype)
    return pl.pallas_call(
        functools.partial(a2a_expert_kernel, n, width),
        out_shape=(out, out),
        in_specs=[pl.BlockSpec(memory_space=pltpu.VMEM)] * 2,
        out_specs=(pl.BlockSpec(memory_space=pltpu.VMEM),) * 2,
        scratch_shapes=[pltpu.SemaphoreType.DMA((2, n)), pltpu.SemaphoreType.DMA((2, n))],
        compiler_params=pltpu.CompilerParams(collective_id=1, has_side_effects=True),
    )(send_x, send_dy)

def local(
    tokens,
    output_gradient,
    routing,
    router_gate_values,
    gate_weight,
    up_weight,
    down_weight,
    adapter_lower_gate,
    adapter_upper_gate,
    adapter_lower_up,
    adapter_upper_up,
    adapter_lower_down,
    adapter_upper_down,
):
    experts = lax.axis_size("expert")
    shards = lax.axis_size("dp")
    tok_local, feat_local = tokens.shape
    choose = routing.shape[1]
    complete_width = feat_local * experts
    capacity = min(tok_local, 6 * tok_local // experts)
    adapter_rank = adapter_lower_gate.shape[1]
    chunks = NUM_CHUNKS
    piece = capacity // chunks
    params = (
        gate_weight[0],
        up_weight[0],
        down_weight[0],
        adapter_lower_gate[0],
        adapter_upper_gate[0],
        adapter_lower_up[0],
        adapter_upper_up[0],
        adapter_lower_down[0],
        adapter_upper_down[0],
    )
    positions = slot_numbers(routing, experts)
    zero_row = jnp.zeros((1, feat_local), jnp.bfloat16)
    source, member = slot_sources(routing, positions, experts, capacity)
    clamped = jnp.minimum(source, tok_local - 1)
    slot_gate = jnp.where(
        source < tok_local, router_gate_values.reshape(-1)[clamped * choose + member], 0.0
    )
    send_x = jnp.concatenate([tokens, zero_row], 0)[source].reshape(experts, capacity, feat_local)
    send_dy = (
        (
            slot_gate[:, None]
            * jnp.concatenate([output_gradient, zero_row], 0)[source].astype(jnp.float32)
        )
        .astype(jnp.bfloat16)
        .reshape(experts, capacity, feat_local)
    )
    x_block, dy_block = a2a_expert(send_x, send_dy)
    x_rows = lax.all_gather(x_block, "dp", axis=0, tiled=True)
    dy_rows = lax.all_gather(dy_block, "dp", axis=0, tiled=True)
    rows_out, parts, owned_total = rows_backward_parts(x_rows, dy_rows, params)
    packed = rows_out.reshape(shards, capacity, complete_width + PART_COLS)
    summed_packed = lax.psum_scatter(packed, "dp", scatter_dimension=0, tiled=True)[0]
    summed = summed_packed[:, :complete_width]
    parts_mine = summed_packed[:, complete_width:]
    parts_sum = gather_dp(parts_mine, shards).reshape(shards * capacity, PART_COLS)
    grad_a_pair = ADAPTER_SCALE * contract_pair(parts_sum[:, :2 * adapter_rank], x_rows, 0, 0)
    grad_a_gate = grad_a_pair[:adapter_rank]
    grad_a_up = grad_a_pair[adapter_rank:]
    grad_b_down = ADAPTER_SCALE * contract_pair(
        dy_rows, parts_sum[:, 2 * adapter_rank:3 * adapter_rank], 0, 0
    )
    returned_rows = lax.all_to_all(
        summed.reshape(capacity, experts, feat_local),
        "expert",
        split_axis=1,
        concat_axis=1,
        tiled=True,
    ).astype(jnp.float32)
    lookup = positions * experts + routing
    grad_x = jnp.sum(returned_rows.reshape(capacity * experts, feat_local)[lookup], axis=1).astype(
        jnp.bfloat16
    )
    return (
        grad_x,
        grad_a_gate[None],
        owned_total[0][None],
        grad_a_up[None],
        owned_total[1][None],
        owned_total[2][None],
        grad_b_down[None],
    )


def solution(mesh):
    return jax.shard_map(
        local,
        mesh=mesh,
        in_specs=(
            P("dp", "expert"),
            P("dp", "expert"),
            P("dp", None),
            P("dp", None),
            P("expert", "dp", None),
            P("expert", "dp", None),
            P("expert", "dp", None),
            P("expert", None, None),
            P("expert", "dp", None),
            P("expert", None, None),
            P("expert", "dp", None),
            P("expert", None, "dp"),
            P("expert", None, None),
        ),
        out_specs=(
            P("dp", "expert"),
            P("expert", None, None),
            P("expert", "dp", None),
            P("expert", None, None),
            P("expert", "dp", None),
            P("expert", None, "dp"),
            P("expert", None, None),
        ),
        check_vma=False,
    )
```

```python
import functools

import jax
import jax.numpy as jnp
from jax import lax
from jax.experimental import pallas as pl
from jax.experimental.pallas import tpu as pltpu
from jax.sharding import PartitionSpec as P

MESH = pl.DeviceIdType.MESH

ADAPTER_SCALE = 2.0
NUM_CHUNKS = 2
PART_COLS = 128


def contract_pair(left, right, left_axis, right_axis):
    return lax.dot_general(
        left, right, (((left_axis,), (right_axis,)), ((), ())), preferred_element_type=jnp.float32
    )


def slot_numbers(route_rows, experts):
    picked = (route_rows[:, :, None] == jnp.arange(experts, dtype=jnp.int32)[None, None, :]).astype(
        jnp.int32
    )
    per_token = jnp.sum(picked, axis=1)
    earlier = jnp.cumsum(per_token, axis=0) - per_token
    return jnp.sum(earlier[:, None, :] * picked, axis=2)


def slot_sources(route_rows, positions, experts, capacity):
    tokens_here, choose = route_rows.shape
    target = (route_rows * capacity + positions).reshape(-1)
    owners = jnp.repeat(jnp.arange(tokens_here, dtype=jnp.int32), choose)
    member_ids = jnp.tile(jnp.arange(choose, dtype=jnp.int32), tokens_here)
    source = jnp.full((experts * capacity,), tokens_here, jnp.int32).at[target].set(owners)
    member = jnp.zeros((experts * capacity,), jnp.int32).at[target].set(member_ids)
    return (source, member)


def rows_backward_pass(input_rows, output_gradient_rows, params):
    (
        gate_weight,
        up_weight,
        down_weight,
        a_gate,
        gate_adapter_upper,
        a_up,
        up_adapter_upper,
        down_adapter_lower,
        b_down,
    ) = params
    gate_projected_lower = contract_pair(a_gate, input_rows, 1, 1).astype(jnp.bfloat16)
    up_projected_lower = contract_pair(a_up, input_rows, 1, 1).astype(jnp.bfloat16)
    gate_preactivation = contract_pair(
        gate_weight, input_rows, 1, 1
    ) + ADAPTER_SCALE * contract_pair(gate_adapter_upper, gate_projected_lower, 1, 0)
    up_preactivation = contract_pair(up_weight, input_rows, 1, 1) + ADAPTER_SCALE * contract_pair(
        up_adapter_upper, up_projected_lower, 1, 0
    )
    sigmoid_gate = jax.nn.sigmoid(gate_preactivation)
    silu_gate = gate_preactivation * sigmoid_gate
    hidden_units = (silu_gate * up_preactivation).astype(jnp.bfloat16)
    down_projected_lower = contract_pair(b_down, output_gradient_rows, 0, 1).astype(jnp.bfloat16)
    hidden_gradient = contract_pair(
        down_weight, output_gradient_rows, 1, 1
    ) + ADAPTER_SCALE * contract_pair(down_adapter_lower, down_projected_lower, 0, 0)
    gate_gradient = (
        hidden_gradient
        * up_preactivation
        * sigmoid_gate
        * (1.0 + gate_preactivation * (1.0 - sigmoid_gate))
    ).astype(jnp.bfloat16)
    up_gradient = (hidden_gradient * silu_gate).astype(jnp.bfloat16)
    gate_partial = contract_pair(gate_adapter_upper, gate_gradient, 0, 0).astype(jnp.bfloat16)
    up_partial = contract_pair(up_adapter_upper, up_gradient, 0, 0).astype(jnp.bfloat16)
    down_partial = contract_pair(down_adapter_lower, hidden_units, 1, 0).astype(jnp.bfloat16)
    paired_partials = jnp.concatenate([gate_partial, up_partial], 0)
    paired_factors = jnp.concatenate([a_gate, a_up], 0)
    gradient_rows_out = (
        contract_pair(gate_gradient, gate_weight, 0, 0)
        + contract_pair(up_gradient, up_weight, 0, 0)
        + ADAPTER_SCALE * contract_pair(paired_partials, paired_factors, 0, 0)
    )
    shared_slice = (
        ADAPTER_SCALE * contract_pair(gate_partial, input_rows, 1, 0),
        ADAPTER_SCALE * contract_pair(up_partial, input_rows, 1, 0),
        ADAPTER_SCALE * contract_pair(output_gradient_rows, down_partial, 0, 1),
    )
    owned_slice = (
        ADAPTER_SCALE * contract_pair(gate_gradient, gate_projected_lower, 1, 1),
        ADAPTER_SCALE * contract_pair(up_gradient, up_projected_lower, 1, 1),
        ADAPTER_SCALE * contract_pair(down_projected_lower, hidden_units, 1, 1),
    )
    return (gradient_rows_out, shared_slice, owned_slice)


def rows_backward_parts(input_rows, output_gradient_rows, params):
    (
        gate_weight,
        up_weight,
        down_weight,
        a_gate,
        gate_adapter_upper,
        a_up,
        up_adapter_upper,
        down_adapter_lower,
        b_down,
    ) = params
    gate_projected_lower = contract_pair(a_gate, input_rows, 1, 1).astype(jnp.bfloat16)
    up_projected_lower = contract_pair(a_up, input_rows, 1, 1).astype(jnp.bfloat16)
    gate_preactivation = contract_pair(
        gate_weight, input_rows, 1, 1
    ) + ADAPTER_SCALE * contract_pair(gate_adapter_upper, gate_projected_lower, 1, 0)
    up_preactivation = contract_pair(up_weight, input_rows, 1, 1) + ADAPTER_SCALE * contract_pair(
        up_adapter_upper, up_projected_lower, 1, 0
    )
    sigmoid_gate = jax.nn.sigmoid(gate_preactivation)
    silu_gate = gate_preactivation * sigmoid_gate
    hidden_units = (silu_gate * up_preactivation).astype(jnp.bfloat16)
    down_partial = contract_pair(hidden_units, down_adapter_lower, 0, 1).astype(jnp.bfloat16)
    (
        output_gradient_rows,
        gate_preactivation,
        up_preactivation,
        sigmoid_gate,
        silu_gate,
        hidden_units,
        down_partial,
        gate_projected_lower,
        up_projected_lower,
    ) = lax.optimization_barrier(
        (
            output_gradient_rows,
            gate_preactivation,
            up_preactivation,
            sigmoid_gate,
            silu_gate,
            hidden_units,
            down_partial,
            gate_projected_lower,
            up_projected_lower,
        )
    )
    down_projected_lower = contract_pair(b_down, output_gradient_rows, 0, 1).astype(jnp.bfloat16)
    hidden_gradient = contract_pair(
        down_weight, output_gradient_rows, 1, 1
    ) + ADAPTER_SCALE * contract_pair(down_adapter_lower, down_projected_lower, 0, 0)
    gate_gradient = (
        hidden_gradient
        * up_preactivation
        * sigmoid_gate
        * (1.0 + gate_preactivation * (1.0 - sigmoid_gate))
    ).astype(jnp.bfloat16)
    up_gradient = (hidden_gradient * silu_gate).astype(jnp.bfloat16)
    gate_partial = contract_pair(gate_gradient, gate_adapter_upper, 0, 0).astype(jnp.bfloat16)
    up_partial = contract_pair(up_gradient, up_adapter_upper, 0, 0).astype(jnp.bfloat16)
    parts = jnp.concatenate([gate_partial, up_partial, down_partial], 1)
    rank3 = parts.shape[1]
    hidden_here, width = gate_weight.shape
    lhs = jnp.concatenate([gate_gradient, up_gradient, parts.T], 0)
    lora_rows = jnp.concatenate(
        [
            (ADAPTER_SCALE * a_gate.astype(jnp.float32)).astype(jnp.bfloat16),
            (ADAPTER_SCALE * a_up.astype(jnp.float32)).astype(jnp.bfloat16),
            jnp.zeros((rank3 - a_gate.shape[0] - a_up.shape[0], width), jnp.bfloat16),
        ],
        0,
    )
    left_block = jnp.concatenate([gate_weight, up_weight, lora_rows], 0)
    picker = (
        jnp.arange(2 * hidden_here + rank3, dtype=jnp.int32)[:, None] - 2 * hidden_here
        == jnp.arange(PART_COLS, dtype=jnp.int32)[None, :]
    ).astype(jnp.bfloat16)
    extended = jnp.concatenate([left_block, picker], 1)
    gradient_rows_out = lax.dot_general(
        lhs, extended, (((0,), (0,)), ((), ())), preferred_element_type=jnp.float32
    ).astype(jnp.bfloat16)
    owned_slice = (
        ADAPTER_SCALE * contract_pair(gate_gradient, gate_projected_lower, 1, 1),
        ADAPTER_SCALE * contract_pair(up_gradient, up_projected_lower, 1, 1),
        ADAPTER_SCALE * contract_pair(down_projected_lower, hidden_units, 1, 1),
    )
    return (gradient_rows_out, parts, owned_slice)


def gather_dp_kernel(n, src_ref, out_ref, send_sem, recv_sem):
    me = lax.axis_index("dp")
    ex = lax.axis_index("expert")
    barrier = pltpu.get_barrier_semaphore()
    for k in range(1, n):
        peer = lax.rem(me + k, n)
        pl.semaphore_signal(barrier, inc=1, device_id=(peer, ex), device_id_type=MESH)
    pl.semaphore_wait(barrier, n - 1)
    copies = []
    for k in range(1, n):
        peer = lax.rem(me + k, n)
        cp = pltpu.make_async_remote_copy(
            src_ref,
            out_ref.at[me],
            send_sem.at[k],
            recv_sem.at[k],
            device_id=(peer, ex),
            device_id_type=MESH,
        )
        cp.start()
        copies.append(cp)
    out_ref[me] = src_ref[...]
    for cp in copies:
        cp.wait()


def gather_dp(block, n):
    return pl.pallas_call(
        functools.partial(gather_dp_kernel, n),
        out_shape=jax.ShapeDtypeStruct((n,) + block.shape, block.dtype),
        in_specs=[pl.BlockSpec(memory_space=pltpu.VMEM)],
        out_specs=pl.BlockSpec(memory_space=pltpu.VMEM),
        scratch_shapes=[pltpu.SemaphoreType.DMA((n,)), pltpu.SemaphoreType.DMA((n,))],
        compiler_params=pltpu.CompilerParams(collective_id=0, has_side_effects=True),
    )(block)


def a2a_expert_kernel(n, width, src_ref, out_ref, send_sem, recv_sem):
    me = lax.axis_index("expert")
    row = lax.axis_index("dp")
    barrier = pltpu.get_barrier_semaphore()
    for k in range(1, n):
        peer = lax.rem(me + k, n)
        pl.semaphore_signal(barrier, inc=1, device_id=(row, peer), device_id_type=MESH)
    pl.semaphore_wait(barrier, n - 1)
    mine = pl.ds(pl.multiple_of(me * width, width), width)
    copies = []
    for k in range(1, n):
        peer = lax.rem(me + k, n)
        cp = pltpu.make_async_remote_copy(
            src_ref.at[peer],
            out_ref.at[:, mine],
            send_sem.at[k],
            recv_sem.at[k],
            device_id=(row, peer),
            device_id_type=MESH,
        )
        cp.start()
        copies.append(cp)
    out_ref[:, mine] = src_ref[me]
    for cp in copies:
        cp.wait()


def a2a_expert(send, exchange_id):
    n, rows, width = send.shape
    return pl.pallas_call(
        functools.partial(a2a_expert_kernel, n, width),
        out_shape=jax.ShapeDtypeStruct((rows, n * width), send.dtype),
        in_specs=[pl.BlockSpec(memory_space=pltpu.VMEM)],
        out_specs=pl.BlockSpec(memory_space=pltpu.VMEM),
        scratch_shapes=[pltpu.SemaphoreType.DMA((n,)), pltpu.SemaphoreType.DMA((n,))],
        compiler_params=pltpu.CompilerParams(collective_id=exchange_id, has_side_effects=True),
    )(send)

def local(
    tokens,
    output_gradient,
    routing,
    router_gate_values,
    gate_weight,
    up_weight,
    down_weight,
    adapter_lower_gate,
    adapter_upper_gate,
    adapter_lower_up,
    adapter_upper_up,
    adapter_lower_down,
    adapter_upper_down,
):
    experts = lax.axis_size("expert")
    shards = lax.axis_size("dp")
    tok_local, feat_local = tokens.shape
    choose = routing.shape[1]
    complete_width = feat_local * experts
    capacity = min(tok_local, 6 * tok_local // experts)
    adapter_rank = adapter_lower_gate.shape[1]
    chunks = NUM_CHUNKS
    piece = capacity // chunks
    params = (
        gate_weight[0],
        up_weight[0],
        down_weight[0],
        adapter_lower_gate[0],
        adapter_upper_gate[0],
        adapter_lower_up[0],
        adapter_upper_up[0],
        adapter_lower_down[0],
        adapter_upper_down[0],
    )
    positions = slot_numbers(routing, experts)
    zero_row = jnp.zeros((1, feat_local), jnp.bfloat16)
    source, member = slot_sources(routing, positions, experts, capacity)
    clamped = jnp.minimum(source, tok_local - 1)
    slot_gate = jnp.where(
        source < tok_local, router_gate_values.reshape(-1)[clamped * choose + member], 0.0
    )
    send_x = jnp.concatenate([tokens, zero_row], 0)[source].reshape(experts, capacity, feat_local)
    send_dy = (
        (
            slot_gate[:, None]
            * jnp.concatenate([output_gradient, zero_row], 0)[source].astype(jnp.float32)
        )
        .astype(jnp.bfloat16)
        .reshape(experts, capacity, feat_local)
    )
    x_block = a2a_expert(send_x, 1)
    x_rows = lax.all_gather(x_block, "dp", axis=0, tiled=True)
    dy_block = a2a_expert(send_dy, 2)
    dy_rows = lax.all_gather(dy_block, "dp", axis=0, tiled=True)
    rows_out, parts, owned_total = rows_backward_parts(x_rows, dy_rows, params)
    packed = rows_out.reshape(shards, capacity, complete_width + PART_COLS)
    summed_packed = lax.psum_scatter(packed, "dp", scatter_dimension=0, tiled=True)[0]
    summed = summed_packed[:, :complete_width]
    parts_mine = summed_packed[:, complete_width:]
    parts_sum = gather_dp(parts_mine, shards).reshape(shards * capacity, PART_COLS)
    grad_a_pair = ADAPTER_SCALE * contract_pair(parts_sum[:, :2 * adapter_rank], x_rows, 0, 0)
    grad_a_gate = grad_a_pair[:adapter_rank]
    grad_a_up = grad_a_pair[adapter_rank:]
    grad_b_down = ADAPTER_SCALE * contract_pair(
        dy_rows, parts_sum[:, 2 * adapter_rank:3 * adapter_rank], 0, 0
    )
    returned_rows = lax.all_to_all(
        summed.reshape(capacity, experts, feat_local),
        "expert",
        split_axis=1,
        concat_axis=1,
        tiled=True,
    ).astype(jnp.float32)
    lookup = positions * experts + routing
    grad_x = jnp.sum(returned_rows.reshape(capacity * experts, feat_local)[lookup], axis=1).astype(
        jnp.bfloat16
    )
    return (
        grad_x,
        grad_a_gate[None],
        owned_total[0][None],
        grad_a_up[None],
        owned_total[1][None],
        owned_total[2][None],
        grad_b_down[None],
    )


def solution(mesh):
    return jax.shard_map(
        local,
        mesh=mesh,
        in_specs=(
            P("dp", "expert"),
            P("dp", "expert"),
            P("dp", None),
            P("dp", None),
            P("expert", "dp", None),
            P("expert", "dp", None),
            P("expert", "dp", None),
            P("expert", None, None),
            P("expert", "dp", None),
            P("expert", None, None),
            P("expert", "dp", None),
            P("expert", None, "dp"),
            P("expert", None, None),
        ),
        out_specs=(
            P("dp", "expert"),
            P("expert", None, None),
            P("expert", "dp", None),
            P("expert", None, None),
            P("expert", "dp", None),
            P("expert", None, "dp"),
            P("expert", None, None),
        ),
        check_vma=False,
    )
```

```python
import functools

import jax
import jax.numpy as jnp
from jax import lax
from jax.experimental import pallas as pl
from jax.experimental.pallas import tpu as pltpu
from jax.sharding import PartitionSpec as P

MESH = pl.DeviceIdType.MESH

ADAPTER_SCALE = 2.0
NUM_CHUNKS = 2
PART_COLS = 128


def contract_pair(left, right, left_axis, right_axis):
    return lax.dot_general(
        left, right, (((left_axis,), (right_axis,)), ((), ())), preferred_element_type=jnp.float32
    )


def slot_numbers(route_rows, experts):
    picked = (route_rows[:, :, None] == jnp.arange(experts, dtype=jnp.int32)[None, None, :]).astype(
        jnp.int32
    )
    per_token = jnp.sum(picked, axis=1)
    earlier = jnp.cumsum(per_token, axis=0) - per_token
    return jnp.sum(earlier[:, None, :] * picked, axis=2)


def slot_sources(route_rows, positions, experts, capacity):
    tokens_here, choose = route_rows.shape
    target = (route_rows * capacity + positions).reshape(-1)
    owners = jnp.repeat(jnp.arange(tokens_here, dtype=jnp.int32), choose)
    member_ids = jnp.tile(jnp.arange(choose, dtype=jnp.int32), tokens_here)
    source = jnp.full((experts * capacity,), tokens_here, jnp.int32).at[target].set(owners)
    member = jnp.zeros((experts * capacity,), jnp.int32).at[target].set(member_ids)
    return (source, member)


def rows_backward_pass(input_rows, output_gradient_rows, params):
    (
        gate_weight,
        up_weight,
        down_weight,
        a_gate,
        gate_adapter_upper,
        a_up,
        up_adapter_upper,
        down_adapter_lower,
        b_down,
    ) = params
    gate_projected_lower = contract_pair(a_gate, input_rows, 1, 1).astype(jnp.bfloat16)
    up_projected_lower = contract_pair(a_up, input_rows, 1, 1).astype(jnp.bfloat16)
    gate_preactivation = contract_pair(
        gate_weight, input_rows, 1, 1
    ) + ADAPTER_SCALE * contract_pair(gate_adapter_upper, gate_projected_lower, 1, 0)
    up_preactivation = contract_pair(up_weight, input_rows, 1, 1) + ADAPTER_SCALE * contract_pair(
        up_adapter_upper, up_projected_lower, 1, 0
    )
    sigmoid_gate = jax.nn.sigmoid(gate_preactivation)
    silu_gate = gate_preactivation * sigmoid_gate
    hidden_units = (silu_gate * up_preactivation).astype(jnp.bfloat16)
    down_projected_lower = contract_pair(b_down, output_gradient_rows, 0, 1).astype(jnp.bfloat16)
    hidden_gradient = contract_pair(
        down_weight, output_gradient_rows, 1, 1
    ) + ADAPTER_SCALE * contract_pair(down_adapter_lower, down_projected_lower, 0, 0)
    gate_gradient = (
        hidden_gradient
        * up_preactivation
        * sigmoid_gate
        * (1.0 + gate_preactivation * (1.0 - sigmoid_gate))
    ).astype(jnp.bfloat16)
    up_gradient = (hidden_gradient * silu_gate).astype(jnp.bfloat16)
    gate_partial = contract_pair(gate_adapter_upper, gate_gradient, 0, 0).astype(jnp.bfloat16)
    up_partial = contract_pair(up_adapter_upper, up_gradient, 0, 0).astype(jnp.bfloat16)
    down_partial = contract_pair(down_adapter_lower, hidden_units, 1, 0).astype(jnp.bfloat16)
    paired_partials = jnp.concatenate([gate_partial, up_partial], 0)
    paired_factors = jnp.concatenate([a_gate, a_up], 0)
    gradient_rows_out = (
        contract_pair(gate_gradient, gate_weight, 0, 0)
        + contract_pair(up_gradient, up_weight, 0, 0)
        + ADAPTER_SCALE * contract_pair(paired_partials, paired_factors, 0, 0)
    )
    shared_slice = (
        ADAPTER_SCALE * contract_pair(gate_partial, input_rows, 1, 0),
        ADAPTER_SCALE * contract_pair(up_partial, input_rows, 1, 0),
        ADAPTER_SCALE * contract_pair(output_gradient_rows, down_partial, 0, 1),
    )
    owned_slice = (
        ADAPTER_SCALE * contract_pair(gate_gradient, gate_projected_lower, 1, 1),
        ADAPTER_SCALE * contract_pair(up_gradient, up_projected_lower, 1, 1),
        ADAPTER_SCALE * contract_pair(down_projected_lower, hidden_units, 1, 1),
    )
    return (gradient_rows_out, shared_slice, owned_slice)


def rows_backward_parts(input_rows, output_gradient_rows, params):
    (
        gate_weight,
        up_weight,
        down_weight,
        a_gate,
        gate_adapter_upper,
        a_up,
        up_adapter_upper,
        down_adapter_lower,
        b_down,
    ) = params
    gate_projected_lower = contract_pair(a_gate, input_rows, 1, 1).astype(jnp.bfloat16)
    up_projected_lower = contract_pair(a_up, input_rows, 1, 1).astype(jnp.bfloat16)
    gate_preactivation = contract_pair(
        gate_weight, input_rows, 1, 1
    ) + ADAPTER_SCALE * contract_pair(gate_adapter_upper, gate_projected_lower, 1, 0)
    up_preactivation = contract_pair(up_weight, input_rows, 1, 1) + ADAPTER_SCALE * contract_pair(
        up_adapter_upper, up_projected_lower, 1, 0
    )
    sigmoid_gate = jax.nn.sigmoid(gate_preactivation)
    silu_gate = gate_preactivation * sigmoid_gate
    hidden_units = (silu_gate * up_preactivation).astype(jnp.bfloat16)
    down_partial = contract_pair(hidden_units, down_adapter_lower, 0, 1).astype(jnp.bfloat16)
    (
        output_gradient_rows,
        gate_preactivation,
        up_preactivation,
        sigmoid_gate,
        silu_gate,
        hidden_units,
        down_partial,
        gate_projected_lower,
        up_projected_lower,
    ) = lax.optimization_barrier(
        (
            output_gradient_rows,
            gate_preactivation,
            up_preactivation,
            sigmoid_gate,
            silu_gate,
            hidden_units,
            down_partial,
            gate_projected_lower,
            up_projected_lower,
        )
    )
    down_projected_lower = contract_pair(b_down, output_gradient_rows, 0, 1).astype(jnp.bfloat16)
    hidden_gradient = contract_pair(
        down_weight, output_gradient_rows, 1, 1
    ) + ADAPTER_SCALE * contract_pair(down_adapter_lower, down_projected_lower, 0, 0)
    gate_gradient = (
        hidden_gradient
        * up_preactivation
        * sigmoid_gate
        * (1.0 + gate_preactivation * (1.0 - sigmoid_gate))
    ).astype(jnp.bfloat16)
    up_gradient = (hidden_gradient * silu_gate).astype(jnp.bfloat16)
    gate_partial = contract_pair(gate_gradient, gate_adapter_upper, 0, 0).astype(jnp.bfloat16)
    up_partial = contract_pair(up_gradient, up_adapter_upper, 0, 0).astype(jnp.bfloat16)
    parts = jnp.concatenate([gate_partial, up_partial, down_partial], 1)
    pair = jnp.concatenate([gate_partial, up_partial], 1)
    lhs = jnp.concatenate([gate_gradient, up_gradient, pair.T], 0)
    lora_rows = jnp.concatenate(
        [
            (ADAPTER_SCALE * a_gate.astype(jnp.float32)).astype(jnp.bfloat16),
            (ADAPTER_SCALE * a_up.astype(jnp.float32)).astype(jnp.bfloat16),
        ],
        0,
    )
    extended = jnp.concatenate([gate_weight, up_weight, lora_rows], 0)
    gradient_rows_out = lax.dot_general(
        lhs, extended, (((0,), (0,)), ((), ())), preferred_element_type=jnp.float32
    ).astype(jnp.bfloat16)
    owned_slice = (
        ADAPTER_SCALE * contract_pair(gate_gradient, gate_projected_lower, 1, 1),
        ADAPTER_SCALE * contract_pair(up_gradient, up_projected_lower, 1, 1),
        ADAPTER_SCALE * contract_pair(down_projected_lower, hidden_units, 1, 1),
    )
    return (gradient_rows_out, parts, owned_slice)


def gather_dp_kernel(n, src_ref, out_ref, send_sem, recv_sem):
    me = lax.axis_index("dp")
    ex = lax.axis_index("expert")
    barrier = pltpu.get_barrier_semaphore()
    for k in range(1, n):
        peer = lax.rem(me + k, n)
        pl.semaphore_signal(barrier, inc=1, device_id=(peer, ex), device_id_type=MESH)
    pl.semaphore_wait(barrier, n - 1)
    copies = []
    for k in range(1, n):
        peer = lax.rem(me + k, n)
        cp = pltpu.make_async_remote_copy(
            src_ref,
            out_ref.at[me],
            send_sem.at[k],
            recv_sem.at[k],
            device_id=(peer, ex),
            device_id_type=MESH,
        )
        cp.start()
        copies.append(cp)
    out_ref[me] = src_ref[...]
    for cp in copies:
        cp.wait()


def gather_dp(block, n):
    return pl.pallas_call(
        functools.partial(gather_dp_kernel, n),
        out_shape=jax.ShapeDtypeStruct((n,) + block.shape, block.dtype),
        in_specs=[pl.BlockSpec(memory_space=pltpu.VMEM)],
        out_specs=pl.BlockSpec(memory_space=pltpu.VMEM),
        scratch_shapes=[pltpu.SemaphoreType.DMA((n,)), pltpu.SemaphoreType.DMA((n,))],
        compiler_params=pltpu.CompilerParams(collective_id=0, has_side_effects=True),
    )(block)


def a2a_expert_kernel(n, width, src_ref, out_ref, send_sem, recv_sem):
    me = lax.axis_index("expert")
    row = lax.axis_index("dp")
    barrier = pltpu.get_barrier_semaphore()
    for k in range(1, n):
        peer = lax.rem(me + k, n)
        pl.semaphore_signal(barrier, inc=1, device_id=(row, peer), device_id_type=MESH)
    pl.semaphore_wait(barrier, n - 1)
    mine = pl.ds(pl.multiple_of(me * width, width), width)
    copies = []
    for k in range(1, n):
        peer = lax.rem(me + k, n)
        cp = pltpu.make_async_remote_copy(
            src_ref.at[peer],
            out_ref.at[:, mine],
            send_sem.at[k],
            recv_sem.at[k],
            device_id=(row, peer),
            device_id_type=MESH,
        )
        cp.start()
        copies.append(cp)
    out_ref[:, mine] = src_ref[me]
    for cp in copies:
        cp.wait()


def a2a_expert(send, exchange_id):
    n, rows, width = send.shape
    return pl.pallas_call(
        functools.partial(a2a_expert_kernel, n, width),
        out_shape=jax.ShapeDtypeStruct((rows, n * width), send.dtype),
        in_specs=[pl.BlockSpec(memory_space=pltpu.VMEM)],
        out_specs=pl.BlockSpec(memory_space=pltpu.VMEM),
        scratch_shapes=[pltpu.SemaphoreType.DMA((n,)), pltpu.SemaphoreType.DMA((n,))],
        compiler_params=pltpu.CompilerParams(collective_id=exchange_id, has_side_effects=True),
    )(send)

def reduce_dp_kernel(n, src_ref, out_ref, landing, send_sem, recv_sem):
    me = lax.axis_index("dp")
    ex = lax.axis_index("expert")
    barrier = pltpu.get_barrier_semaphore()
    for k in range(1, n):
        peer = lax.rem(me + k, n)
        pl.semaphore_signal(barrier, inc=1, device_id=(peer, ex), device_id_type=MESH)
    pl.semaphore_wait(barrier, n - 1)
    copies = []
    for k in range(1, n):
        peer = lax.rem(me + k, n)
        cp = pltpu.make_async_remote_copy(
            src_ref.at[peer],
            landing.at[me],
            send_sem.at[k],
            recv_sem.at[k],
            device_id=(peer, ex),
            device_id_type=MESH,
        )
        cp.start()
        copies.append(cp)
    landing[me] = src_ref[me]
    for cp in copies:
        cp.wait()
    out_ref[...] = jnp.sum(landing[...].astype(jnp.float32), axis=0)


def reduce_dp(blocks):
    n, rows, cols = blocks.shape
    return pl.pallas_call(
        functools.partial(reduce_dp_kernel, n),
        out_shape=jax.ShapeDtypeStruct((rows, cols), jnp.float32),
        in_specs=[pl.BlockSpec(memory_space=pltpu.VMEM)],
        out_specs=pl.BlockSpec(memory_space=pltpu.VMEM),
        scratch_shapes=[
            pltpu.VMEM((n, rows, cols), blocks.dtype),
            pltpu.SemaphoreType.DMA((n,)),
            pltpu.SemaphoreType.DMA((n,)),
        ],
        compiler_params=pltpu.CompilerParams(collective_id=3, has_side_effects=True),
    )(blocks)


def local(
    tokens,
    output_gradient,
    routing,
    router_gate_values,
    gate_weight,
    up_weight,
    down_weight,
    adapter_lower_gate,
    adapter_upper_gate,
    adapter_lower_up,
    adapter_upper_up,
    adapter_lower_down,
    adapter_upper_down,
):
    experts = lax.axis_size("expert")
    shards = lax.axis_size("dp")
    tok_local, feat_local = tokens.shape
    choose = routing.shape[1]
    complete_width = feat_local * experts
    capacity = min(tok_local, 6 * tok_local // experts)
    adapter_rank = adapter_lower_gate.shape[1]
    chunks = NUM_CHUNKS
    piece = capacity // chunks
    params = (
        gate_weight[0],
        up_weight[0],
        down_weight[0],
        adapter_lower_gate[0],
        adapter_upper_gate[0],
        adapter_lower_up[0],
        adapter_upper_up[0],
        adapter_lower_down[0],
        adapter_upper_down[0],
    )
    positions = slot_numbers(routing, experts)
    zero_row = jnp.zeros((1, feat_local), jnp.bfloat16)
    source, member = slot_sources(routing, positions, experts, capacity)
    clamped = jnp.minimum(source, tok_local - 1)
    slot_gate = jnp.where(
        source < tok_local, router_gate_values.reshape(-1)[clamped * choose + member], 0.0
    )
    send_x = jnp.concatenate([tokens, zero_row], 0)[source].reshape(experts, capacity, feat_local)
    send_dy = (
        (
            slot_gate[:, None]
            * jnp.concatenate([output_gradient, zero_row], 0)[source].astype(jnp.float32)
        )
        .astype(jnp.bfloat16)
        .reshape(experts, capacity, feat_local)
    )
    x_block = a2a_expert(send_x, 1)
    x_rows = lax.all_gather(x_block, "dp", axis=0, tiled=True)
    dy_block = a2a_expert(send_dy, 2)
    dy_rows = lax.all_gather(dy_block, "dp", axis=0, tiled=True)
    rows_out, parts, owned_total = rows_backward_parts(x_rows, dy_rows, params)
    packed = rows_out.reshape(shards, capacity, complete_width)
    summed = lax.psum_scatter(packed, "dp", scatter_dimension=0, tiled=True)[0]
    parts_blocks = jnp.pad(parts, ((0, 0), (0, PART_COLS - 3 * adapter_rank)))
    parts_mine = reduce_dp(parts_blocks.reshape(shards, capacity, PART_COLS))
    parts_sum = gather_dp(parts_mine, shards).reshape(shards * capacity, PART_COLS)
    grad_a_pair = ADAPTER_SCALE * contract_pair(parts_sum[:, :2 * adapter_rank], x_rows, 0, 0)
    grad_a_gate = grad_a_pair[:adapter_rank]
    grad_a_up = grad_a_pair[adapter_rank:]
    grad_b_down = ADAPTER_SCALE * contract_pair(
        dy_rows, parts_sum[:, 2 * adapter_rank:3 * adapter_rank], 0, 0
    )
    returned_rows = lax.all_to_all(
        summed.reshape(capacity, experts, feat_local),
        "expert",
        split_axis=1,
        concat_axis=1,
        tiled=True,
    ).astype(jnp.float32)
    lookup = positions * experts + routing
    grad_x = jnp.sum(returned_rows.reshape(capacity * experts, feat_local)[lookup], axis=1).astype(
        jnp.bfloat16
    )
    return (
        grad_x,
        grad_a_gate[None],
        owned_total[0][None],
        grad_a_up[None],
        owned_total[1][None],
        owned_total[2][None],
        grad_b_down[None],
    )


def solution(mesh):
    return jax.shard_map(
        local,
        mesh=mesh,
        in_specs=(
            P("dp", "expert"),
            P("dp", "expert"),
            P("dp", None),
            P("dp", None),
            P("expert", "dp", None),
            P("expert", "dp", None),
            P("expert", "dp", None),
            P("expert", None, None),
            P("expert", "dp", None),
            P("expert", None, None),
            P("expert", "dp", None),
            P("expert", None, "dp"),
            P("expert", None, None),
        ),
        out_specs=(
            P("dp", "expert"),
            P("expert", None, None),
            P("expert", "dp", None),
            P("expert", None, None),
            P("expert", "dp", None),
            P("expert", None, "dp"),
            P("expert", None, None),
        ),
        check_vma=False,
    )
```

```python
import functools

import jax
import jax.numpy as jnp
from jax import lax
from jax.experimental import pallas as pl
from jax.experimental.pallas import tpu as pltpu
from jax.sharding import PartitionSpec as P

MESH = pl.DeviceIdType.MESH

ADAPTER_SCALE = 2.0
NUM_CHUNKS = 2
PART_COLS = 128


def contract_pair(left, right, left_axis, right_axis):
    return lax.dot_general(
        left, right, (((left_axis,), (right_axis,)), ((), ())), preferred_element_type=jnp.float32
    )


def slot_numbers(route_rows, experts):
    picked = (route_rows[:, :, None] == jnp.arange(experts, dtype=jnp.int32)[None, None, :]).astype(
        jnp.int32
    )
    per_token = jnp.sum(picked, axis=1)
    earlier = jnp.cumsum(per_token, axis=0) - per_token
    return jnp.sum(earlier[:, None, :] * picked, axis=2)


def slot_sources(route_rows, positions, experts, capacity):
    tokens_here, choose = route_rows.shape
    target = (route_rows * capacity + positions).reshape(-1)
    owners = jnp.repeat(jnp.arange(tokens_here, dtype=jnp.int32), choose)
    member_ids = jnp.tile(jnp.arange(choose, dtype=jnp.int32), tokens_here)
    source = jnp.full((experts * capacity,), tokens_here, jnp.int32).at[target].set(owners)
    member = jnp.zeros((experts * capacity,), jnp.int32).at[target].set(member_ids)
    return (source, member)


def rows_backward_pass(input_rows, output_gradient_rows, params):
    (
        gate_weight,
        up_weight,
        down_weight,
        a_gate,
        gate_adapter_upper,
        a_up,
        up_adapter_upper,
        down_adapter_lower,
        b_down,
    ) = params
    gate_projected_lower = contract_pair(a_gate, input_rows, 1, 1).astype(jnp.bfloat16)
    up_projected_lower = contract_pair(a_up, input_rows, 1, 1).astype(jnp.bfloat16)
    gate_preactivation = contract_pair(
        gate_weight, input_rows, 1, 1
    ) + ADAPTER_SCALE * contract_pair(gate_adapter_upper, gate_projected_lower, 1, 0)
    up_preactivation = contract_pair(up_weight, input_rows, 1, 1) + ADAPTER_SCALE * contract_pair(
        up_adapter_upper, up_projected_lower, 1, 0
    )
    sigmoid_gate = jax.nn.sigmoid(gate_preactivation)
    silu_gate = gate_preactivation * sigmoid_gate
    hidden_units = (silu_gate * up_preactivation).astype(jnp.bfloat16)
    down_projected_lower = contract_pair(b_down, output_gradient_rows, 0, 1).astype(jnp.bfloat16)
    hidden_gradient = contract_pair(
        down_weight, output_gradient_rows, 1, 1
    ) + ADAPTER_SCALE * contract_pair(down_adapter_lower, down_projected_lower, 0, 0)
    gate_gradient = (
        hidden_gradient
        * up_preactivation
        * sigmoid_gate
        * (1.0 + gate_preactivation * (1.0 - sigmoid_gate))
    ).astype(jnp.bfloat16)
    up_gradient = (hidden_gradient * silu_gate).astype(jnp.bfloat16)
    gate_partial = contract_pair(gate_adapter_upper, gate_gradient, 0, 0).astype(jnp.bfloat16)
    up_partial = contract_pair(up_adapter_upper, up_gradient, 0, 0).astype(jnp.bfloat16)
    down_partial = contract_pair(down_adapter_lower, hidden_units, 1, 0).astype(jnp.bfloat16)
    paired_partials = jnp.concatenate([gate_partial, up_partial], 0)
    paired_factors = jnp.concatenate([a_gate, a_up], 0)
    gradient_rows_out = (
        contract_pair(gate_gradient, gate_weight, 0, 0)
        + contract_pair(up_gradient, up_weight, 0, 0)
        + ADAPTER_SCALE * contract_pair(paired_partials, paired_factors, 0, 0)
    )
    shared_slice = (
        ADAPTER_SCALE * contract_pair(gate_partial, input_rows, 1, 0),
        ADAPTER_SCALE * contract_pair(up_partial, input_rows, 1, 0),
        ADAPTER_SCALE * contract_pair(output_gradient_rows, down_partial, 0, 1),
    )
    owned_slice = (
        ADAPTER_SCALE * contract_pair(gate_gradient, gate_projected_lower, 1, 1),
        ADAPTER_SCALE * contract_pair(up_gradient, up_projected_lower, 1, 1),
        ADAPTER_SCALE * contract_pair(down_projected_lower, hidden_units, 1, 1),
    )
    return (gradient_rows_out, shared_slice, owned_slice)


def rows_backward_parts(input_rows, output_gradient_rows, params):
    (
        gate_weight,
        up_weight,
        down_weight,
        a_gate,
        gate_adapter_upper,
        a_up,
        up_adapter_upper,
        down_adapter_lower,
        b_down,
    ) = params
    gate_projected_lower = contract_pair(a_gate, input_rows, 1, 1).astype(jnp.bfloat16)
    up_projected_lower = contract_pair(a_up, input_rows, 1, 1).astype(jnp.bfloat16)
    gate_preactivation = contract_pair(
        gate_weight, input_rows, 1, 1
    ) + ADAPTER_SCALE * contract_pair(gate_adapter_upper, gate_projected_lower, 1, 0)
    up_preactivation = contract_pair(up_weight, input_rows, 1, 1) + ADAPTER_SCALE * contract_pair(
        up_adapter_upper, up_projected_lower, 1, 0
    )
    sigmoid_gate = jax.nn.sigmoid(gate_preactivation)
    silu_gate = gate_preactivation * sigmoid_gate
    hidden_units = (silu_gate * up_preactivation).astype(jnp.bfloat16)
    down_partial = contract_pair(hidden_units, down_adapter_lower, 0, 1).astype(jnp.bfloat16)
    (
        output_gradient_rows,
        gate_preactivation,
        up_preactivation,
        sigmoid_gate,
        silu_gate,
        hidden_units,
        down_partial,
        gate_projected_lower,
        up_projected_lower,
    ) = lax.optimization_barrier(
        (
            output_gradient_rows,
            gate_preactivation,
            up_preactivation,
            sigmoid_gate,
            silu_gate,
            hidden_units,
            down_partial,
            gate_projected_lower,
            up_projected_lower,
        )
    )
    down_projected_lower = contract_pair(b_down, output_gradient_rows, 0, 1).astype(jnp.bfloat16)
    hidden_gradient = contract_pair(
        down_weight, output_gradient_rows, 1, 1
    ) + ADAPTER_SCALE * contract_pair(down_adapter_lower, down_projected_lower, 0, 0)
    gate_gradient = (
        hidden_gradient
        * up_preactivation
        * sigmoid_gate
        * (1.0 + gate_preactivation * (1.0 - sigmoid_gate))
    ).astype(jnp.bfloat16)
    up_gradient = (hidden_gradient * silu_gate).astype(jnp.bfloat16)
    gate_partial = contract_pair(gate_gradient, gate_adapter_upper, 0, 0).astype(jnp.bfloat16)
    up_partial = contract_pair(up_gradient, up_adapter_upper, 0, 0).astype(jnp.bfloat16)
    parts = jnp.concatenate([gate_partial, up_partial, down_partial], 1)
    pair = jnp.concatenate([gate_partial, up_partial], 1)
    lhs = jnp.concatenate([gate_gradient, up_gradient, pair.T], 0)
    lora_rows = jnp.concatenate(
        [
            (ADAPTER_SCALE * a_gate.astype(jnp.float32)).astype(jnp.bfloat16),
            (ADAPTER_SCALE * a_up.astype(jnp.float32)).astype(jnp.bfloat16),
        ],
        0,
    )
    extended = jnp.concatenate([gate_weight, up_weight, lora_rows], 0)
    gradient_rows_out = lax.dot_general(
        lhs, extended, (((0,), (0,)), ((), ())), preferred_element_type=jnp.float32
    ).astype(jnp.bfloat16)
    owned_slice = (
        ADAPTER_SCALE * contract_pair(gate_gradient, gate_projected_lower, 1, 1),
        ADAPTER_SCALE * contract_pair(up_gradient, up_projected_lower, 1, 1),
        ADAPTER_SCALE * contract_pair(down_projected_lower, hidden_units, 1, 1),
    )
    return (gradient_rows_out, parts, owned_slice)


def gather_dp_kernel(n, src_ref, out_ref, send_sem, recv_sem):
    me = lax.axis_index("dp")
    ex = lax.axis_index("expert")
    barrier = pltpu.get_barrier_semaphore()
    for k in range(1, n):
        peer = lax.rem(me + k, n)
        pl.semaphore_signal(barrier, inc=1, device_id=(peer, ex), device_id_type=MESH)
    pl.semaphore_wait(barrier, n - 1)
    copies = []
    for k in range(1, n):
        peer = lax.rem(me + k, n)
        cp = pltpu.make_async_remote_copy(
            src_ref,
            out_ref.at[me],
            send_sem.at[k],
            recv_sem.at[k],
            device_id=(peer, ex),
            device_id_type=MESH,
        )
        cp.start()
        copies.append(cp)
    out_ref[me] = src_ref[...]
    for cp in copies:
        cp.wait()


def gather_dp(block, n):
    return pl.pallas_call(
        functools.partial(gather_dp_kernel, n),
        out_shape=jax.ShapeDtypeStruct((n,) + block.shape, block.dtype),
        in_specs=[pl.BlockSpec(memory_space=pltpu.VMEM)],
        out_specs=pl.BlockSpec(memory_space=pltpu.VMEM),
        scratch_shapes=[pltpu.SemaphoreType.DMA((n,)), pltpu.SemaphoreType.DMA((n,))],
        compiler_params=pltpu.CompilerParams(collective_id=0, has_side_effects=True),
    )(block)


def a2a_expert_kernel(n, width, src_ref, out_ref, send_sem, recv_sem):
    me = lax.axis_index("expert")
    row = lax.axis_index("dp")
    barrier = pltpu.get_barrier_semaphore()
    for k in range(1, n):
        peer = lax.rem(me + k, n)
        pl.semaphore_signal(barrier, inc=1, device_id=(row, peer), device_id_type=MESH)
    pl.semaphore_wait(barrier, n - 1)
    mine = pl.ds(pl.multiple_of(me * width, width), width)
    copies = []
    for k in range(1, n):
        peer = lax.rem(me + k, n)
        cp = pltpu.make_async_remote_copy(
            src_ref.at[peer],
            out_ref.at[:, mine],
            send_sem.at[k],
            recv_sem.at[k],
            device_id=(row, peer),
            device_id_type=MESH,
        )
        cp.start()
        copies.append(cp)
    out_ref[:, mine] = src_ref[me]
    for cp in copies:
        cp.wait()


def a2a_expert(send, exchange_id):
    n, rows, width = send.shape
    return pl.pallas_call(
        functools.partial(a2a_expert_kernel, n, width),
        out_shape=jax.ShapeDtypeStruct((rows, n * width), send.dtype),
        in_specs=[pl.BlockSpec(memory_space=pltpu.VMEM)],
        out_specs=pl.BlockSpec(memory_space=pltpu.VMEM),
        scratch_shapes=[pltpu.SemaphoreType.DMA((n,)), pltpu.SemaphoreType.DMA((n,))],
        compiler_params=pltpu.CompilerParams(collective_id=exchange_id, has_side_effects=True),
    )(send)

def reduce_dp_kernel(n, src_ref, out_ref, landing, send_sem, recv_sem):
    me = lax.axis_index("dp")
    ex = lax.axis_index("expert")
    barrier = pltpu.get_barrier_semaphore()
    for k in range(1, n):
        peer = lax.rem(me + k, n)
        pl.semaphore_signal(barrier, inc=1, device_id=(peer, ex), device_id_type=MESH)
    pl.semaphore_wait(barrier, n - 1)
    copies = []
    for k in range(1, n):
        peer = lax.rem(me + k, n)
        cp = pltpu.make_async_remote_copy(
            src_ref.at[peer],
            landing.at[me],
            send_sem.at[k],
            recv_sem.at[k],
            device_id=(peer, ex),
            device_id_type=MESH,
        )
        cp.start()
        copies.append(cp)
    landing[me] = src_ref[me]
    for cp in copies:
        cp.wait()
    out_ref[...] = jnp.sum(landing[...].astype(jnp.float32), axis=0)


def reduce_dp(blocks):
    n, rows, cols = blocks.shape
    return pl.pallas_call(
        functools.partial(reduce_dp_kernel, n),
        out_shape=jax.ShapeDtypeStruct((rows, cols), jnp.float32),
        in_specs=[pl.BlockSpec(memory_space=pltpu.VMEM)],
        out_specs=pl.BlockSpec(memory_space=pltpu.VMEM),
        scratch_shapes=[
            pltpu.VMEM((n, rows, cols), blocks.dtype),
            pltpu.SemaphoreType.DMA((n,)),
            pltpu.SemaphoreType.DMA((n,)),
        ],
        compiler_params=pltpu.CompilerParams(collective_id=3, has_side_effects=True),
    )(blocks)


def local(
    tokens,
    output_gradient,
    routing,
    router_gate_values,
    gate_weight,
    up_weight,
    down_weight,
    adapter_lower_gate,
    adapter_upper_gate,
    adapter_lower_up,
    adapter_upper_up,
    adapter_lower_down,
    adapter_upper_down,
):
    experts = lax.axis_size("expert")
    shards = lax.axis_size("dp")
    tok_local, feat_local = tokens.shape
    choose = routing.shape[1]
    complete_width = feat_local * experts
    capacity = min(tok_local, 6 * tok_local // experts)
    adapter_rank = adapter_lower_gate.shape[1]
    chunks = NUM_CHUNKS
    piece = capacity // chunks
    params = (
        gate_weight[0],
        up_weight[0],
        down_weight[0],
        adapter_lower_gate[0],
        adapter_upper_gate[0],
        adapter_lower_up[0],
        adapter_upper_up[0],
        adapter_lower_down[0],
        adapter_upper_down[0],
    )
    positions = slot_numbers(routing, experts)
    zero_row = jnp.zeros((1, feat_local), jnp.bfloat16)
    source, member = slot_sources(routing, positions, experts, capacity)
    clamped = jnp.minimum(source, tok_local - 1)
    slot_gate = jnp.where(
        source < tok_local, router_gate_values.reshape(-1)[clamped * choose + member], 0.0
    )
    send_x = jnp.concatenate([tokens, zero_row], 0)[source].reshape(experts, capacity, feat_local)
    send_dy = (
        (
            slot_gate[:, None]
            * jnp.concatenate([output_gradient, zero_row], 0)[source].astype(jnp.float32)
        )
        .astype(jnp.bfloat16)
        .reshape(experts, capacity, feat_local)
    )
    x_block = a2a_expert(send_x, 1)
    x_rows = lax.all_gather(x_block, "dp", axis=0, tiled=True)
    dy_block = a2a_expert(send_dy, 2)
    dy_rows = lax.all_gather(dy_block, "dp", axis=0, tiled=True)
    rows_out, parts, owned_total = rows_backward_parts(x_rows, dy_rows, params)
    packed = rows_out.reshape(shards, capacity, complete_width)
    summed = lax.psum_scatter(packed, "dp", scatter_dimension=0, tiled=True)[0]
    dense_rows = capacity * 3 * adapter_rank // PART_COLS
    parts_blocks = parts.reshape(shards, dense_rows, PART_COLS)
    parts_mine = reduce_dp(parts_blocks)
    parts_sum = gather_dp(parts_mine, shards).reshape(shards * capacity, 3 * adapter_rank)
    grad_a_pair = ADAPTER_SCALE * contract_pair(parts_sum[:, :2 * adapter_rank], x_rows, 0, 0)
    grad_a_gate = grad_a_pair[:adapter_rank]
    grad_a_up = grad_a_pair[adapter_rank:]
    grad_b_down = ADAPTER_SCALE * contract_pair(
        dy_rows, parts_sum[:, 2 * adapter_rank:3 * adapter_rank], 0, 0
    )
    returned_rows = lax.all_to_all(
        summed.reshape(capacity, experts, feat_local),
        "expert",
        split_axis=1,
        concat_axis=1,
        tiled=True,
    ).astype(jnp.float32)
    lookup = positions * experts + routing
    grad_x = jnp.sum(returned_rows.reshape(capacity * experts, feat_local)[lookup], axis=1).astype(
        jnp.bfloat16
    )
    return (
        grad_x,
        grad_a_gate[None],
        owned_total[0][None],
        grad_a_up[None],
        owned_total[1][None],
        owned_total[2][None],
        grad_b_down[None],
    )


def solution(mesh):
    return jax.shard_map(
        local,
        mesh=mesh,
        in_specs=(
            P("dp", "expert"),
            P("dp", "expert"),
            P("dp", None),
            P("dp", None),
            P("expert", "dp", None),
            P("expert", "dp", None),
            P("expert", "dp", None),
            P("expert", None, None),
            P("expert", "dp", None),
            P("expert", None, None),
            P("expert", "dp", None),
            P("expert", None, "dp"),
            P("expert", None, None),
        ),
        out_specs=(
            P("dp", "expert"),
            P("expert", None, None),
            P("expert", "dp", None),
            P("expert", None, None),
            P("expert", "dp", None),
            P("expert", None, "dp"),
            P("expert", None, None),
        ),
        check_vma=False,
    )
```

```python
import functools

import jax
import jax.numpy as jnp
from jax import lax
from jax.experimental import pallas as pl
from jax.experimental.pallas import tpu as pltpu
from jax.sharding import PartitionSpec as P

MESH = pl.DeviceIdType.MESH

ADAPTER_SCALE = 2.0
NUM_CHUNKS = 2
PART_COLS = 128


def contract_pair(left, right, left_axis, right_axis):
    return lax.dot_general(
        left, right, (((left_axis,), (right_axis,)), ((), ())), preferred_element_type=jnp.float32
    )


def slot_numbers(route_rows, experts):
    picked = (route_rows[:, :, None] == jnp.arange(experts, dtype=jnp.int32)[None, None, :]).astype(
        jnp.int32
    )
    per_token = jnp.sum(picked, axis=1)
    earlier = jnp.cumsum(per_token, axis=0) - per_token
    return jnp.sum(earlier[:, None, :] * picked, axis=2)


def slot_sources(route_rows, positions, experts, capacity):
    tokens_here, choose = route_rows.shape
    target = (route_rows * capacity + positions).reshape(-1)
    owners = jnp.repeat(jnp.arange(tokens_here, dtype=jnp.int32), choose)
    member_ids = jnp.tile(jnp.arange(choose, dtype=jnp.int32), tokens_here)
    source = jnp.full((experts * capacity,), tokens_here, jnp.int32).at[target].set(owners)
    member = jnp.zeros((experts * capacity,), jnp.int32).at[target].set(member_ids)
    return (source, member)


def rows_backward_pass(input_rows, output_gradient_rows, params):
    (
        gate_weight,
        up_weight,
        down_weight,
        a_gate,
        gate_adapter_upper,
        a_up,
        up_adapter_upper,
        down_adapter_lower,
        b_down,
    ) = params
    gate_projected_lower = contract_pair(a_gate, input_rows, 1, 1).astype(jnp.bfloat16)
    up_projected_lower = contract_pair(a_up, input_rows, 1, 1).astype(jnp.bfloat16)
    gate_preactivation = contract_pair(
        gate_weight, input_rows, 1, 1
    ) + ADAPTER_SCALE * contract_pair(gate_adapter_upper, gate_projected_lower, 1, 0)
    up_preactivation = contract_pair(up_weight, input_rows, 1, 1) + ADAPTER_SCALE * contract_pair(
        up_adapter_upper, up_projected_lower, 1, 0
    )
    sigmoid_gate = jax.nn.sigmoid(gate_preactivation)
    silu_gate = gate_preactivation * sigmoid_gate
    hidden_units = (silu_gate * up_preactivation).astype(jnp.bfloat16)
    down_projected_lower = contract_pair(b_down, output_gradient_rows, 0, 1).astype(jnp.bfloat16)
    hidden_gradient = contract_pair(
        down_weight, output_gradient_rows, 1, 1
    ) + ADAPTER_SCALE * contract_pair(down_adapter_lower, down_projected_lower, 0, 0)
    gate_gradient = (
        hidden_gradient
        * up_preactivation
        * sigmoid_gate
        * (1.0 + gate_preactivation * (1.0 - sigmoid_gate))
    ).astype(jnp.bfloat16)
    up_gradient = (hidden_gradient * silu_gate).astype(jnp.bfloat16)
    gate_partial = contract_pair(gate_adapter_upper, gate_gradient, 0, 0).astype(jnp.bfloat16)
    up_partial = contract_pair(up_adapter_upper, up_gradient, 0, 0).astype(jnp.bfloat16)
    down_partial = contract_pair(down_adapter_lower, hidden_units, 1, 0).astype(jnp.bfloat16)
    paired_partials = jnp.concatenate([gate_partial, up_partial], 0)
    paired_factors = jnp.concatenate([a_gate, a_up], 0)
    gradient_rows_out = (
        contract_pair(gate_gradient, gate_weight, 0, 0)
        + contract_pair(up_gradient, up_weight, 0, 0)
        + ADAPTER_SCALE * contract_pair(paired_partials, paired_factors, 0, 0)
    )
    shared_slice = (
        ADAPTER_SCALE * contract_pair(gate_partial, input_rows, 1, 0),
        ADAPTER_SCALE * contract_pair(up_partial, input_rows, 1, 0),
        ADAPTER_SCALE * contract_pair(output_gradient_rows, down_partial, 0, 1),
    )
    owned_slice = (
        ADAPTER_SCALE * contract_pair(gate_gradient, gate_projected_lower, 1, 1),
        ADAPTER_SCALE * contract_pair(up_gradient, up_projected_lower, 1, 1),
        ADAPTER_SCALE * contract_pair(down_projected_lower, hidden_units, 1, 1),
    )
    return (gradient_rows_out, shared_slice, owned_slice)


def rows_backward_parts(input_rows, output_gradient_rows, params):
    (
        gate_weight,
        up_weight,
        down_weight,
        a_gate,
        gate_adapter_upper,
        a_up,
        up_adapter_upper,
        down_adapter_lower,
        b_down,
    ) = params
    gate_projected_lower = contract_pair(a_gate, input_rows, 1, 1).astype(jnp.bfloat16)
    up_projected_lower = contract_pair(a_up, input_rows, 1, 1).astype(jnp.bfloat16)
    gate_preactivation = contract_pair(
        gate_weight, input_rows, 1, 1
    ) + ADAPTER_SCALE * contract_pair(gate_adapter_upper, gate_projected_lower, 1, 0)
    up_preactivation = contract_pair(up_weight, input_rows, 1, 1) + ADAPTER_SCALE * contract_pair(
        up_adapter_upper, up_projected_lower, 1, 0
    )
    sigmoid_gate = jax.nn.sigmoid(gate_preactivation)
    silu_gate = gate_preactivation * sigmoid_gate
    hidden_units = (silu_gate * up_preactivation).astype(jnp.bfloat16)
    down_partial = contract_pair(hidden_units, down_adapter_lower, 0, 1).astype(jnp.bfloat16)
    (
        output_gradient_rows,
        gate_preactivation,
        up_preactivation,
        sigmoid_gate,
        silu_gate,
        hidden_units,
        down_partial,
        gate_projected_lower,
        up_projected_lower,
    ) = lax.optimization_barrier(
        (
            output_gradient_rows,
            gate_preactivation,
            up_preactivation,
            sigmoid_gate,
            silu_gate,
            hidden_units,
            down_partial,
            gate_projected_lower,
            up_projected_lower,
        )
    )
    hidden_here = down_weight.shape[0]
    down_both = contract_pair(
        jnp.concatenate([down_weight, b_down.T], 0), output_gradient_rows, 1, 1
    )
    down_projected_lower = down_both[hidden_here:].astype(jnp.bfloat16)
    hidden_gradient = down_both[:hidden_here] + ADAPTER_SCALE * contract_pair(
        down_adapter_lower, down_projected_lower, 0, 0
    )
    gate_gradient = (
        hidden_gradient
        * up_preactivation
        * sigmoid_gate
        * (1.0 + gate_preactivation * (1.0 - sigmoid_gate))
    ).astype(jnp.bfloat16)
    up_gradient = (hidden_gradient * silu_gate).astype(jnp.bfloat16)
    gate_partial = contract_pair(gate_gradient, gate_adapter_upper, 0, 0).astype(jnp.bfloat16)
    up_partial = contract_pair(up_gradient, up_adapter_upper, 0, 0).astype(jnp.bfloat16)
    parts = jnp.concatenate([gate_partial, up_partial, down_partial], 1)
    pair = jnp.concatenate([gate_partial, up_partial], 1)
    lhs = jnp.concatenate([gate_gradient, up_gradient, pair.T], 0)
    lora_rows = jnp.concatenate(
        [
            (ADAPTER_SCALE * a_gate.astype(jnp.float32)).astype(jnp.bfloat16),
            (ADAPTER_SCALE * a_up.astype(jnp.float32)).astype(jnp.bfloat16),
        ],
        0,
    )
    extended = jnp.concatenate([gate_weight, up_weight, lora_rows], 0)
    gradient_rows_out = lax.dot_general(
        lhs, extended, (((0,), (0,)), ((), ())), preferred_element_type=jnp.float32
    ).astype(jnp.bfloat16)
    owned_slice = (
        ADAPTER_SCALE * contract_pair(gate_gradient, gate_projected_lower, 1, 1),
        ADAPTER_SCALE * contract_pair(up_gradient, up_projected_lower, 1, 1),
        ADAPTER_SCALE * contract_pair(down_projected_lower, hidden_units, 1, 1),
    )
    return (gradient_rows_out, parts, owned_slice)


def gather_dp_kernel(n, src_ref, out_ref, send_sem, recv_sem):
    me = lax.axis_index("dp")
    ex = lax.axis_index("expert")
    barrier = pltpu.get_barrier_semaphore()
    for k in range(1, n):
        peer = lax.rem(me + k, n)
        pl.semaphore_signal(barrier, inc=1, device_id=(peer, ex), device_id_type=MESH)
    pl.semaphore_wait(barrier, n - 1)
    copies = []
    for k in range(1, n):
        peer = lax.rem(me + k, n)
        cp = pltpu.make_async_remote_copy(
            src_ref,
            out_ref.at[me],
            send_sem.at[k],
            recv_sem.at[k],
            device_id=(peer, ex),
            device_id_type=MESH,
        )
        cp.start()
        copies.append(cp)
    out_ref[me] = src_ref[...]
    for cp in copies:
        cp.wait()


def gather_dp(block, n):
    return pl.pallas_call(
        functools.partial(gather_dp_kernel, n),
        out_shape=jax.ShapeDtypeStruct((n,) + block.shape, block.dtype),
        in_specs=[pl.BlockSpec(memory_space=pltpu.VMEM)],
        out_specs=pl.BlockSpec(memory_space=pltpu.VMEM),
        scratch_shapes=[pltpu.SemaphoreType.DMA((n,)), pltpu.SemaphoreType.DMA((n,))],
        compiler_params=pltpu.CompilerParams(collective_id=0, has_side_effects=True),
    )(block)


def a2a_expert_kernel(n, width, src_ref, out_ref, send_sem, recv_sem):
    me = lax.axis_index("expert")
    row = lax.axis_index("dp")
    barrier = pltpu.get_barrier_semaphore()
    for k in range(1, n):
        peer = lax.rem(me + k, n)
        pl.semaphore_signal(barrier, inc=1, device_id=(row, peer), device_id_type=MESH)
    pl.semaphore_wait(barrier, n - 1)
    mine = pl.ds(pl.multiple_of(me * width, width), width)
    copies = []
    for k in range(1, n):
        peer = lax.rem(me + k, n)
        cp = pltpu.make_async_remote_copy(
            src_ref.at[peer],
            out_ref.at[:, mine],
            send_sem.at[k],
            recv_sem.at[k],
            device_id=(row, peer),
            device_id_type=MESH,
        )
        cp.start()
        copies.append(cp)
    out_ref[:, mine] = src_ref[me]
    for cp in copies:
        cp.wait()


def a2a_expert(send, exchange_id):
    n, rows, width = send.shape
    return pl.pallas_call(
        functools.partial(a2a_expert_kernel, n, width),
        out_shape=jax.ShapeDtypeStruct((rows, n * width), send.dtype),
        in_specs=[pl.BlockSpec(memory_space=pltpu.VMEM)],
        out_specs=pl.BlockSpec(memory_space=pltpu.VMEM),
        scratch_shapes=[pltpu.SemaphoreType.DMA((n,)), pltpu.SemaphoreType.DMA((n,))],
        compiler_params=pltpu.CompilerParams(collective_id=exchange_id, has_side_effects=True),
    )(send)

def reduce_dp_kernel(n, src_ref, out_ref, landing, send_sem, recv_sem):
    me = lax.axis_index("dp")
    ex = lax.axis_index("expert")
    barrier = pltpu.get_barrier_semaphore()
    for k in range(1, n):
        peer = lax.rem(me + k, n)
        pl.semaphore_signal(barrier, inc=1, device_id=(peer, ex), device_id_type=MESH)
    pl.semaphore_wait(barrier, n - 1)
    copies = []
    for k in range(1, n):
        peer = lax.rem(me + k, n)
        cp = pltpu.make_async_remote_copy(
            src_ref.at[peer],
            landing.at[me],
            send_sem.at[k],
            recv_sem.at[k],
            device_id=(peer, ex),
            device_id_type=MESH,
        )
        cp.start()
        copies.append(cp)
    landing[me] = src_ref[me]
    for cp in copies:
        cp.wait()
    out_ref[...] = jnp.sum(landing[...].astype(jnp.float32), axis=0)


def reduce_dp(blocks):
    n, rows, cols = blocks.shape
    return pl.pallas_call(
        functools.partial(reduce_dp_kernel, n),
        out_shape=jax.ShapeDtypeStruct((rows, cols), jnp.float32),
        in_specs=[pl.BlockSpec(memory_space=pltpu.VMEM)],
        out_specs=pl.BlockSpec(memory_space=pltpu.VMEM),
        scratch_shapes=[
            pltpu.VMEM((n, rows, cols), blocks.dtype),
            pltpu.SemaphoreType.DMA((n,)),
            pltpu.SemaphoreType.DMA((n,)),
        ],
        compiler_params=pltpu.CompilerParams(collective_id=3, has_side_effects=True),
    )(blocks)


def local(
    tokens,
    output_gradient,
    routing,
    router_gate_values,
    gate_weight,
    up_weight,
    down_weight,
    adapter_lower_gate,
    adapter_upper_gate,
    adapter_lower_up,
    adapter_upper_up,
    adapter_lower_down,
    adapter_upper_down,
):
    experts = lax.axis_size("expert")
    shards = lax.axis_size("dp")
    tok_local, feat_local = tokens.shape
    choose = routing.shape[1]
    complete_width = feat_local * experts
    capacity = min(tok_local, 6 * tok_local // experts)
    adapter_rank = adapter_lower_gate.shape[1]
    chunks = NUM_CHUNKS
    piece = capacity // chunks
    params = (
        gate_weight[0],
        up_weight[0],
        down_weight[0],
        adapter_lower_gate[0],
        adapter_upper_gate[0],
        adapter_lower_up[0],
        adapter_upper_up[0],
        adapter_lower_down[0],
        adapter_upper_down[0],
    )
    positions = slot_numbers(routing, experts)
    zero_row = jnp.zeros((1, feat_local), jnp.bfloat16)
    source, member = slot_sources(routing, positions, experts, capacity)
    clamped = jnp.minimum(source, tok_local - 1)
    slot_gate = jnp.where(
        source < tok_local, router_gate_values.reshape(-1)[clamped * choose + member], 0.0
    )
    send_x = jnp.concatenate([tokens, zero_row], 0)[source].reshape(experts, capacity, feat_local)
    send_dy = (
        (
            slot_gate[:, None]
            * jnp.concatenate([output_gradient, zero_row], 0)[source].astype(jnp.float32)
        )
        .astype(jnp.bfloat16)
        .reshape(experts, capacity, feat_local)
    )
    x_block = a2a_expert(send_x, 1)
    x_rows = lax.all_gather(x_block, "dp", axis=0, tiled=True)
    dy_block = a2a_expert(send_dy, 2)
    dy_rows = lax.all_gather(dy_block, "dp", axis=0, tiled=True)
    rows_out, parts, owned_total = rows_backward_parts(x_rows, dy_rows, params)
    packed = rows_out.reshape(shards, capacity, complete_width)
    summed = lax.psum_scatter(packed, "dp", scatter_dimension=0, tiled=True)[0]
    dense_rows = capacity * 3 * adapter_rank // PART_COLS
    parts_blocks = parts.reshape(shards, dense_rows, PART_COLS)
    parts_mine = reduce_dp(parts_blocks)
    parts_sum = gather_dp(parts_mine, shards).reshape(shards * capacity, 3 * adapter_rank)
    grad_a_pair = ADAPTER_SCALE * contract_pair(parts_sum[:, :2 * adapter_rank], x_rows, 0, 0)
    grad_a_gate = grad_a_pair[:adapter_rank]
    grad_a_up = grad_a_pair[adapter_rank:]
    grad_b_down = ADAPTER_SCALE * contract_pair(
        dy_rows, parts_sum[:, 2 * adapter_rank:3 * adapter_rank], 0, 0
    )
    returned_rows = lax.all_to_all(
        summed.reshape(capacity, experts, feat_local),
        "expert",
        split_axis=1,
        concat_axis=1,
        tiled=True,
    ).astype(jnp.float32)
    lookup = positions * experts + routing
    grad_x = jnp.sum(returned_rows.reshape(capacity * experts, feat_local)[lookup], axis=1).astype(
        jnp.bfloat16
    )
    return (
        grad_x,
        grad_a_gate[None],
        owned_total[0][None],
        grad_a_up[None],
        owned_total[1][None],
        owned_total[2][None],
        grad_b_down[None],
    )


def solution(mesh):
    return jax.shard_map(
        local,
        mesh=mesh,
        in_specs=(
            P("dp", "expert"),
            P("dp", "expert"),
            P("dp", None),
            P("dp", None),
            P("expert", "dp", None),
            P("expert", "dp", None),
            P("expert", "dp", None),
            P("expert", None, None),
            P("expert", "dp", None),
            P("expert", None, None),
            P("expert", "dp", None),
            P("expert", None, "dp"),
            P("expert", None, None),
        ),
        out_specs=(
            P("dp", "expert"),
            P("expert", None, None),
            P("expert", "dp", None),
            P("expert", None, None),
            P("expert", "dp", None),
            P("expert", None, "dp"),
            P("expert", None, None),
        ),
        check_vma=False,
    )
```

```python
import functools

import jax
import jax.numpy as jnp
from jax import lax
from jax.experimental import pallas as pl
from jax.experimental.pallas import tpu as pltpu
from jax.sharding import PartitionSpec as P

MESH = pl.DeviceIdType.MESH

ADAPTER_SCALE = 2.0
NUM_CHUNKS = 2
PART_COLS = 128


def contract_pair(left, right, left_axis, right_axis):
    return lax.dot_general(
        left, right, (((left_axis,), (right_axis,)), ((), ())), preferred_element_type=jnp.float32
    )


def slot_numbers(route_rows, experts):
    picked = (route_rows[:, :, None] == jnp.arange(experts, dtype=jnp.int32)[None, None, :]).astype(
        jnp.int32
    )
    per_token = jnp.sum(picked, axis=1)
    earlier = jnp.cumsum(per_token, axis=0) - per_token
    return jnp.sum(earlier[:, None, :] * picked, axis=2)


def slot_sources(route_rows, positions, experts, capacity):
    tokens_here, choose = route_rows.shape
    target = (route_rows * capacity + positions).reshape(-1)
    owners = jnp.repeat(jnp.arange(tokens_here, dtype=jnp.int32), choose)
    member_ids = jnp.tile(jnp.arange(choose, dtype=jnp.int32), tokens_here)
    source = jnp.full((experts * capacity,), tokens_here, jnp.int32).at[target].set(owners)
    member = jnp.zeros((experts * capacity,), jnp.int32).at[target].set(member_ids)
    return (source, member)


def rows_backward_pass(input_rows, output_gradient_rows, params):
    (
        gate_weight,
        up_weight,
        down_weight,
        a_gate,
        gate_adapter_upper,
        a_up,
        up_adapter_upper,
        down_adapter_lower,
        b_down,
    ) = params
    gate_projected_lower = contract_pair(a_gate, input_rows, 1, 1).astype(jnp.bfloat16)
    up_projected_lower = contract_pair(a_up, input_rows, 1, 1).astype(jnp.bfloat16)
    gate_preactivation = contract_pair(
        gate_weight, input_rows, 1, 1
    ) + ADAPTER_SCALE * contract_pair(gate_adapter_upper, gate_projected_lower, 1, 0)
    up_preactivation = contract_pair(up_weight, input_rows, 1, 1) + ADAPTER_SCALE * contract_pair(
        up_adapter_upper, up_projected_lower, 1, 0
    )
    sigmoid_gate = jax.nn.sigmoid(gate_preactivation)
    silu_gate = gate_preactivation * sigmoid_gate
    hidden_units = (silu_gate * up_preactivation).astype(jnp.bfloat16)
    down_projected_lower = contract_pair(b_down, output_gradient_rows, 0, 1).astype(jnp.bfloat16)
    hidden_gradient = contract_pair(
        down_weight, output_gradient_rows, 1, 1
    ) + ADAPTER_SCALE * contract_pair(down_adapter_lower, down_projected_lower, 0, 0)
    gate_gradient = (
        hidden_gradient
        * up_preactivation
        * sigmoid_gate
        * (1.0 + gate_preactivation * (1.0 - sigmoid_gate))
    ).astype(jnp.bfloat16)
    up_gradient = (hidden_gradient * silu_gate).astype(jnp.bfloat16)
    gate_partial = contract_pair(gate_adapter_upper, gate_gradient, 0, 0).astype(jnp.bfloat16)
    up_partial = contract_pair(up_adapter_upper, up_gradient, 0, 0).astype(jnp.bfloat16)
    down_partial = contract_pair(down_adapter_lower, hidden_units, 1, 0).astype(jnp.bfloat16)
    paired_partials = jnp.concatenate([gate_partial, up_partial], 0)
    paired_factors = jnp.concatenate([a_gate, a_up], 0)
    gradient_rows_out = (
        contract_pair(gate_gradient, gate_weight, 0, 0)
        + contract_pair(up_gradient, up_weight, 0, 0)
        + ADAPTER_SCALE * contract_pair(paired_partials, paired_factors, 0, 0)
    )
    shared_slice = (
        ADAPTER_SCALE * contract_pair(gate_partial, input_rows, 1, 0),
        ADAPTER_SCALE * contract_pair(up_partial, input_rows, 1, 0),
        ADAPTER_SCALE * contract_pair(output_gradient_rows, down_partial, 0, 1),
    )
    owned_slice = (
        ADAPTER_SCALE * contract_pair(gate_gradient, gate_projected_lower, 1, 1),
        ADAPTER_SCALE * contract_pair(up_gradient, up_projected_lower, 1, 1),
        ADAPTER_SCALE * contract_pair(down_projected_lower, hidden_units, 1, 1),
    )
    return (gradient_rows_out, shared_slice, owned_slice)


def rows_backward_parts(input_rows, output_gradient_rows, params):
    (
        gate_weight,
        up_weight,
        down_weight,
        a_gate,
        gate_adapter_upper,
        a_up,
        up_adapter_upper,
        down_adapter_lower,
        b_down,
    ) = params
    gate_projected_lower = contract_pair(a_gate, input_rows, 1, 1).astype(jnp.bfloat16)
    up_projected_lower = contract_pair(a_up, input_rows, 1, 1).astype(jnp.bfloat16)
    gate_preactivation = contract_pair(
        gate_weight, input_rows, 1, 1
    ) + ADAPTER_SCALE * contract_pair(gate_adapter_upper, gate_projected_lower, 1, 0)
    up_preactivation = contract_pair(up_weight, input_rows, 1, 1) + ADAPTER_SCALE * contract_pair(
        up_adapter_upper, up_projected_lower, 1, 0
    )
    sigmoid_gate = jax.nn.sigmoid(gate_preactivation)
    silu_gate = gate_preactivation * sigmoid_gate
    hidden_units = (silu_gate * up_preactivation).astype(jnp.bfloat16)
    down_partial = contract_pair(hidden_units, down_adapter_lower, 0, 1).astype(jnp.bfloat16)
    (
        output_gradient_rows,
        gate_preactivation,
        up_preactivation,
        sigmoid_gate,
        silu_gate,
        hidden_units,
        down_partial,
        gate_projected_lower,
        up_projected_lower,
    ) = lax.optimization_barrier(
        (
            output_gradient_rows,
            gate_preactivation,
            up_preactivation,
            sigmoid_gate,
            silu_gate,
            hidden_units,
            down_partial,
            gate_projected_lower,
            up_projected_lower,
        )
    )
    hidden_here = down_weight.shape[0]
    down_both = contract_pair(
        jnp.concatenate([down_weight, b_down.T], 0), output_gradient_rows, 1, 1
    )
    down_projected_lower = down_both[hidden_here:].astype(jnp.bfloat16)
    hidden_gradient = down_both[:hidden_here] + ADAPTER_SCALE * contract_pair(
        down_adapter_lower, down_projected_lower, 0, 0
    )
    gate_gradient = (
        hidden_gradient
        * up_preactivation
        * sigmoid_gate
        * (1.0 + gate_preactivation * (1.0 - sigmoid_gate))
    ).astype(jnp.bfloat16)
    up_gradient = (hidden_gradient * silu_gate).astype(jnp.bfloat16)
    gate_partial = contract_pair(gate_gradient, gate_adapter_upper, 0, 0).astype(jnp.bfloat16)
    up_partial = contract_pair(up_gradient, up_adapter_upper, 0, 0).astype(jnp.bfloat16)
    parts = jnp.concatenate([gate_partial, up_partial, down_partial], 1)
    pair = jnp.concatenate([gate_partial, up_partial], 1)
    lhs = jnp.concatenate([gate_gradient, up_gradient, pair.T], 0)
    lora_rows = jnp.concatenate(
        [
            (ADAPTER_SCALE * a_gate.astype(jnp.float32)).astype(jnp.bfloat16),
            (ADAPTER_SCALE * a_up.astype(jnp.float32)).astype(jnp.bfloat16),
        ],
        0,
    )
    extended = jnp.concatenate([gate_weight, up_weight, lora_rows], 0)
    gradient_rows_out = lax.dot_general(
        lhs, extended, (((0,), (0,)), ((), ())), preferred_element_type=jnp.float32
    ).astype(jnp.bfloat16)
    owned_slice = (
        ADAPTER_SCALE * contract_pair(gate_gradient, gate_projected_lower, 1, 1),
        ADAPTER_SCALE * contract_pair(up_gradient, up_projected_lower, 1, 1),
        ADAPTER_SCALE * contract_pair(down_projected_lower, hidden_units, 1, 1),
    )
    return (gradient_rows_out, parts, owned_slice)


def gather_dp_kernel(n, src_ref, out_ref, send_sem, recv_sem):
    me = lax.axis_index("dp")
    ex = lax.axis_index("expert")
    barrier = pltpu.get_barrier_semaphore()
    for k in range(1, n):
        peer = lax.rem(me + k, n)
        pl.semaphore_signal(barrier, inc=1, device_id=(peer, ex), device_id_type=MESH)
    pl.semaphore_wait(barrier, n - 1)
    copies = []
    for k in range(1, n):
        peer = lax.rem(me + k, n)
        cp = pltpu.make_async_remote_copy(
            src_ref,
            out_ref.at[me],
            send_sem.at[k],
            recv_sem.at[k],
            device_id=(peer, ex),
            device_id_type=MESH,
        )
        cp.start()
        copies.append(cp)
    out_ref[me] = src_ref[...]
    for cp in copies:
        cp.wait()


def gather_dp(block, n):
    return pl.pallas_call(
        functools.partial(gather_dp_kernel, n),
        out_shape=jax.ShapeDtypeStruct((n,) + block.shape, block.dtype),
        in_specs=[pl.BlockSpec(memory_space=pltpu.VMEM)],
        out_specs=pl.BlockSpec(memory_space=pltpu.VMEM),
        scratch_shapes=[pltpu.SemaphoreType.DMA((n,)), pltpu.SemaphoreType.DMA((n,))],
        compiler_params=pltpu.CompilerParams(collective_id=0, has_side_effects=True),
    )(block)


def a2a_expert_kernel(n, width, src_ref, out_ref, send_sem, recv_sem):
    me = lax.axis_index("expert")
    row = lax.axis_index("dp")
    barrier = pltpu.get_barrier_semaphore()
    for k in range(1, n):
        peer = lax.rem(me + k, n)
        pl.semaphore_signal(barrier, inc=1, device_id=(row, peer), device_id_type=MESH)
    pl.semaphore_wait(barrier, n - 1)
    mine = pl.ds(pl.multiple_of(me * width, width), width)
    copies = []
    for k in range(1, n):
        peer = lax.rem(me + k, n)
        cp = pltpu.make_async_remote_copy(
            src_ref.at[peer],
            out_ref.at[:, mine],
            send_sem.at[k],
            recv_sem.at[k],
            device_id=(row, peer),
            device_id_type=MESH,
        )
        cp.start()
        copies.append(cp)
    out_ref[:, mine] = src_ref[me]
    for cp in copies:
        cp.wait()


def a2a_expert(send, exchange_id):
    n, rows, width = send.shape
    return pl.pallas_call(
        functools.partial(a2a_expert_kernel, n, width),
        out_shape=jax.ShapeDtypeStruct((rows, n * width), send.dtype),
        in_specs=[pl.BlockSpec(memory_space=pltpu.VMEM)],
        out_specs=pl.BlockSpec(memory_space=pltpu.VMEM),
        scratch_shapes=[pltpu.SemaphoreType.DMA((n,)), pltpu.SemaphoreType.DMA((n,))],
        compiler_params=pltpu.CompilerParams(collective_id=exchange_id, has_side_effects=True),
    )(send)

def reduce_dp_kernel(n, src_ref, out_ref, landing, send_sem, recv_sem):
    me = lax.axis_index("dp")
    ex = lax.axis_index("expert")
    barrier = pltpu.get_barrier_semaphore()
    for k in range(1, n):
        peer = lax.rem(me + k, n)
        pl.semaphore_signal(barrier, inc=1, device_id=(peer, ex), device_id_type=MESH)
    pl.semaphore_wait(barrier, n - 1)
    copies = []
    for k in range(1, n):
        peer = lax.rem(me + k, n)
        cp = pltpu.make_async_remote_copy(
            src_ref.at[peer],
            landing.at[me],
            send_sem.at[k],
            recv_sem.at[k],
            device_id=(peer, ex),
            device_id_type=MESH,
        )
        cp.start()
        copies.append(cp)
    landing[me] = src_ref[me]
    for cp in copies:
        cp.wait()
    out_ref[...] = jnp.sum(landing[...].astype(jnp.float32), axis=0)


def reduce_dp(blocks):
    n, rows, cols = blocks.shape
    return pl.pallas_call(
        functools.partial(reduce_dp_kernel, n),
        out_shape=jax.ShapeDtypeStruct((rows, cols), jnp.float32),
        in_specs=[pl.BlockSpec(memory_space=pltpu.VMEM)],
        out_specs=pl.BlockSpec(memory_space=pltpu.VMEM),
        scratch_shapes=[
            pltpu.VMEM((n, rows, cols), blocks.dtype),
            pltpu.SemaphoreType.DMA((n,)),
            pltpu.SemaphoreType.DMA((n,)),
        ],
        compiler_params=pltpu.CompilerParams(collective_id=3, has_side_effects=True),
    )(blocks)


def local(
    tokens,
    output_gradient,
    routing,
    router_gate_values,
    gate_weight,
    up_weight,
    down_weight,
    adapter_lower_gate,
    adapter_upper_gate,
    adapter_lower_up,
    adapter_upper_up,
    adapter_lower_down,
    adapter_upper_down,
):
    experts = lax.axis_size("expert")
    shards = lax.axis_size("dp")
    tok_local, feat_local = tokens.shape
    choose = routing.shape[1]
    complete_width = feat_local * experts
    capacity = min(tok_local, 6 * tok_local // experts)
    adapter_rank = adapter_lower_gate.shape[1]
    chunks = NUM_CHUNKS
    piece = capacity // chunks
    params = (
        gate_weight[0],
        up_weight[0],
        down_weight[0],
        adapter_lower_gate[0],
        adapter_upper_gate[0],
        adapter_lower_up[0],
        adapter_upper_up[0],
        adapter_lower_down[0],
        adapter_upper_down[0],
    )
    positions = slot_numbers(routing, experts)
    zero_row = jnp.zeros((1, feat_local), jnp.bfloat16)
    source, member = slot_sources(routing, positions, experts, capacity)
    clamped = jnp.minimum(source, tok_local - 1)
    slot_gate = jnp.where(
        source < tok_local, router_gate_values.reshape(-1)[clamped * choose + member], 0.0
    )
    send_x = jnp.concatenate([tokens, zero_row], 0)[source].reshape(experts, capacity, feat_local)
    send_dy = (
        (
            slot_gate[:, None]
            * jnp.concatenate([output_gradient, zero_row], 0)[source].astype(jnp.float32)
        )
        .astype(jnp.bfloat16)
        .reshape(experts, capacity, feat_local)
    )
    x_block = a2a_expert(send_x, 1)
    x_rows = lax.all_gather(x_block, "dp", axis=0, tiled=True)
    dy_block = a2a_expert(send_dy, 2)
    dy_rows = lax.all_gather(dy_block, "dp", axis=0, tiled=True)
    rows_out, parts, owned_total = rows_backward_parts(x_rows, dy_rows, params)
    packed = rows_out.reshape(shards, capacity, complete_width)
    summed = lax.psum_scatter(packed, "dp", scatter_dimension=0, tiled=True)[0]
    dense_rows = capacity * 3 * adapter_rank // PART_COLS
    parts_blocks = parts.reshape(shards, dense_rows, PART_COLS)
    parts_mine = reduce_dp(parts_blocks)
    parts_sum = gather_dp(parts_mine, shards).reshape(shards * capacity, 3 * adapter_rank)
    grad_a_pair = ADAPTER_SCALE * contract_pair(parts_sum[:, :2 * adapter_rank], x_rows, 0, 0)
    grad_a_gate = grad_a_pair[:adapter_rank]
    grad_a_up = grad_a_pair[adapter_rank:]
    grad_b_down = ADAPTER_SCALE * contract_pair(
        dy_rows, parts_sum[:, 2 * adapter_rank:3 * adapter_rank], 0, 0
    )
    returned_rows = a2a_expert(
        summed.reshape(capacity, experts, feat_local).transpose(1, 0, 2), 4
    ).astype(jnp.float32)
    lookup = positions * experts + routing
    grad_x = jnp.sum(returned_rows.reshape(capacity * experts, feat_local)[lookup], axis=1).astype(
        jnp.bfloat16
    )
    return (
        grad_x,
        grad_a_gate[None],
        owned_total[0][None],
        grad_a_up[None],
        owned_total[1][None],
        owned_total[2][None],
        grad_b_down[None],
    )


def solution(mesh):
    return jax.shard_map(
        local,
        mesh=mesh,
        in_specs=(
            P("dp", "expert"),
            P("dp", "expert"),
            P("dp", None),
            P("dp", None),
            P("expert", "dp", None),
            P("expert", "dp", None),
            P("expert", "dp", None),
            P("expert", None, None),
            P("expert", "dp", None),
            P("expert", None, None),
            P("expert", "dp", None),
            P("expert", None, "dp"),
            P("expert", None, None),
        ),
        out_specs=(
            P("dp", "expert"),
            P("expert", None, None),
            P("expert", "dp", None),
            P("expert", None, None),
            P("expert", "dp", None),
            P("expert", None, "dp"),
            P("expert", None, None),
        ),
        check_vma=False,
    )
```

```python
import functools

import jax
import jax.numpy as jnp
from jax import lax
from jax.experimental import pallas as pl
from jax.experimental.pallas import tpu as pltpu
from jax.sharding import PartitionSpec as P

MESH = pl.DeviceIdType.MESH

ADAPTER_SCALE = 2.0
NUM_CHUNKS = 2
PART_COLS = 128


def contract_pair(left, right, left_axis, right_axis):
    return lax.dot_general(
        left, right, (((left_axis,), (right_axis,)), ((), ())), preferred_element_type=jnp.float32
    )


def slot_numbers(route_rows, experts):
    picked = (route_rows[:, :, None] == jnp.arange(experts, dtype=jnp.int32)[None, None, :]).astype(
        jnp.int32
    )
    per_token = jnp.sum(picked, axis=1)
    earlier = jnp.cumsum(per_token, axis=0) - per_token
    return jnp.sum(earlier[:, None, :] * picked, axis=2)


def slot_sources(route_rows, positions, experts, capacity):
    tokens_here, choose = route_rows.shape
    target = (route_rows * capacity + positions).reshape(-1)
    owners = jnp.repeat(jnp.arange(tokens_here, dtype=jnp.int32), choose)
    member_ids = jnp.tile(jnp.arange(choose, dtype=jnp.int32), tokens_here)
    source = jnp.full((experts * capacity,), tokens_here, jnp.int32).at[target].set(owners)
    member = jnp.zeros((experts * capacity,), jnp.int32).at[target].set(member_ids)
    return (source, member)


def rows_backward_pass(input_rows, output_gradient_rows, params):
    (
        gate_weight,
        up_weight,
        down_weight,
        a_gate,
        gate_adapter_upper,
        a_up,
        up_adapter_upper,
        down_adapter_lower,
        b_down,
    ) = params
    gate_projected_lower = contract_pair(a_gate, input_rows, 1, 1).astype(jnp.bfloat16)
    up_projected_lower = contract_pair(a_up, input_rows, 1, 1).astype(jnp.bfloat16)
    gate_preactivation = contract_pair(
        gate_weight, input_rows, 1, 1
    ) + ADAPTER_SCALE * contract_pair(gate_adapter_upper, gate_projected_lower, 1, 0)
    up_preactivation = contract_pair(up_weight, input_rows, 1, 1) + ADAPTER_SCALE * contract_pair(
        up_adapter_upper, up_projected_lower, 1, 0
    )
    sigmoid_gate = jax.nn.sigmoid(gate_preactivation)
    silu_gate = gate_preactivation * sigmoid_gate
    hidden_units = (silu_gate * up_preactivation).astype(jnp.bfloat16)
    down_projected_lower = contract_pair(b_down, output_gradient_rows, 0, 1).astype(jnp.bfloat16)
    hidden_gradient = contract_pair(
        down_weight, output_gradient_rows, 1, 1
    ) + ADAPTER_SCALE * contract_pair(down_adapter_lower, down_projected_lower, 0, 0)
    gate_gradient = (
        hidden_gradient
        * up_preactivation
        * sigmoid_gate
        * (1.0 + gate_preactivation * (1.0 - sigmoid_gate))
    ).astype(jnp.bfloat16)
    up_gradient = (hidden_gradient * silu_gate).astype(jnp.bfloat16)
    gate_partial = contract_pair(gate_adapter_upper, gate_gradient, 0, 0).astype(jnp.bfloat16)
    up_partial = contract_pair(up_adapter_upper, up_gradient, 0, 0).astype(jnp.bfloat16)
    down_partial = contract_pair(down_adapter_lower, hidden_units, 1, 0).astype(jnp.bfloat16)
    paired_partials = jnp.concatenate([gate_partial, up_partial], 0)
    paired_factors = jnp.concatenate([a_gate, a_up], 0)
    gradient_rows_out = (
        contract_pair(gate_gradient, gate_weight, 0, 0)
        + contract_pair(up_gradient, up_weight, 0, 0)
        + ADAPTER_SCALE * contract_pair(paired_partials, paired_factors, 0, 0)
    )
    shared_slice = (
        ADAPTER_SCALE * contract_pair(gate_partial, input_rows, 1, 0),
        ADAPTER_SCALE * contract_pair(up_partial, input_rows, 1, 0),
        ADAPTER_SCALE * contract_pair(output_gradient_rows, down_partial, 0, 1),
    )
    owned_slice = (
        ADAPTER_SCALE * contract_pair(gate_gradient, gate_projected_lower, 1, 1),
        ADAPTER_SCALE * contract_pair(up_gradient, up_projected_lower, 1, 1),
        ADAPTER_SCALE * contract_pair(down_projected_lower, hidden_units, 1, 1),
    )
    return (gradient_rows_out, shared_slice, owned_slice)


def rows_backward_parts(input_rows, output_gradient_rows, params):
    (
        gate_weight,
        up_weight,
        down_weight,
        a_gate,
        gate_adapter_upper,
        a_up,
        up_adapter_upper,
        down_adapter_lower,
        b_down,
    ) = params
    gate_projected_lower = contract_pair(a_gate, input_rows, 1, 1).astype(jnp.bfloat16)
    up_projected_lower = contract_pair(a_up, input_rows, 1, 1).astype(jnp.bfloat16)
    gate_preactivation = contract_pair(
        gate_weight, input_rows, 1, 1
    ) + ADAPTER_SCALE * contract_pair(gate_adapter_upper, gate_projected_lower, 1, 0)
    up_preactivation = contract_pair(up_weight, input_rows, 1, 1) + ADAPTER_SCALE * contract_pair(
        up_adapter_upper, up_projected_lower, 1, 0
    )
    sigmoid_gate = jax.nn.sigmoid(gate_preactivation)
    silu_gate = gate_preactivation * sigmoid_gate
    hidden_units = (silu_gate * up_preactivation).astype(jnp.bfloat16)
    down_partial = contract_pair(hidden_units, down_adapter_lower, 0, 1).astype(jnp.bfloat16)
    (
        output_gradient_rows,
        gate_preactivation,
        up_preactivation,
        sigmoid_gate,
        silu_gate,
        hidden_units,
        down_partial,
        gate_projected_lower,
        up_projected_lower,
    ) = lax.optimization_barrier(
        (
            output_gradient_rows,
            gate_preactivation,
            up_preactivation,
            sigmoid_gate,
            silu_gate,
            hidden_units,
            down_partial,
            gate_projected_lower,
            up_projected_lower,
        )
    )
    hidden_here = down_weight.shape[0]
    down_both = contract_pair(
        jnp.concatenate([down_weight, b_down.T], 0), output_gradient_rows, 1, 1
    )
    down_projected_lower = down_both[hidden_here:].astype(jnp.bfloat16)
    hidden_gradient = down_both[:hidden_here] + ADAPTER_SCALE * contract_pair(
        down_adapter_lower, down_projected_lower, 0, 0
    )
    gate_gradient = (
        hidden_gradient
        * up_preactivation
        * sigmoid_gate
        * (1.0 + gate_preactivation * (1.0 - sigmoid_gate))
    ).astype(jnp.bfloat16)
    up_gradient = (hidden_gradient * silu_gate).astype(jnp.bfloat16)
    gate_partial = contract_pair(gate_gradient, gate_adapter_upper, 0, 0).astype(jnp.bfloat16)
    up_partial = contract_pair(up_gradient, up_adapter_upper, 0, 0).astype(jnp.bfloat16)
    parts = jnp.concatenate([gate_partial, up_partial, down_partial], 1)
    pair = jnp.concatenate([gate_partial, up_partial], 1)
    lhs = jnp.concatenate([gate_gradient, up_gradient, pair.T], 0)
    lora_rows = jnp.concatenate(
        [
            (ADAPTER_SCALE * a_gate.astype(jnp.float32)).astype(jnp.bfloat16),
            (ADAPTER_SCALE * a_up.astype(jnp.float32)).astype(jnp.bfloat16),
        ],
        0,
    )
    extended = jnp.concatenate([gate_weight, up_weight, lora_rows], 0)
    gradient_rows_out = lax.dot_general(
        lhs, extended, (((0,), (0,)), ((), ())), preferred_element_type=jnp.float32
    ).astype(jnp.bfloat16)
    owned_slice = (
        ADAPTER_SCALE * contract_pair(gate_gradient, gate_projected_lower, 1, 1),
        ADAPTER_SCALE * contract_pair(up_gradient, up_projected_lower, 1, 1),
        ADAPTER_SCALE * contract_pair(down_projected_lower, hidden_units, 1, 1),
    )
    return (gradient_rows_out, parts, owned_slice)


def gather_dp_kernel(n, src_ref, out_ref, send_sem, recv_sem):
    me = lax.axis_index("dp")
    ex = lax.axis_index("expert")
    barrier = pltpu.get_barrier_semaphore()
    for k in range(1, n):
        peer = lax.rem(me + k, n)
        pl.semaphore_signal(barrier, inc=1, device_id=(peer, ex), device_id_type=MESH)
    pl.semaphore_wait(barrier, n - 1)
    copies = []
    for k in range(1, n):
        peer = lax.rem(me + k, n)
        cp = pltpu.make_async_remote_copy(
            src_ref,
            out_ref.at[me],
            send_sem.at[k],
            recv_sem.at[k],
            device_id=(peer, ex),
            device_id_type=MESH,
        )
        cp.start()
        copies.append(cp)
    out_ref[me] = src_ref[...]
    for cp in copies:
        cp.wait()


def gather_dp(block, n):
    return pl.pallas_call(
        functools.partial(gather_dp_kernel, n),
        out_shape=jax.ShapeDtypeStruct((n,) + block.shape, block.dtype),
        in_specs=[pl.BlockSpec(memory_space=pltpu.VMEM)],
        out_specs=pl.BlockSpec(memory_space=pltpu.VMEM),
        scratch_shapes=[pltpu.SemaphoreType.DMA((n,)), pltpu.SemaphoreType.DMA((n,))],
        compiler_params=pltpu.CompilerParams(collective_id=0, has_side_effects=True),
    )(block)


def a2a_expert_kernel(n, width, sliced, src_ref, out_ref, send_sem, recv_sem):
    me = lax.axis_index("expert")
    row = lax.axis_index("dp")
    barrier = pltpu.get_barrier_semaphore()
    for k in range(1, n):
        peer = lax.rem(me + k, n)
        pl.semaphore_signal(barrier, inc=1, device_id=(row, peer), device_id_type=MESH)
    pl.semaphore_wait(barrier, n - 1)
    mine = pl.ds(pl.multiple_of(me * width, width), width)
    copies = []
    for k in range(1, n):
        peer = lax.rem(me + k, n)
        if sliced:
            block = src_ref.at[:, pl.ds(pl.multiple_of(peer * width, width), width)]
        else:
            block = src_ref.at[peer]
        cp = pltpu.make_async_remote_copy(
            block,
            out_ref.at[:, mine],
            send_sem.at[k],
            recv_sem.at[k],
            device_id=(row, peer),
            device_id_type=MESH,
        )
        cp.start()
        copies.append(cp)
    if sliced:
        out_ref[:, mine] = src_ref[:, mine]
    else:
        out_ref[:, mine] = src_ref[me]
    for cp in copies:
        cp.wait()


def a2a_expert(send, exchange_id, n=None):
    sliced = n is not None
    if sliced:
        rows, width = send.shape[0], send.shape[1] // n
    else:
        n, rows, width = send.shape
    return pl.pallas_call(
        functools.partial(a2a_expert_kernel, n, width, sliced),
        out_shape=jax.ShapeDtypeStruct((rows, n * width), send.dtype),
        in_specs=[pl.BlockSpec(memory_space=pltpu.VMEM)],
        out_specs=pl.BlockSpec(memory_space=pltpu.VMEM),
        scratch_shapes=[pltpu.SemaphoreType.DMA((n,)), pltpu.SemaphoreType.DMA((n,))],
        compiler_params=pltpu.CompilerParams(collective_id=exchange_id, has_side_effects=True),
    )(send)

def reduce_dp_kernel(n, src_ref, out_ref, landing, send_sem, recv_sem):
    me = lax.axis_index("dp")
    ex = lax.axis_index("expert")
    barrier = pltpu.get_barrier_semaphore()
    for k in range(1, n):
        peer = lax.rem(me + k, n)
        pl.semaphore_signal(barrier, inc=1, device_id=(peer, ex), device_id_type=MESH)
    pl.semaphore_wait(barrier, n - 1)
    copies = []
    for k in range(1, n):
        peer = lax.rem(me + k, n)
        cp = pltpu.make_async_remote_copy(
            src_ref.at[peer],
            landing.at[me],
            send_sem.at[k],
            recv_sem.at[k],
            device_id=(peer, ex),
            device_id_type=MESH,
        )
        cp.start()
        copies.append(cp)
    landing[me] = src_ref[me]
    for cp in copies:
        cp.wait()
    out_ref[...] = jnp.sum(landing[...].astype(jnp.float32), axis=0)


def reduce_dp(blocks):
    n, rows, cols = blocks.shape
    return pl.pallas_call(
        functools.partial(reduce_dp_kernel, n),
        out_shape=jax.ShapeDtypeStruct((rows, cols), jnp.float32),
        in_specs=[pl.BlockSpec(memory_space=pltpu.VMEM)],
        out_specs=pl.BlockSpec(memory_space=pltpu.VMEM),
        scratch_shapes=[
            pltpu.VMEM((n, rows, cols), blocks.dtype),
            pltpu.SemaphoreType.DMA((n,)),
            pltpu.SemaphoreType.DMA((n,)),
        ],
        compiler_params=pltpu.CompilerParams(collective_id=3, has_side_effects=True),
    )(blocks)


def local(
    tokens,
    output_gradient,
    routing,
    router_gate_values,
    gate_weight,
    up_weight,
    down_weight,
    adapter_lower_gate,
    adapter_upper_gate,
    adapter_lower_up,
    adapter_upper_up,
    adapter_lower_down,
    adapter_upper_down,
):
    experts = lax.axis_size("expert")
    shards = lax.axis_size("dp")
    tok_local, feat_local = tokens.shape
    choose = routing.shape[1]
    complete_width = feat_local * experts
    capacity = min(tok_local, 6 * tok_local // experts)
    adapter_rank = adapter_lower_gate.shape[1]
    chunks = NUM_CHUNKS
    piece = capacity // chunks
    params = (
        gate_weight[0],
        up_weight[0],
        down_weight[0],
        adapter_lower_gate[0],
        adapter_upper_gate[0],
        adapter_lower_up[0],
        adapter_upper_up[0],
        adapter_lower_down[0],
        adapter_upper_down[0],
    )
    positions = slot_numbers(routing, experts)
    zero_row = jnp.zeros((1, feat_local), jnp.bfloat16)
    source, member = slot_sources(routing, positions, experts, capacity)
    clamped = jnp.minimum(source, tok_local - 1)
    slot_gate = jnp.where(
        source < tok_local, router_gate_values.reshape(-1)[clamped * choose + member], 0.0
    )
    send_x = jnp.concatenate([tokens, zero_row], 0)[source].reshape(experts, capacity, feat_local)
    send_dy = (
        (
            slot_gate[:, None]
            * jnp.concatenate([output_gradient, zero_row], 0)[source].astype(jnp.float32)
        )
        .astype(jnp.bfloat16)
        .reshape(experts, capacity, feat_local)
    )
    x_block = a2a_expert(send_x, 1)
    x_rows = lax.all_gather(x_block, "dp", axis=0, tiled=True)
    dy_block = a2a_expert(send_dy, 2)
    dy_rows = lax.all_gather(dy_block, "dp", axis=0, tiled=True)
    rows_out, parts, owned_total = rows_backward_parts(x_rows, dy_rows, params)
    packed = rows_out.reshape(shards, capacity, complete_width)
    summed = lax.psum_scatter(packed, "dp", scatter_dimension=0, tiled=True)[0]
    dense_rows = capacity * 3 * adapter_rank // PART_COLS
    parts_blocks = parts.reshape(shards, dense_rows, PART_COLS)
    parts_mine = reduce_dp(parts_blocks)
    parts_sum = gather_dp(parts_mine, shards).reshape(shards * capacity, 3 * adapter_rank)
    grad_a_pair = ADAPTER_SCALE * contract_pair(parts_sum[:, :2 * adapter_rank], x_rows, 0, 0)
    grad_a_gate = grad_a_pair[:adapter_rank]
    grad_a_up = grad_a_pair[adapter_rank:]
    grad_b_down = ADAPTER_SCALE * contract_pair(
        dy_rows, parts_sum[:, 2 * adapter_rank:3 * adapter_rank], 0, 0
    )
    returned_rows = a2a_expert(summed, 4, experts).astype(jnp.float32)
    lookup = positions * experts + routing
    grad_x = jnp.sum(returned_rows.reshape(capacity * experts, feat_local)[lookup], axis=1).astype(
        jnp.bfloat16
    )
    return (
        grad_x,
        grad_a_gate[None],
        owned_total[0][None],
        grad_a_up[None],
        owned_total[1][None],
        owned_total[2][None],
        grad_b_down[None],
    )


def solution(mesh):
    return jax.shard_map(
        local,
        mesh=mesh,
        in_specs=(
            P("dp", "expert"),
            P("dp", "expert"),
            P("dp", None),
            P("dp", None),
            P("expert", "dp", None),
            P("expert", "dp", None),
            P("expert", "dp", None),
            P("expert", None, None),
            P("expert", "dp", None),
            P("expert", None, None),
            P("expert", "dp", None),
            P("expert", None, "dp"),
            P("expert", None, None),
        ),
        out_specs=(
            P("dp", "expert"),
            P("expert", None, None),
            P("expert", "dp", None),
            P("expert", None, None),
            P("expert", "dp", None),
            P("expert", None, "dp"),
            P("expert", None, None),
        ),
        check_vma=False,
    )
```
